128 devices in a mesh: grp: 8 (over y, x_lo), cell: 16 (over x_hi, z, core).
Axes of the slice: x: 4 (x_hi: 2, x_lo: 2; x = x_hi * 2 + x_lo), y: 4, z: 4, core: 2. Of those that a mesh axis runs over, the one named last changes fastest.
Arguments:
- expression: bfloat16 [2000, 65536], P(None, ('grp', 'cell')), may hold values from 0.019897461 to 4
- dataset_id: int32 [65536], P(('grp', 'cell')), may hold values from 0 to 7, as said below
- dataset_map: int32 [8], P('grp'), may hold values from 0 to 7, as said below
- sweep_count: int32 [8], replicated, may hold values from 2 to 4
- picks: int32 [2, 16384], P(None, ('grp', 'cell')), may hold values from 0 to 511
- shared_init: float32 [64, 2000], replicated, may hold values from 0.004 to 0.06
- specific_init: float32 [8, 64, 2000], P('grp'), may hold values from 0.001 to 0.02
Outputs:
- loadings: float32 [2, 64, 16384], P(None, None, ('grp', 'cell'))
- shared_basis: float32 [64, 2000], replicated
- specific_basis: float32 [8, 64, 2000], P('grp')
The draws below stay inside these ranges and needn't reach their ends.
Inputs may be any that keep to these rules, and one draw needn't show every extreme that they name: `dataset_map`: a permutation of the datasets; entry g is the one dataset of device group g. `dataset_id`: every cell held by the devices of group g belongs to one of the datasets that dataset_map gives to group g. `picks`: an index into the cells held by the device that holds the slot; a cell may be picked more than once.
All inputs are finite; a program needn't handle non-finite values.
Results may differ from the reference program's by a relative error of at most 0.0065.
The reference program's roundings to bfloat16 on the way count: a program that leaves them out, or rounds other values in their place, can miss the bound.
Values sent between devices are 32-bit elements; how exact they have to be, the bound alone decides.
No kernel may reach another device: no remote copies, remote signals or barrier semaphores. Data moves between devices by JAX's collectives and lax.ppermute only.
A program may use at most 128 MiB of HBM per device.

```python
import math
import jax
import jax.numpy as jnp
from jax import lax

G = 2000
K = 64
SWEEPS = 4
ROUNDS = 2
DS_GRP = 1
CELLS_DEV = 128
POOL_DEV = 512
DATASETS = 8
CELLS = 16384
POOL = 65536
N_GRP = 8
N_CELL = 16


def map_and_slots(key):
    base_key = jax.random.fold_in(key, 7001)
    dataset_order = jax.random.permutation(jax.random.fold_in(base_key, 1), DATASETS).astype(jnp.int32)
    first_pick = jax.random.randint(jax.random.fold_in(base_key, 2), (POOL,), 0, DS_GRP)
    second = jax.random.randint(jax.random.fold_in(base_key, 3), (POOL,), 0, DS_GRP)
    slot_pick = jnp.minimum(first_pick, second)
    group_of = jnp.arange(POOL, dtype=jnp.int32) // (POOL_DEV * N_CELL)
    identities = dataset_order[group_of * DS_GRP + slot_pick]
    return (dataset_order, identities.astype(jnp.int32))


def draw_dataset_map(key, part):
    return map_and_slots(key)[0]


def draw_dataset_id(key, part):
    return map_and_slots(key)[1]


def with_ends(entries, own_key, least, top_value):
    shape = entries.shape
    place = [jax.random.randint(jax.random.fold_in(own_key, axis), (), 0, shape[axis]) for axis in range(len(shape))]
    entries = entries.at[tuple(place)].set(least)
    longest = shape.index(max(shape))
    place[longest] = (place[longest] + 1) % shape[longest]
    return entries.at[tuple(place)].set(top_value)


def level_of(own_key, shape, cuts, smallest, largest):
    level = 1.0
    for axis_at, blocks in cuts:
        steps = jax.random.uniform(jax.random.fold_in(jax.random.fold_in(own_key, 6), axis_at), (blocks,), jnp.float32, smallest / len(cuts), largest / len(cuts))
        level = level * jnp.repeat(jnp.exp(steps), shape[axis_at] // blocks).reshape((-1,) + (1,) * (len(shape) - 1 - axis_at))
    return level


def setup_inputs(seed: int = 0) -> dict:
    key_of = jax.random.split(jax.random.key(seed), 8)
    return {
        "expression": jnp.clip(jnp.exp(math.log(4.0) - 5.3034575 * jax.random.uniform(key_of[0], (G, POOL), jnp.float32) ** level_of(key_of[0], (G, POOL), ((1, 128),), -0.2, 0.2)), 0.019897461, 4.0).astype(jnp.bfloat16),
        "dataset_id": draw_dataset_id(jax.random.fold_in(key_of[7], 71), 0),
        "dataset_map": draw_dataset_map(jax.random.fold_in(key_of[7], 71), 0),
        "sweep_count": with_ends(jax.random.randint(key_of[3], (DATASETS,), 2, SWEEPS + 1), jax.random.fold_in(key_of[3], 1), 2, SWEEPS).astype(jnp.int32),
        "picks": with_ends(jax.random.randint(key_of[4], (ROUNDS, CELLS), 0, POOL_DEV), jax.random.fold_in(key_of[4], 1), 0, POOL_DEV - 1).astype(jnp.int32),
        "shared_init": jnp.clip(jnp.exp(jax.random.uniform(key_of[5], (K, G), jnp.float32, math.log(0.004), math.log(0.06))), 0.004, 0.06),
        "specific_init": jnp.clip(jnp.exp(math.log(0.02) - 2.9957322 * jax.random.uniform(key_of[6], (DATASETS, K, G), jnp.float32) ** level_of(key_of[6], (DATASETS, K, G), ((0, 8),), -0.2, 0.2)), 0.001, 0.02),
    }


EPSILON = 1e-6
LAMBDA = 5.0
HIGHEST = lax.Precision.HIGHEST


def hals_loadings(target, gram_matrix, member, counts):
    divisor = jnp.einsum("jk,jn->kn", jnp.diagonal(gram_matrix, axis1=1, axis2=2) + EPSILON, member, precision=HIGHEST)

    def sweep(sweep_index, current):
        active = sweep_index < counts
        for factor in range(K):
            row_terms = jnp.einsum("jl,ln->jn", gram_matrix[:, factor, :], current, precision=HIGHEST)
            product = jnp.sum(row_terms * member, axis=0)
            updated = jnp.maximum(current[factor] + (target[factor] - product) / divisor[factor], 0.0)
            current = current.at[factor].set(jnp.where(active, updated, current[factor]))
        return current

    return lax.fori_loop(0, SWEEPS, sweep, jnp.zeros(target.shape, jnp.float32))


def solve_loadings(cell_data, member, counts, shared, specific):
    combined = shared[None] + specific
    slot_total = specific.shape[0]
    stacked = combined.astype(jnp.bfloat16).reshape(slot_total * K, combined.shape[2])
    target = jnp.dot(stacked, cell_data, preferred_element_type=jnp.float32)
    target = jnp.sum(target.reshape(slot_total, K, cell_data.shape[1]) * member[:, None, :], axis=0)
    gram_matrix = jnp.einsum("jkg,jlg->jkl", combined, combined, precision=HIGHEST) + LAMBDA * jnp.einsum("jkg,jlg->jkl", specific, specific, precision=HIGHEST)
    return hals_loadings(target, gram_matrix, member, counts)


def renew_shared(shared, gram_total, carried):
    for factor in range(K):
        change = (carried[factor] - jnp.dot(gram_total[factor], shared, precision=HIGHEST)) / jnp.maximum(gram_total[factor, factor], 1.0)
        shared = shared.at[factor].set(jnp.maximum(shared[factor] + change, 0.0))
    return shared


def renew_specific(specific, shared, gram_sets, stat_sets):
    for factor in range(K):
        weights = gram_sets[:, factor, :]
        pulled = jnp.dot(weights, shared, precision=HIGHEST) + (1.0 + LAMBDA) * jnp.einsum("sl,slg->sg", weights, specific, precision=HIGHEST)
        divisor = jnp.maximum((1.0 + LAMBDA) * gram_sets[:, factor, factor], 1.0)
        updated = jnp.maximum(specific[:, factor] + (stat_sets[:, factor] - pulled) / divisor[:, None], 0.0)
        specific = specific.at[:, factor].set(updated)
    return specific


def reference(expression, dataset_id, dataset_map, sweep_count, picks, shared_init, specific_init):
    group_width = CELLS_DEV * N_CELL
    listing = jnp.arange(DATASETS, dtype=jnp.int32)
    slot_sweeps = jnp.sum(jnp.where(dataset_map[:, None] == listing[None, :], sweep_count[None, :], 0), axis=1).astype(jnp.int32)
    device_of = jnp.arange(CELLS, dtype=jnp.int32) // CELLS_DEV
    group_of = device_of // N_CELL
    group_slots = dataset_map.reshape(N_GRP, DS_GRP)[group_of]
    group_sweeps = slot_sweeps.reshape(N_GRP, DS_GRP)[group_of]
    basis_list = [(shared_init, specific_init)]
    gram_sets = jnp.zeros((DATASETS, K, K), jnp.float32)
    stat_sets = jnp.zeros((DATASETS, K, G), jnp.float32)
    gram_total = jnp.zeros((K, K), jnp.float32)
    results = []
    for round_index in range(ROUNDS):
        pool_index = (device_of * POOL_DEV + picks[round_index]).astype(jnp.int32)
        cell_data = jnp.take(expression, pool_index, axis=1)
        matches = group_slots == dataset_id[pool_index][:, None]
        member = matches.astype(jnp.float32).T
        counts = jnp.sum(jnp.where(matches, group_sweeps, 0), axis=1).astype(jnp.int32)
        shared_use, specific_use = basis_list[max(round_index - 1, 0)]
        grouped_data = cell_data.reshape(G, N_GRP, group_width).transpose(1, 0, 2)
        grouped_member = member.reshape(DS_GRP, N_GRP, group_width).transpose(1, 0, 2)
        grouped_counts = counts.reshape(N_GRP, group_width)
        grouped_specific = specific_use.reshape(N_GRP, DS_GRP, K, G)

        def one_group(items):
            return solve_loadings(items[0], items[1], items[2], shared_use, items[3])

        grouped_loads = lax.map(one_group, (grouped_data, grouped_member, grouped_counts, grouped_specific))
        results.append(grouped_loads.transpose(1, 0, 2).reshape(K, CELLS))
        masked = grouped_loads[:, None] * grouped_member[:, :, None]
        rounded = lax.optimization_barrier(grouped_loads.astype(jnp.bfloat16)).astype(jnp.float32)
        rounded = rounded[:, None] * grouped_member[:, :, None]
        stat_round = jnp.einsum("ajkn,agn->ajkg", rounded, grouped_data.astype(jnp.float32), precision=HIGHEST)
        gram_round = jnp.einsum("ajkn,aln->ajkl", masked, grouped_loads, precision=HIGHEST)
        gram_sets = gram_sets + gram_round.reshape(DATASETS, K, K)
        stat_sets = stat_sets + stat_round.reshape(DATASETS, K, G)
        gram_total = gram_total + jnp.sum(gram_round, axis=(0, 1))
        shared_prev, specific_prev = basis_list[-1]
        carried = jnp.sum(stat_sets, axis=0) - jnp.einsum("jkl,jlg->kg", gram_sets, specific_prev, precision=HIGHEST)
        shared_next = renew_shared(shared_prev, gram_total, carried)
        specific_next = renew_specific(specific_prev, shared_next, gram_sets, stat_sets)
        basis_list.append((shared_next, specific_next))
    return jnp.stack(results), basis_list[-1][0], basis_list[-1][1]
```

```python
import jax
import jax.numpy as jnp
from jax import lax
from jax.experimental import pallas as pl
from jax.experimental.pallas import tpu as pltpu
from jax.sharding import Mesh, PartitionSpec as P

K = 64
G = 2000
N = 128
HALF = 8 * N
LAST = G - 15 * N
EPSILON = 1e-06
LAMBDA = 5.0
RIDGE = 1.0 + LAMBDA
HIGHEST = lax.Precision.HIGHEST
GRP = ("y", "xl")
RING = ("xh", "z")
ALL = ("y", "xl", "xh", "z", "c")
NT = (((1,), (1,)), ((), ()))
F32 = jnp.float32
BF16 = jnp.bfloat16


def dot_nt(a, b, precision=None):
    return lax.dot_general(a, b, NT, precision=precision, preferred_element_type=F32)


def diagonal(square):
    n = square.shape[0]
    rows = lax.broadcasted_iota(jnp.int32, (n, n), 0)
    cols = lax.broadcasted_iota(jnp.int32, (n, n), 1)
    return jnp.sum(jnp.where(rows == cols, square, 0.0), axis=1, keepdims=True)


def rows_of(x):
    return [x[8 * t : 8 * t + 8] for t in range(K // 8)]


def coordinate_steps(state, residual, column):
    sub = lax.broadcasted_iota(jnp.int32, (8, N), 0)
    for k in range(K):
        t, s = divmod(k, 8)
        cols = column(k)
        for half in range(len(state)):
            h, r = state[half], residual[half]
            change = jnp.maximum(-h[t], r[t])
            spread = jnp.broadcast_to(change[s : s + 1], (8, N))
            h[t] = jnp.where(sub == s, h[t] + change, h[t])
            for j in range(K // 8):
                r[j] = r[j] - cols[j] * spread
    return state


def front_kernel(where, dmap, sweeps, x, picks, w, v, loads, keep, send, w_own, v_own, table):
    core, tile = where[0], where[1]
    count = sweeps[dmap[0]]
    shared, specific = w[...], v[0]
    mixed = shared + specific

    @pl.when(tile < 15)
    def _():
        at = pl.multiple_of(jnp.minimum(tile, 14) * N, N)
        w_own[...] = w[:, pl.ds(at, N)]
        v_own[...] = v[0, :, pl.ds(at, N)]

    @pl.when(tile == 15)
    def _():
        w_own[...] = jnp.zeros((K, N), F32)
        v_own[...] = jnp.zeros((K, N), F32)
        w_own[:, :LAST] = w[:, 15 * N :]
        v_own[:, :LAST] = v[0, :, 15 * N :]

    gram = dot_nt(mixed, mixed, HIGHEST) + LAMBDA * dot_nt(specific, specific, HIGHEST)
    inverse = 1.0 / (diagonal(gram) + EPSILON)
    scaled = gram * inverse
    for k in range(K):
        table[k] = jnp.broadcast_to(scaled[:, k : k + 1], (K, N))

    pool = lax.broadcasted_iota(jnp.int32, (x.shape[1], N), 0)
    choose = jnp.concatenate(
        [(pool == picks[r : r + 1, :]).astype(F32).astype(BF16) for r in range(2)], axis=1
    )
    cells = jnp.dot(x[...], choose, preferred_element_type=F32).astype(BF16)
    target = jnp.dot(mixed.astype(BF16), cells, preferred_element_type=F32) * inverse

    def sweep(_, carry):
        state = [list(carry[0]), list(carry[1])]
        residual = [list(carry[2]), list(carry[3])]
        coordinate_steps(state, residual, lambda k: [table[k, 8 * j : 8 * j + 8] for j in range(K // 8)])
        return (tuple(state[0]), tuple(state[1]), tuple(residual[0]), tuple(residual[1]))

    none = tuple(jnp.zeros((8, N), F32) for _ in range(K // 8))
    carry = (none, none, tuple(rows_of(target[:, :N])), tuple(rows_of(target[:, N:])))
    carry = lax.fori_loop(0, count, sweep, carry)
    first = jnp.concatenate(carry[0], axis=0)
    second = jnp.concatenate(carry[1], axis=0)
    loads[0] = first
    loads[1] = second
    zero = jnp.zeros((K, N), F32)
    both = jnp.concatenate([first, second], axis=1)
    block = jnp.concatenate(
        [jnp.concatenate([first, zero], axis=1), jnp.concatenate([zero, second], axis=1)], axis=0
    )
    gram_part = dot_nt(both, block, HIGHEST)
    keep[HALF:] = gram_part
    send[HALF:] = gram_part
    rounded = block.astype(BF16)
    low = dot_nt(cells[:HALF], rounded)
    high = dot_nt(cells[HALF:], rounded)

    @pl.when(core == 0)
    def _():
        keep[:HALF] = low
        send[: G - HALF] = high
        send[G - HALF : HALF] = jnp.zeros((2 * HALF - G, N), F32)

    @pl.when(core == 1)
    def _():
        send[:HALF] = low
        keep[: G - HALF] = high
        keep[G - HALF : HALF] = jnp.zeros((2 * HALF - G, N), F32)


def pack_kernel(keep, came, out):
    gram = keep[HALF:] + came[HALF:]
    for i in range(8):
        out[i, :N] = keep[N * i : N * i + N] + came[N * i : N * i + N]
        out[i, N:] = gram


def group_kernel(came, v_own, out, stats, grams):
    total = came[0]
    for i in range(1, 8):
        total = total + came[i]
    rows = total[:N].T
    first = rows[:K]
    stats[0] = first
    stats[1] = first + rows[K:]
    gram = total[N:]
    grams[0] = gram[:, :K]
    grams[1] = gram[:, :K] + gram[:, K:]
    carried = first - jnp.dot(gram[:, :K], v_own[...], precision=HIGHEST, preferred_element_type=F32)
    for i in range(8):
        out[i, :K] = carried
        out[i, K:] = gram


def renew(w, v, gram_total, gram, carried, stat):
    inverse = 1.0 / jnp.maximum(diagonal(gram_total), 1.0)
    scaled = gram_total * inverse
    start = carried - jnp.dot(gram_total, w, precision=HIGHEST, preferred_element_type=F32)
    state, residual = [rows_of(w)], [rows_of(start * inverse)]

    def columns(table):
        return lambda k: rows_of(jnp.broadcast_to(table[:, k : k + 1], (K, N)))

    coordinate_steps(state, residual, columns(scaled))
    w_next = jnp.concatenate(state[0], axis=0)
    own_inverse = 1.0 / jnp.maximum(RIDGE * diagonal(gram), 1.0)
    own_scaled = (RIDGE * gram) * own_inverse
    pulled = jnp.dot(gram, w_next + RIDGE * v, precision=HIGHEST, preferred_element_type=F32)
    state, residual = [rows_of(v)], [rows_of((stat - pulled) * own_inverse)]
    coordinate_steps(state, residual, columns(own_scaled))
    return w_next, jnp.concatenate(state[0], axis=0)


def first_kernel(came, stats, grams, w_own, v_own, out, w_next, v_next, gram_total):
    total = came[0]
    for i in range(1, 8):
        total = total + came[i]
    all_grams = total[K:]
    gram_total[...] = all_grams[:, :K] + all_grams[:, K:]
    shared, specific = renew(w_own[...], v_own[...], all_grams[:, :K], grams[0], total[:K], stats[0])
    w_next[...] = shared
    v_next[...] = specific
    carried = stats[1] - jnp.dot(grams[1], specific, precision=HIGHEST, preferred_element_type=F32)
    for i in range(8):
        out[i] = carried


def second_kernel(came, stats, grams, w_own, v_own, gram_total, out):
    total = came[0]
    for i in range(1, 8):
        total = total + came[i]
    shared, specific = renew(w_own[...], v_own[...], gram_total[...], grams[1], total, stats[1])
    for i in range(8):
        out[i, :K] = shared
        out[i, K:] = specific


def finish_kernel(where, mine, other, w, v):
    def write(first, second):
        for half, part in enumerate((first, second)):
            for i in range(8):
                at = (8 * half + i) * N
                wide = min(N, G - at)
                w[:, at : at + wide] = part[i, :K, :wide]
                v[0, :, at : at + wide] = part[i, K:, :wide]

    @pl.when(where[0] == 0)
    def _():
        write(mine, other)

    @pl.when(where[0] == 1)
    def _():
        write(other, mine)


def shape(*dims):
    return jax.ShapeDtypeStruct(dims, F32)


VM = pl.BlockSpec(memory_space=pltpu.VMEM)
SM = pl.BlockSpec(memory_space=pltpu.SMEM)
SWAP = [(0, 1), (1, 0)]


def on_device(expression, dataset_id, dataset_map, sweep_count, picks, shared_init, specific_init):
    core = lax.axis_index("c")
    tile = core * 8 + lax.axis_index("xh") * 4 + lax.axis_index("z")
    where = jnp.stack([core, tile]).astype(jnp.int32)
    loads, keep, send, w_own, v_own = pl.pallas_call(
        front_kernel,
        name="front",
        out_shape=(shape(2, K, N), shape(HALF + K, N), shape(HALF + K, N), shape(K, N), shape(K, N)),
        in_specs=[SM, SM, SM, VM, VM, VM, VM],
        out_specs=[VM] * 5,
        scratch_shapes=[pltpu.VMEM((K, K, N), F32)],
    )(where, dataset_map, sweep_count, expression, picks, shared_init, specific_init)
    came = lax.ppermute(send, "c", SWAP)
    packed = pl.pallas_call(
        pack_kernel, name="pack", out_shape=shape(8, N + K, N), in_specs=[VM, VM], out_specs=VM
    )(keep, came)
    came = lax.all_to_all(packed, RING, 0, 0, tiled=True)
    spread, stats, grams = pl.pallas_call(
        group_kernel,
        name="group",
        out_shape=(shape(8, N, N), shape(2, K, N), shape(2, K, K)),
        in_specs=[VM, VM],
        out_specs=[VM] * 3,
    )(came, v_own)
    came = lax.all_to_all(spread, GRP, 0, 0, tiled=True)
    spread, w_own, v_own, gram_total = pl.pallas_call(
        first_kernel,
        name="first",
        out_shape=(shape(8, K, N), shape(K, N), shape(K, N), shape(K, K)),
        in_specs=[VM] * 5,
        out_specs=[VM] * 4,
    )(came, stats, grams, w_own, v_own)
    came = lax.all_to_all(spread, GRP, 0, 0, tiled=True)
    spread = pl.pallas_call(
        second_kernel, name="second", out_shape=shape(8, N, N), in_specs=[VM] * 6, out_specs=VM
    )(came, stats, grams, w_own, v_own, gram_total)
    mine = lax.all_to_all(spread, RING, 0, 0, tiled=True)
    other = lax.ppermute(mine, "c", SWAP)
    shared, specific = pl.pallas_call(
        finish_kernel,
        name="finish",
        out_shape=(shape(K, G), shape(1, K, G)),
        in_specs=[SM, VM, VM],
        out_specs=[VM, VM],
    )(where, mine, other)
    return loads, shared, specific


def solution(mesh):
    fine = Mesh(mesh.devices.reshape(4, 2, 2, 4, 2), ALL)
    return jax.shard_map(
        on_device,
        mesh=fine,
        in_specs=(P(None, ALL), P(ALL), P(GRP), P(), P(None, ALL), P(), P(GRP, None, None)),
        out_specs=(P(None, None, ALL), P(), P(GRP, None, None)),
        check_vma=False,
    )
```

```python
import jax
import jax.numpy as jnp
from jax import lax
from jax.experimental import pallas as pl
from jax.experimental.pallas import tpu as pltpu
from jax.sharding import Mesh, PartitionSpec as P

K = 64
G = 2000
N = 128
HALF = 8 * N
LAST = G - 15 * N
EPSILON = 1e-06
LAMBDA = 5.0
RIDGE = 1.0 + LAMBDA
HIGHEST = lax.Precision.HIGHEST
GRP = ("y", "xl")
RING = ("xh", "z")
ALL = ("y", "xl", "xh", "z", "c")
NT = (((1,), (1,)), ((), ()))
F32 = jnp.float32
BF16 = jnp.bfloat16


def dot_nt(a, b, precision=None):
    return lax.dot_general(a, b, NT, precision=precision, preferred_element_type=F32)


def diagonal(square):
    n = square.shape[0]
    rows = lax.broadcasted_iota(jnp.int32, (n, n), 0)
    cols = lax.broadcasted_iota(jnp.int32, (n, n), 1)
    return jnp.sum(jnp.where(rows == cols, square, 0.0), axis=1, keepdims=True)


def rows_of(x):
    return [x[8 * t : 8 * t + 8] for t in range(K // 8)]


def coordinate_steps(state, residual, column):
    sub = lax.broadcasted_iota(jnp.int32, (8, N), 0)
    for k in range(K):
        t, s = divmod(k, 8)
        cols = column(k)
        for half in range(len(state)):
            h, r = state[half], residual[half]
            change = jnp.maximum(-h[t], r[t])
            spread = jnp.broadcast_to(change[s : s + 1], (8, N))
            h[t] = jnp.where(sub == s, h[t] + change, h[t])
            for j in range(K // 8):
                r[j] = r[j] - cols[j] * spread
    return state


def front_kernel(dmap, sweeps, x, picks, w, v, loads, keep, send, w_own, v_own, table):
    core = lax.axis_index("c")
    tile = core * 8 + lax.axis_index("xh") * 4 + lax.axis_index("z")
    count = sweeps[dmap[0]]
    shared, specific = w[...], v[0]
    mixed = shared + specific

    @pl.when(tile < 15)
    def _():
        at = pl.multiple_of(jnp.minimum(tile, 14) * N, N)
        w_own[...] = w[:, pl.ds(at, N)]
        v_own[...] = v[0, :, pl.ds(at, N)]

    @pl.when(tile == 15)
    def _():
        w_own[...] = jnp.zeros((K, N), F32)
        v_own[...] = jnp.zeros((K, N), F32)
        w_own[:, :LAST] = w[:, 15 * N :]
        v_own[:, :LAST] = v[0, :, 15 * N :]

    gram = dot_nt(mixed, mixed, HIGHEST) + LAMBDA * dot_nt(specific, specific, HIGHEST)
    inverse = 1.0 / (diagonal(gram) + EPSILON)
    scaled = gram * inverse
    for k in range(K):
        table[k] = jnp.broadcast_to(scaled[:, k : k + 1], (K, N))

    pool = lax.broadcasted_iota(jnp.int32, (x.shape[1], N), 0)
    choose = jnp.concatenate(
        [(pool == picks[r : r + 1, :]).astype(F32).astype(BF16) for r in range(2)], axis=1
    )
    cells = jnp.dot(x[...], choose, preferred_element_type=F32).astype(BF16)
    target = jnp.dot(mixed.astype(BF16), cells, preferred_element_type=F32) * inverse

    def sweep(_, carry):
        state = [list(carry[0]), list(carry[1])]
        residual = [list(carry[2]), list(carry[3])]
        coordinate_steps(state, residual, lambda k: [table[k, 8 * j : 8 * j + 8] for j in range(K // 8)])
        return (tuple(state[0]), tuple(state[1]), tuple(residual[0]), tuple(residual[1]))

    none = tuple(jnp.zeros((8, N), F32) for _ in range(K // 8))
    carry = (none, none, tuple(rows_of(target[:, :N])), tuple(rows_of(target[:, N:])))
    carry = lax.fori_loop(0, count, sweep, carry)
    first = jnp.concatenate(carry[0], axis=0)
    second = jnp.concatenate(carry[1], axis=0)
    loads[0] = first
    loads[1] = second
    zero = jnp.zeros((K, N), F32)
    both = jnp.concatenate([first, second], axis=1)
    block = jnp.concatenate(
        [jnp.concatenate([first, zero], axis=1), jnp.concatenate([zero, second], axis=1)], axis=0
    )
    gram_part = dot_nt(both, block, HIGHEST)
    keep[HALF:] = gram_part
    send[HALF:] = gram_part
    rounded = block.astype(BF16)
    low = dot_nt(cells[:HALF], rounded)
    high = dot_nt(cells[HALF:], rounded)

    @pl.when(core == 0)
    def _():
        keep[:HALF] = low
        send[: G - HALF] = high
        send[G - HALF : HALF] = jnp.zeros((2 * HALF - G, N), F32)

    @pl.when(core == 1)
    def _():
        send[:HALF] = low
        keep[: G - HALF] = high
        keep[G - HALF : HALF] = jnp.zeros((2 * HALF - G, N), F32)


def pack_kernel(keep, came, out):
    gram = keep[HALF:] + came[HALF:]
    for i in range(8):
        out[i, :N] = keep[N * i : N * i + N] + came[N * i : N * i + N]
        out[i, N:] = gram


def group_kernel(came, v_own, out):
    total = came[0]
    for i in range(1, 8):
        total = total + came[i]
    rows = total[:N].T
    first, second = rows[:K], rows[:K] + rows[K:]
    gram = total[N:]
    lanes = lax.broadcasted_iota(jnp.int32, (K, N), 1)
    early = pltpu.roll(gram, K, 1)
    grams = jnp.where(lanes < K, gram, gram + early)
    specific = v_own[...]
    for i in range(8):
        out[i, :K] = first
        out[i, K:N] = second
        out[i, N : N + K] = grams
        out[i, N + K :] = specific


def dot_split(a, b):
    a_high = a.astype(BF16)
    b_high = b.astype(BF16)
    a_low = (a - a_high.astype(F32)).astype(BF16)
    b_low = (b - b_high.astype(F32)).astype(BF16)
    out = jnp.dot(a_high, b_low, preferred_element_type=F32)
    out = out + jnp.dot(a_low, b_high, preferred_element_type=F32)
    return out + jnp.dot(a_high, b_high, preferred_element_type=F32)


def one_pass(state, residual, tables, first_lane):
    sub = lax.broadcasted_iota(jnp.int32, (8, N), 0)
    for k in range(K):
        t, s = divmod(k, 8)
        lane = first_lane + k
        for h, r, table in zip(state, residual, tables):
            change = jnp.maximum(-h[t], r[t])
            spread = jnp.broadcast_to(change[s : s + 1], (8, N))
            h[t] = jnp.where(sub == s, h[t] + change, h[t])
            for j in range(t if s < 7 else t + 1, K // 8):
                weight = jnp.broadcast_to(table[8 * j : 8 * j + 8, lane : lane + 1], (8, N))
                r[j] = r[j] - weight * spread
    return [jnp.concatenate(h, axis=0) for h in state]


def update_kernel(came, w_own, out, v_first):
    group = lax.axis_index("y") * 2 + lax.axis_index("xl")
    zero = jnp.zeros((K, N), F32)
    stat = came[0, :K]
    stat_next = came[0, K:N]
    total = came[0, N : N + K]
    for i in range(1, 8):
        stat = stat + came[i, :K]
        stat_next = stat_next + came[i, K:N]
        total = total + came[i, N : N + K]
    grams = [came[i, N : N + K] for i in range(8)]

    def scaled_of(gram, scale, at):
        inverse = 1.0 / jnp.maximum(scale * diagonal(gram[:, at : at + K]), 1.0)
        return (scale * gram) * inverse, inverse

    pulls = [dot_split(grams[i], jnp.concatenate([came[i, N + K :], zero], axis=0)) for i in range(8)]
    carried = stat
    for i in range(8):
        carried = carried - pulls[i]
    shared = w_own[...]
    table, inverse = scaled_of(total, 1.0, 0)
    start = carried - dot_split(total, jnp.concatenate([shared, zero], axis=0))
    (shared,) = one_pass([rows_of(shared)], [rows_of(start * inverse)], [table], 0)

    stacked = jnp.concatenate(grams, axis=0)
    pushed = dot_split(stacked, jnp.concatenate([shared, zero], axis=0))
    for pair in range(0, 8, 4):
        state, residual, tables = [], [], []
        for i in range(pair, pair + 4):
            table, inverse = scaled_of(grams[i], RIDGE, 0)
            rest = came[i, :K] - pushed[K * i : K * i + K] - RIDGE * pulls[i]
            state.append(rows_of(came[i, N + K :]))
            residual.append(rows_of(rest * inverse))
            tables.append(table)
        for i, value in enumerate(one_pass(state, residual, tables, 0)):
            v_first[pair + i] = value

    wide = jnp.concatenate(grams, axis=1)
    tall = jnp.concatenate([part for i in range(8) for part in (zero, v_first[i])], axis=0)
    carried = stat_next - dot_split(wide, tall)
    table, inverse = scaled_of(total, 1.0, K)
    start = carried - dot_split(total, jnp.concatenate([zero, shared], axis=0))
    (shared,) = one_pass([rows_of(shared)], [rows_of(start * inverse)], [table], K)

    gram = came[group, N : N + K]
    specific = v_first[group]
    table, inverse = scaled_of(gram, RIDGE, K)
    rest = came[group, K:N] - dot_split(gram, jnp.concatenate([zero, shared + RIDGE * specific], axis=0))
    (specific,) = one_pass([rows_of(specific)], [rows_of(rest * inverse)], [table], K)
    for i in range(8):
        out[i, :K] = shared
        out[i, K:] = specific


def finish_kernel(mine, other, w, v):
    core = lax.axis_index("c")

    def write(first, second):
        for half, part in enumerate((first, second)):
            for i in range(8):
                at = (8 * half + i) * N
                wide = min(N, G - at)
                w[:, at : at + wide] = part[i, :K, :wide]
                v[0, :, at : at + wide] = part[i, K:, :wide]

    @pl.when(core == 0)
    def _():
        write(mine, other)

    @pl.when(core == 1)
    def _():
        write(other, mine)


def shape(*dims):
    return jax.ShapeDtypeStruct(dims, F32)


def near(*dims):
    return pltpu.VMEM(dims, F32)


def held(x):
    return pltpu.with_memory_space_constraint(x, pltpu.VMEM)


VM = pl.BlockSpec(memory_space=pltpu.VMEM)
SM = pl.BlockSpec(memory_space=pltpu.SMEM)
SWAP = [(0, 1), (1, 0)]


def on_device(expression, dataset_id, dataset_map, sweep_count, picks, shared_init, specific_init):
    loads, keep, send, w_own, v_own = pl.pallas_call(
        front_kernel,
        name="front",
        out_shape=(shape(2, K, N), near(HALF + K, N), near(HALF + K, N), near(K, N), near(K, N)),
        in_specs=[SM, SM, VM, VM, VM, VM],
        out_specs=[VM] * 5,
        scratch_shapes=[pltpu.VMEM((K, K, N), F32)],
    )(dataset_map, sweep_count, expression, picks, shared_init, specific_init)
    came = lax.ppermute(send, "c", SWAP)
    packed = pl.pallas_call(
        pack_kernel, name="pack", out_shape=near(8, N + K, N), in_specs=[VM, VM], out_specs=VM
    )(held(keep), held(came))
    came = lax.all_to_all(packed, RING, 0, 0, tiled=True)
    spread = pl.pallas_call(
        group_kernel, name="group", out_shape=near(8, 2 * N, N), in_specs=[VM, VM], out_specs=VM
    )(held(came), held(v_own))
    came = lax.all_to_all(spread, GRP, 0, 0, tiled=True)
    spread = pl.pallas_call(
        update_kernel,
        name="update",
        out_shape=near(8, N, N),
        in_specs=[VM, VM],
        out_specs=VM,
        scratch_shapes=[pltpu.VMEM((8, K, N), F32)],
    )(held(came), held(w_own))
    mine = lax.all_to_all(spread, RING, 0, 0, tiled=True)
    other = lax.ppermute(mine, "c", SWAP)
    shared, specific = pl.pallas_call(
        finish_kernel,
        name="finish",
        out_shape=(shape(K, G), shape(1, K, G)),
        in_specs=[VM, VM],
        out_specs=[VM, VM],
    )(held(mine), held(other))
    return loads, shared, specific


def solution(mesh):
    fine = Mesh(mesh.devices.reshape(4, 2, 2, 4, 2), ALL)
    return jax.shard_map(
        on_device,
        mesh=fine,
        in_specs=(P(None, ALL), P(ALL), P(GRP), P(), P(None, ALL), P(), P(GRP, None, None)),
        out_specs=(P(None, None, ALL), P(), P(GRP, None, None)),
        check_vma=False,
    )
```

```python
import jax
import jax.numpy as jnp
from jax import lax
from jax.experimental import pallas as pl
from jax.experimental.pallas import tpu as pltpu
from jax.sharding import Mesh, PartitionSpec as P

K = 64
G = 2000
N = 128
HALF = 8 * N
PACKED = K // 2 + 8
LAST = G - 15 * N
EPSILON = 1e-06
LAMBDA = 5.0
RIDGE = 1.0 + LAMBDA
HIGHEST = lax.Precision.HIGHEST
GRP = ("y", "xl")
RING = ("xh", "z")
PLANE = ("xl", "xh", "z")
ALL = ("y", "xl", "xh", "z", "c")
NT = (((1,), (1,)), ((), ()))
F32 = jnp.float32
BF16 = jnp.bfloat16


def dot_nt(a, b, precision=None):
    return lax.dot_general(a, b, NT, precision=precision, preferred_element_type=F32)


def diagonal(square):
    n = square.shape[0]
    rows = lax.broadcasted_iota(jnp.int32, (n, n), 0)
    cols = lax.broadcasted_iota(jnp.int32, (n, n), 1)
    return jnp.sum(jnp.where(rows == cols, square, 0.0), axis=1, keepdims=True)


def rows_of(x):
    return [x[8 * t : 8 * t + 8] for t in range(K // 8)]


def coordinate_steps(state, residual, column):
    sub = lax.broadcasted_iota(jnp.int32, (8, N), 0)
    for k in range(K):
        t, s = divmod(k, 8)
        cols = column(k)
        for half in range(len(state)):
            h, r = state[half], residual[half]
            change = jnp.maximum(-h[t], r[t])
            spread = jnp.broadcast_to(change[s : s + 1], (8, N))
            h[t] = jnp.where(sub == s, h[t] + change, h[t])
            for j in range(K // 8):
                r[j] = r[j] - cols[j] * spread
    return state


def lanes_of(rows):
    return lax.broadcasted_iota(jnp.int32, (rows, N), 1)


def swapped(x):
    return pltpu.roll(x, K, 1)


def left_left(a, b):
    return jnp.where(lanes_of(a.shape[0]) < K, a, swapped(b))


def right_right(a, b):
    return jnp.where(lanes_of(a.shape[0]) < K, swapped(a), b)


def split_rows(x):
    return left_left(x[: K // 2], x[K // 2 :]), right_right(x[: K // 2], x[K // 2 :])


def pair_rows(a, b):
    return jnp.concatenate([left_left(a, b), right_right(a, b)], axis=0)


def corners(x):
    left = lanes_of(K) < K
    return jnp.concatenate([jnp.where(left, x, 0.0), jnp.where(left, 0.0, x)], axis=0)


def fold_grams(gram):
    rows = lax.broadcasted_iota(jnp.int32, (K, N), 0)
    other = swapped(gram)
    square = jnp.where(lanes_of(K) <= rows, gram, other)
    packed = left_left(square[: K // 2], square[K // 2 :])
    diag = jnp.sum(jnp.where(lanes_of(K) == rows, other, 0.0), axis=0, keepdims=True)
    return jnp.concatenate([packed, jnp.broadcast_to(diag, (8, N))], axis=0)


def unfold_grams(a, b):
    square = pair_rows(a[: K // 2], b[: K // 2])
    turned = corners(square).T
    turned = turned[:K] + turned[K:]
    diag = left_left(a[K // 2 :], b[K // 2 :])[:1]
    rows = lax.broadcasted_iota(jnp.int32, (K, N), 0)
    cols = lanes_of(K) % K
    first = jnp.where(cols <= rows, square, turned)
    second = jnp.where(cols < rows, turned, jnp.where(cols == rows, diag, square))
    return first, first + second


def front_kernel(dmap, sweeps, x, picks, w, v, loads, keep, send, w_own, v_own, table):
    core = lax.axis_index("c")
    tile = core * 8 + lax.axis_index("xh") * 4 + lax.axis_index("z")
    count = sweeps[dmap[0]]
    shared, specific = w[...], v[0]
    mixed = shared + specific

    @pl.when(tile < 15)
    def _():
        at = pl.multiple_of(jnp.minimum(tile, 14) * N, N)
        w_own[...] = w[:, pl.ds(at, N)]
        v_own[...] = v[0, :, pl.ds(at, N)]

    @pl.when(tile == 15)
    def _():
        w_own[...] = jnp.zeros((K, N), F32)
        v_own[...] = jnp.zeros((K, N), F32)
        w_own[:, :LAST] = w[:, 15 * N :]
        v_own[:, :LAST] = v[0, :, 15 * N :]

    gram = dot_nt(mixed, mixed, HIGHEST) + LAMBDA * dot_nt(specific, specific, HIGHEST)
    inverse = 1.0 / (diagonal(gram) + EPSILON)
    scaled = gram * inverse
    for k in range(K):
        table[k] = jnp.broadcast_to(scaled[:, k : k + 1], (K, N))

    pool = lax.broadcasted_iota(jnp.int32, (x.shape[1], N), 0)
    choose = jnp.concatenate(
        [(pool == picks[r : r + 1, :]).astype(F32).astype(BF16) for r in range(2)], axis=1
    )
    cells = jnp.dot(x[...], choose, preferred_element_type=F32).astype(BF16)
    target = jnp.dot(mixed.astype(BF16), cells, preferred_element_type=F32) * inverse

    def sweep(_, carry):
        state = [list(carry[0]), list(carry[1])]
        residual = [list(carry[2]), list(carry[3])]
        coordinate_steps(state, residual, lambda k: [table[k, 8 * j : 8 * j + 8] for j in range(K // 8)])
        return (tuple(state[0]), tuple(state[1]), tuple(residual[0]), tuple(residual[1]))

    none = tuple(jnp.zeros((8, N), F32) for _ in range(K // 8))
    carry = (none, none, tuple(rows_of(target[:, :N])), tuple(rows_of(target[:, N:])))
    carry = lax.fori_loop(0, count, sweep, carry)
    first = jnp.concatenate(carry[0], axis=0)
    second = jnp.concatenate(carry[1], axis=0)
    loads[0] = first
    loads[1] = second
    zero = jnp.zeros((K, N), F32)
    both = jnp.concatenate([first, second], axis=1)
    block = jnp.concatenate(
        [jnp.concatenate([first, zero], axis=1), jnp.concatenate([zero, second], axis=1)], axis=0
    )
    gram_part = fold_grams(dot_nt(both, block, HIGHEST))
    keep[HALF:] = gram_part
    send[HALF:] = gram_part
    rounded = block.astype(BF16)
    low = dot_nt(cells[:HALF], rounded)
    high = dot_nt(cells[HALF:], rounded)

    @pl.when(core == 0)
    def _():
        keep[:HALF] = low
        send[: G - HALF] = high
        send[G - HALF : HALF] = jnp.zeros((2 * HALF - G, N), F32)

    @pl.when(core == 1)
    def _():
        send[:HALF] = low
        keep[: G - HALF] = high
        keep[G - HALF : HALF] = jnp.zeros((2 * HALF - G, N), F32)


def pack_kernel(keep, came, out):
    gram = keep[HALF:] + came[HALF:]
    for i in range(8):
        out[i, :N] = keep[N * i : N * i + N] + came[N * i : N * i + N]
        out[i, N:] = gram


def group_kernel(came, v_own, out):
    total = came[0]
    for i in range(1, 8):
        total = total + came[i]
    rows = total[:N].T
    first, second = rows[:K], rows[:K] + rows[K:]
    stats = (left_left(first, second), right_right(first, second))
    bases = split_rows(v_own[...])
    for i in range(8):
        out[i, :K] = stats[i % 2]
        out[i, K : K + K // 2] = bases[i % 2]
        out[i, K + K // 2 :] = total[N:]


def dot_split(a, b):
    a_high = a.astype(BF16)
    b_high = b.astype(BF16)
    a_low = (a - a_high.astype(F32)).astype(BF16)
    b_low = (b - b_high.astype(F32)).astype(BF16)
    out = jnp.dot(a_high, b_low, preferred_element_type=F32)
    out = out + jnp.dot(a_low, b_high, preferred_element_type=F32)
    return out + jnp.dot(a_high, b_high, preferred_element_type=F32)


def one_pass(state, residual, tables, paired):
    sub = lax.broadcasted_iota(jnp.int32, (8, N), 0)
    half = jnp.where(lanes_of(8) < K, 0, K)
    for k in range(K):
        t, s = divmod(k, 8)
        for h, r, table in zip(state, residual, tables):
            change = jnp.maximum(-h[t], r[t])
            spread = jnp.broadcast_to(change[s : s + 1], (8, N))
            h[t] = jnp.where(sub == s, h[t] + change, h[t])
            for j in range(t if s < 7 else t + 1, K // 8):
                weight = table[8 * j : 8 * j + 8]
                if paired:
                    weight = jnp.take_along_axis(weight, half + k, axis=1, mode="promise_in_bounds")
                else:
                    weight = jnp.broadcast_to(weight[:, k : k + 1], (8, N))
                r[j] = r[j] - weight * spread
    return [jnp.concatenate(h, axis=0) for h in state]


def both_halves(x):
    return x + swapped(x)


def shared_pass(shared, gram, carried):
    inverse = 1.0 / jnp.maximum(diagonal(gram[:, :K]), 1.0)
    start = carried - dot_split(gram, jnp.concatenate([shared, jnp.zeros((K, N), F32)], axis=0))
    return one_pass([rows_of(shared)], [rows_of(start * inverse)], [gram * inverse], False)[0]


def ridge_scale(gram):
    rows = lax.broadcasted_iota(jnp.int32, (K, N), 0)
    left = jnp.sum(jnp.where(lanes_of(K) == rows, gram, 0.0), axis=1, keepdims=True)
    right = jnp.sum(jnp.where(lanes_of(K) == rows + K, gram, 0.0), axis=1, keepdims=True)
    return 1.0 / jnp.maximum(RIDGE * jnp.where(lanes_of(K) < K, left, right), 1.0)


def update_kernel(came, w_own, out, stats, grams_next, v_first):
    at_y, at_xl = lax.axis_index("y"), lax.axis_index("xl")
    pairs = range(4)
    stat, base, grams = [], [], []
    for p in pairs:
        a, b = 2 * p, 2 * p + 1
        stat.append(left_left(came[a, :K], came[b, :K]))
        stats[p] = right_right(came[a, :K], came[b, :K])
        base.append(pair_rows(came[a, K : K + K // 2], came[b, K : K + K // 2]))
        first, both = unfold_grams(came[a, K + K // 2 :], came[b, K + K // 2 :])
        grams.append(first)
        grams_next[p] = both
    wide = w_own[...]
    shared = jnp.where(at_xl == 0, left_left(wide, wide), right_right(wide, wide))

    pulls = [dot_split(grams[p], corners(base[p])) for p in pairs]
    carried = sum(stat[p] - pulls[p] for p in pairs)
    shared = shared_pass(shared, both_halves(sum(grams)), both_halves(carried))

    pushed = dot_split(jnp.concatenate(grams, axis=0), corners(shared))
    state, residual, tables = [], [], []
    for p in pairs:
        inverse = ridge_scale(grams[p])
        rest = stat[p] - pushed[K * p : K * p + K] - RIDGE * pulls[p]
        state.append(rows_of(base[p]))
        residual.append(rows_of(rest * inverse))
        tables.append((RIDGE * grams[p]) * inverse)
    values = one_pass(state, residual, tables, True)
    for p in pairs:
        v_first[p] = values[p]

    later = [grams_next[p] for p in pairs]
    pulled = dot_split(jnp.concatenate(later, axis=1), jnp.concatenate([corners(v) for v in values], axis=0))
    carried = sum(stats[p] for p in pairs) - pulled
    shared = shared_pass(shared, both_halves(sum(later)), both_halves(carried))

    gram, specific = grams_next[at_y], v_first[at_y]
    inverse = ridge_scale(gram)
    rest = stats[at_y] - dot_split(gram, corners(shared + RIDGE * specific))
    (specific,) = one_pass([rows_of(specific)], [rows_of(rest * inverse)], [(RIDGE * gram) * inverse], True)
    pieces = (left_left(shared, specific), jnp.where(lanes_of(K) < K, shared, specific))
    for i in range(16):
        out[i] = pieces[i // 8]


def finish_kernel(mine, other, w, v):
    core = lax.axis_index("c")

    def write(first, second):
        for half, part in enumerate((first, second)):
            for i in range(8):
                at = (8 * half + i) * N
                wide = min(N, G - at)
                w[:, at : at + wide] = left_left(part[i], part[8 + i])[:, :wide]
                v[0, :, at : at + wide] = right_right(part[i], part[8 + i])[:, :wide]

    @pl.when(core == 0)
    def _():
        write(mine, other)

    @pl.when(core == 1)
    def _():
        write(other, mine)


def shape(*dims):
    return jax.ShapeDtypeStruct(dims, F32)


def near(*dims):
    return pltpu.VMEM(dims, F32)


def held(x):
    return pltpu.with_memory_space_constraint(x, pltpu.VMEM)


VM = pl.BlockSpec(memory_space=pltpu.VMEM)
SM = pl.BlockSpec(memory_space=pltpu.SMEM)
SWAP = [(0, 1), (1, 0)]


def on_device(expression, dataset_id, dataset_map, sweep_count, picks, shared_init, specific_init):
    loads, keep, send, w_own, v_own = pl.pallas_call(
        front_kernel,
        name="front",
        out_shape=(shape(2, K, N), near(HALF + PACKED, N), near(HALF + PACKED, N), near(K, N), near(K, N)),
        in_specs=[SM, SM, VM, VM, VM, VM],
        out_specs=[VM] * 5,
        scratch_shapes=[pltpu.VMEM((K, K, N), F32)],
    )(dataset_map, sweep_count, expression, picks, shared_init, specific_init)
    came = lax.ppermute(send, "c", SWAP)
    packed = pl.pallas_call(
        pack_kernel, name="pack", out_shape=near(8, N + PACKED, N), in_specs=[VM, VM], out_specs=VM
    )(held(keep), held(came))
    came = lax.all_to_all(packed, RING, 0, 0, tiled=True)
    spread = pl.pallas_call(
        group_kernel, name="group", out_shape=near(8, K + K // 2 + PACKED, N), in_specs=[VM, VM], out_specs=VM
    )(held(came), held(v_own))
    came = lax.all_to_all(spread, GRP, 0, 0, tiled=True)
    spread = pl.pallas_call(
        update_kernel,
        name="update",
        out_shape=near(16, K, N),
        in_specs=[VM, VM],
        out_specs=VM,
        scratch_shapes=[pltpu.VMEM((4, K, N), F32)] * 3,
    )(held(came), held(w_own))
    mine = lax.all_to_all(spread, PLANE, 0, 0, tiled=True)
    other = lax.ppermute(mine, "c", SWAP)
    shared, specific = pl.pallas_call(
        finish_kernel,
        name="finish",
        out_shape=(shape(K, G), shape(1, K, G)),
        in_specs=[VM, VM],
        out_specs=[VM, VM],
    )(held(mine), held(other))
    return loads, shared, specific


def solution(mesh):
    fine = Mesh(mesh.devices.reshape(4, 2, 2, 4, 2), ALL)
    return jax.shard_map(
        on_device,
        mesh=fine,
        in_specs=(P(None, ALL), P(ALL), P(GRP), P(), P(None, ALL), P(), P(GRP, None, None)),
        out_specs=(P(None, None, ALL), P(), P(GRP, None, None)),
        check_vma=False,
    )
```

```python
import jax
import jax.numpy as jnp
from jax import lax
from jax.experimental import pallas as pl
from jax.experimental.pallas import tpu as pltpu
from jax.sharding import Mesh, PartitionSpec as P

K = 64
G = 2000
N = 128
HALF = 8 * N
PACKED = K // 2 + 8
LAST = G - 15 * N
EPSILON = 1e-06
LAMBDA = 5.0
RIDGE = 1.0 + LAMBDA
HIGHEST = lax.Precision.HIGHEST
GRP = ("y", "xl")
RING = ("xh", "z")
PLANE = ("xl", "xh", "z")
ALL = ("y", "xl", "xh", "z", "c")
NT = (((1,), (1,)), ((), ()))
F32 = jnp.float32
BF16 = jnp.bfloat16


def dot_nt(a, b, precision=None):
    return lax.dot_general(a, b, NT, precision=precision, preferred_element_type=F32)


def diagonal(square):
    n = square.shape[0]
    rows = lax.broadcasted_iota(jnp.int32, (n, n), 0)
    cols = lax.broadcasted_iota(jnp.int32, (n, n), 1)
    return jnp.sum(jnp.where(rows == cols, square, 0.0), axis=1, keepdims=True)


def rows_of(x):
    return [x[8 * t : 8 * t + 8] for t in range(K // 8)]


def coordinate_steps(state, residual, column, last):
    sub = lax.broadcasted_iota(jnp.int32, (8, N), 0)
    for k in range(K):
        t, s = divmod(k, 8)
        for half, (h, r) in enumerate(zip(state, residual)):
            change = jnp.maximum(-h[t], r[t])
            spread = jnp.broadcast_to(change[s : s + 1], (8, N))
            h[t] = jnp.where(sub == s, h[t] + change, h[t])
            for j in range((t if s < 7 else t + 1) if last else 0, K // 8):
                r[j] = r[j] - column(half, k, j) * spread
    return [jnp.concatenate(h, axis=0) for h in state]


def lanes_of(rows):
    return lax.broadcasted_iota(jnp.int32, (rows, N), 1)


def swapped(x):
    return pltpu.roll(x, K, 1)


def left_left(a, b):
    return jnp.where(lanes_of(a.shape[0]) < K, a, swapped(b))


def right_right(a, b):
    return jnp.where(lanes_of(a.shape[0]) < K, swapped(a), b)


def split_rows(x):
    return left_left(x[: K // 2], x[K // 2 :]), right_right(x[: K // 2], x[K // 2 :])


def pair_rows(a, b):
    return jnp.concatenate([left_left(a, b), right_right(a, b)], axis=0)


def corners(x):
    left = lanes_of(K) < K
    return jnp.concatenate([jnp.where(left, x, 0.0), jnp.where(left, 0.0, x)], axis=0)


def fold_grams(gram):
    rows = lax.broadcasted_iota(jnp.int32, (K, N), 0)
    other = swapped(gram)
    square = jnp.where(lanes_of(K) <= rows, gram, other)
    packed = left_left(square[: K // 2], square[K // 2 :])
    diag = jnp.sum(jnp.where(lanes_of(K) == rows, other, 0.0), axis=0, keepdims=True)
    return jnp.concatenate([packed, jnp.broadcast_to(diag, (8, N))], axis=0)


def unfold_grams(a, b):
    square = pair_rows(a[: K // 2], b[: K // 2])
    turned = corners(square).T
    turned = turned[:K] + turned[K:]
    diag = left_left(a[K // 2 :], b[K // 2 :])[:1]
    rows = lax.broadcasted_iota(jnp.int32, (K, N), 0)
    cols = lanes_of(K) % K
    first = jnp.where(cols <= rows, square, turned)
    second = jnp.where(cols < rows, turned, jnp.where(cols == rows, diag, square))
    return first, first + second


def split(x):
    high = x.astype(BF16)
    return high, (x - high.astype(F32)).astype(BF16)


def gram_of(high, low):
    both = dot_nt(jnp.concatenate([high, low], axis=0), high)
    return both[:K], both[K:]


CHUNK = 512


def front_kernel(
    picks, dmap_hbm, sweeps_hbm, x_hbm, w_hbm, v_hbm,
    send, cells, state, w_own, v_own,
    x, w, v, dmap, sweeps, table, sems,
):
    core = lax.axis_index("c")
    tile = core * 8 + lax.axis_index("xh") * 4 + lax.axis_index("z")
    spans = [(at, min(CHUNK, G - at)) for at in range(0, G, CHUNK)]
    early = [
        pltpu.make_async_copy(w_hbm, w, sems.at[0]),
        pltpu.make_async_copy(v_hbm.at[0], v, sems.at[1]),
        pltpu.make_async_copy(dmap_hbm, dmap, sems.at[2]),
        pltpu.make_async_copy(sweeps_hbm, sweeps, sems.at[3]),
    ]
    parts = [
        pltpu.make_async_copy(x_hbm.at[pl.ds(at, rows)], x.at[pl.ds(at, rows)], sems.at[4 + i])
        for i, (at, rows) in enumerate(spans)
    ]
    for copy in early + parts:
        copy.start()
    early[0].wait()
    early[1].wait()

    @pl.when(tile < 15)
    def _():
        at = pl.multiple_of(jnp.minimum(tile, 14) * N, N)
        w_own[...] = w[:, pl.ds(at, N)]
        v_own[...] = v[:, pl.ds(at, N)]

    @pl.when(tile == 15)
    def _():
        w_own[...] = jnp.zeros((K, N), F32)
        v_own[...] = jnp.zeros((K, N), F32)
        w_own[:, :LAST] = w[:, 15 * N :]
        v_own[:, :LAST] = v[:, 15 * N :]

    specific = v[...]
    mixed_high, mixed_low = split(w[...] + specific)
    mixed_gram, mixed_cross = gram_of(mixed_high, mixed_low)
    own_gram, own_cross = gram_of(*split(specific))
    cross = mixed_cross + LAMBDA * own_cross
    gram = mixed_gram + LAMBDA * own_gram + cross + cross.T
    inverse = 1.0 / (diagonal(gram) + EPSILON)
    scaled = gram * inverse
    for k in range(K):
        table[k] = jnp.broadcast_to(scaled[:, k : k + 1], (K, N))

    pool = lax.broadcasted_iota(jnp.int32, (x.shape[1], N), 0)
    choose = jnp.concatenate(
        [(pool == picks[r : r + 1, :]).astype(F32).astype(BF16) for r in range(2)], axis=1
    )
    for copy, (at, rows) in zip(parts, spans):
        copy.wait()
        part = jnp.dot(x[at : at + rows], choose, preferred_element_type=F32)
        cells[at : at + rows] = part.astype(BF16)
    cells[G:] = jnp.zeros((2 * HALF - G, 2 * N), BF16)
    target = jnp.dot(mixed_high, cells[:G], preferred_element_type=F32) * inverse
    early[2].wait()
    early[3].wait()
    count = sweeps[dmap[0]]

    def column(_, k, j):
        return table[k, 8 * j : 8 * j + 8]

    def sweep(_, carry):
        parts = [list(part) for part in carry]
        coordinate_steps(parts[:2], parts[2:], column, False)
        return tuple(tuple(part) for part in parts)

    none = tuple(jnp.zeros((8, N), F32) for _ in range(K // 8))
    carry = (none, none, tuple(rows_of(target[:, :N])), tuple(rows_of(target[:, N:])))
    parts = [list(part) for part in lax.fori_loop(0, count - 1, sweep, carry)]
    first, second = coordinate_steps(parts[:2], parts[2:], column, True)
    zero = jnp.zeros((K, N), F32)
    both = jnp.concatenate([first, second], axis=1)
    block = jnp.concatenate(
        [jnp.concatenate([first, zero], axis=1), jnp.concatenate([zero, second], axis=1)], axis=0
    )
    state[...] = block
    away = pl.multiple_of((1 - core) * HALF, HALF)
    send[:HALF] = dot_nt(cells[pl.ds(away, HALF)], block.astype(BF16))
    send[HALF:] = fold_grams(dot_nt(both, block, HIGHEST))


def keep_kernel(cells, state, keep, loads):
    core = lax.axis_index("c")
    home = pl.multiple_of(core * HALF, HALF)
    block = state[...]
    loads[0] = block[:K, :N]
    loads[1] = block[K:, N:]
    keep[...] = dot_nt(cells[pl.ds(home, HALF)], block.astype(BF16))


def pack_kernel(keep, send, came, out):
    gram = send[HALF:] + came[HALF:]
    for i in range(8):
        out[i, :N] = keep[N * i : N * i + N] + came[N * i : N * i + N]
        out[i, N:] = gram


def group_kernel(came, v_own, out):
    total = came[0]
    for i in range(1, 8):
        total = total + came[i]
    rows = total[:N].T
    first, second = rows[:K], rows[:K] + rows[K:]
    stats = (left_left(first, second), right_right(first, second))
    bases = split_rows(v_own[...])
    for i in range(8):
        out[i, :K] = stats[i % 2]
        out[i, K : K + K // 2] = bases[i % 2]
        out[i, K + K // 2 :] = total[N:]


def dot_split(a, b):
    a_high = a.astype(BF16)
    b_high = b.astype(BF16)
    a_low = (a - a_high.astype(F32)).astype(BF16)
    b_low = (b - b_high.astype(F32)).astype(BF16)
    out = jnp.dot(a_high, b_low, preferred_element_type=F32)
    out = out + jnp.dot(a_low, b_high, preferred_element_type=F32)
    return out + jnp.dot(a_high, b_high, preferred_element_type=F32)


def one_pass(state, residual, tables, paired):
    sub = lax.broadcasted_iota(jnp.int32, (8, N), 0)
    half = jnp.where(lanes_of(8) < K, 0, K)
    for k in range(K):
        t, s = divmod(k, 8)
        for h, r, table in zip(state, residual, tables):
            change = jnp.maximum(-h[t], r[t])
            spread = jnp.broadcast_to(change[s : s + 1], (8, N))
            h[t] = jnp.where(sub == s, h[t] + change, h[t])
            for j in range(t if s < 7 else t + 1, K // 8):
                weight = table[8 * j : 8 * j + 8]
                if paired:
                    weight = jnp.take_along_axis(weight, half + k, axis=1, mode="promise_in_bounds")
                else:
                    weight = jnp.broadcast_to(weight[:, k : k + 1], (8, N))
                r[j] = r[j] - weight * spread
    return [jnp.concatenate(h, axis=0) for h in state]


def both_halves(x):
    return x + swapped(x)


def shared_pass(shared, gram, carried):
    inverse = 1.0 / jnp.maximum(diagonal(gram[:, :K]), 1.0)
    start = carried - dot_split(gram, jnp.concatenate([shared, jnp.zeros((K, N), F32)], axis=0))
    return one_pass([rows_of(shared)], [rows_of(start * inverse)], [gram * inverse], False)[0]


def ridge_scale(gram):
    rows = lax.broadcasted_iota(jnp.int32, (K, N), 0)
    left = jnp.sum(jnp.where(lanes_of(K) == rows, gram, 0.0), axis=1, keepdims=True)
    right = jnp.sum(jnp.where(lanes_of(K) == rows + K, gram, 0.0), axis=1, keepdims=True)
    return 1.0 / jnp.maximum(RIDGE * jnp.where(lanes_of(K) < K, left, right), 1.0)


def update_kernel(came, w_own, out, stats, grams_next, v_first):
    at_y, at_xl = lax.axis_index("y"), lax.axis_index("xl")
    pairs = range(4)
    stat, base, grams = [], [], []
    for p in pairs:
        a, b = 2 * p, 2 * p + 1
        stat.append(left_left(came[a, :K], came[b, :K]))
        stats[p] = right_right(came[a, :K], came[b, :K])
        base.append(pair_rows(came[a, K : K + K // 2], came[b, K : K + K // 2]))
        first, both = unfold_grams(came[a, K + K // 2 :], came[b, K + K // 2 :])
        grams.append(first)
        grams_next[p] = both
    wide = w_own[...]
    shared = jnp.where(at_xl == 0, left_left(wide, wide), right_right(wide, wide))

    pulls = [dot_split(grams[p], corners(base[p])) for p in pairs]
    carried = sum(stat[p] - pulls[p] for p in pairs)
    shared = shared_pass(shared, both_halves(sum(grams)), both_halves(carried))

    pushed = dot_split(jnp.concatenate(grams, axis=0), corners(shared))
    state, residual, tables = [], [], []
    for p in pairs:
        inverse = ridge_scale(grams[p])
        rest = stat[p] - pushed[K * p : K * p + K] - RIDGE * pulls[p]
        state.append(rows_of(base[p]))
        residual.append(rows_of(rest * inverse))
        tables.append((RIDGE * grams[p]) * inverse)
    values = one_pass(state, residual, tables, True)
    for p in pairs:
        v_first[p] = values[p]

    later = [grams_next[p] for p in pairs]
    pulled = dot_split(jnp.concatenate(later, axis=1), jnp.concatenate([corners(v) for v in values], axis=0))
    carried = sum(stats[p] for p in pairs) - pulled
    shared = shared_pass(shared, both_halves(sum(later)), both_halves(carried))

    gram, specific = grams_next[at_y], v_first[at_y]
    inverse = ridge_scale(gram)
    rest = stats[at_y] - dot_split(gram, corners(shared + RIDGE * specific))
    (specific,) = one_pass([rows_of(specific)], [rows_of(rest * inverse)], [(RIDGE * gram) * inverse], True)
    pieces = (left_left(shared, specific), jnp.where(lanes_of(K) < K, shared, specific))
    for i in range(16):
        out[i] = pieces[i // 8]


def finish_kernel(mine, other, w, v):
    core = lax.axis_index("c")

    def write(first, second):
        for half, part in enumerate((first, second)):
            for i in range(8):
                at = (8 * half + i) * N
                wide = min(N, G - at)
                w[:, at : at + wide] = left_left(part[i], part[8 + i])[:, :wide]
                v[0, :, at : at + wide] = right_right(part[i], part[8 + i])[:, :wide]

    @pl.when(core == 0)
    def _():
        write(mine, other)

    @pl.when(core == 1)
    def _():
        write(other, mine)


def shape(*dims):
    return jax.ShapeDtypeStruct(dims, F32)


def near(*dims):
    return pltpu.VMEM(dims, F32)


def held(x):
    return pltpu.with_memory_space_constraint(x, pltpu.VMEM)


VM = pl.BlockSpec(memory_space=pltpu.VMEM)
FAR = pl.BlockSpec(memory_space=pltpu.HBM)
SWAP = [(0, 1), (1, 0)]
LIMIT = pltpu.CompilerParams(vmem_limit_bytes=24 << 20)


def on_device(expression, dataset_id, dataset_map, sweep_count, picks, shared_init, specific_init):
    send, cells, state, w_own, v_own = pl.pallas_call(
        front_kernel,
        name="front",
        out_shape=(
            near(HALF + PACKED, N),
            pltpu.VMEM((2 * HALF, 2 * N), BF16),
            near(N, 2 * N),
            near(K, N),
            near(K, N),
        ),
        in_specs=[VM] + [FAR] * 5,
        out_specs=[VM] * 5,
        scratch_shapes=[
            pltpu.VMEM((G, expression.shape[1]), BF16),
            pltpu.VMEM((K, G), F32),
            pltpu.VMEM((K, G), F32),
            pltpu.SMEM(dataset_map.shape, jnp.int32),
            pltpu.SMEM(sweep_count.shape, jnp.int32),
            pltpu.VMEM((K, K, N), F32),
            pltpu.SemaphoreType.DMA((8,)),
        ],
    )(picks, dataset_map, sweep_count, expression, shared_init, specific_init)
    came = lax.ppermute(send, "c", SWAP)
    keep, loads = pl.pallas_call(
        keep_kernel,
        name="keep",
        compiler_params=LIMIT,
        out_shape=(near(HALF, N), shape(2, K, N)),
        in_specs=[VM, VM],
        out_specs=[VM, VM],
    )(held(cells), held(state))
    packed = pl.pallas_call(
        pack_kernel,
        name="pack",
        compiler_params=LIMIT,
        out_shape=near(8, N + PACKED, N),
        in_specs=[VM] * 3,
        out_specs=VM,
    )(held(keep), held(send), held(came))
    came = lax.all_to_all(packed, RING, 0, 0, tiled=True)
    spread = pl.pallas_call(
        group_kernel, name="group", compiler_params=LIMIT, out_shape=near(8, K + K // 2 + PACKED, N), in_specs=[VM, VM], out_specs=VM
    )(held(came), held(v_own))
    came = lax.all_to_all(spread, GRP, 0, 0, tiled=True)
    spread = pl.pallas_call(
        update_kernel,
        name="update",
        compiler_params=LIMIT,
        out_shape=near(16, K, N),
        in_specs=[VM, VM],
        out_specs=VM,
        scratch_shapes=[pltpu.VMEM((4, K, N), F32)] * 3,
    )(held(came), held(w_own))
    mine = lax.all_to_all(spread, PLANE, 0, 0, tiled=True)
    other = lax.ppermute(mine, "c", SWAP)
    shared, specific = pl.pallas_call(
        finish_kernel,
        name="finish",
        compiler_params=LIMIT,
        out_shape=(shape(K, G), shape(1, K, G)),
        in_specs=[VM, VM],
        out_specs=[VM, VM],
    )(held(mine), held(other))
    return loads, shared, specific


def solution(mesh):
    fine = Mesh(mesh.devices.reshape(4, 2, 2, 4, 2), ALL)
    return jax.shard_map(
        on_device,
        mesh=fine,
        in_specs=(P(None, ALL), P(ALL), P(GRP), P(), P(None, ALL), P(), P(GRP, None, None)),
        out_specs=(P(None, None, ALL), P(), P(GRP, None, None)),
        check_vma=False,
    )
```

```python
import jax
import jax.numpy as jnp
from jax import lax
from jax.experimental import pallas as pl
from jax.experimental.pallas import tpu as pltpu
from jax.sharding import Mesh, PartitionSpec as P

K = 64
G = 2000
N = 128
HALF = 8 * N
PACKED = K // 2 + 8
LAST = G - 15 * N
EPSILON = 1e-06
LAMBDA = 5.0
RIDGE = 1.0 + LAMBDA
HIGHEST = lax.Precision.HIGHEST
GRP = ("y", "xl")
RING = ("xh", "z")
PLANE = ("xl", "xh", "z")
ALL = ("y", "xl", "xh", "z", "c")
NT = (((1,), (1,)), ((), ()))
F32 = jnp.float32
BF16 = jnp.bfloat16


def dot_nt(a, b, precision=None):
    return lax.dot_general(a, b, NT, precision=precision, preferred_element_type=F32)


def diagonal(square):
    n = square.shape[0]
    rows = lax.broadcasted_iota(jnp.int32, (n, n), 0)
    cols = lax.broadcasted_iota(jnp.int32, (n, n), 1)
    return jnp.sum(jnp.where(rows == cols, square, 0.0), axis=1, keepdims=True)


def rows_of(x):
    return [x[8 * t : 8 * t + 8] for t in range(K // 8)]


def coordinate_steps(state, residual, column, last):
    sub = lax.broadcasted_iota(jnp.int32, (8, N), 0)
    for k in range(K):
        t, s = divmod(k, 8)
        for half, (h, r) in enumerate(zip(state, residual)):
            change = jnp.maximum(-h[t], r[t])
            spread = jnp.broadcast_to(change[s : s + 1], (8, N))
            h[t] = jnp.where(sub == s, h[t] + change, h[t])
            for j in range((t if s < 7 else t + 1) if last else 0, K // 8):
                r[j] = r[j] - column(half, k, j) * spread
    return [jnp.concatenate(h, axis=0) for h in state]


def lanes_of(rows):
    return lax.broadcasted_iota(jnp.int32, (rows, N), 1)


def swapped(x):
    return pltpu.roll(x, K, 1)


def left_left(a, b):
    return jnp.where(lanes_of(a.shape[0]) < K, a, swapped(b))


def right_right(a, b):
    return jnp.where(lanes_of(a.shape[0]) < K, swapped(a), b)


def split_rows(x):
    return left_left(x[: K // 2], x[K // 2 :]), right_right(x[: K // 2], x[K // 2 :])


def pair_rows(a, b):
    return jnp.concatenate([left_left(a, b), right_right(a, b)], axis=0)


def corners(x):
    left = lanes_of(K) < K
    return jnp.concatenate([jnp.where(left, x, 0.0), jnp.where(left, 0.0, x)], axis=0)


def fold_grams(gram):
    rows = lax.broadcasted_iota(jnp.int32, (K, N), 0)
    other = swapped(gram)
    square = jnp.where(lanes_of(K) <= rows, gram, other)
    packed = left_left(square[: K // 2], square[K // 2 :])
    diag = jnp.sum(jnp.where(lanes_of(K) == rows, other, 0.0), axis=0, keepdims=True)
    return jnp.concatenate([packed, jnp.broadcast_to(diag, (8, N))], axis=0)


def unfold_grams(a, b):
    square = pair_rows(a[: K // 2], b[: K // 2])
    turned = corners(square).T
    turned = turned[:K] + turned[K:]
    diag = left_left(a[K // 2 :], b[K // 2 :])[:1]
    rows = lax.broadcasted_iota(jnp.int32, (K, N), 0)
    cols = lanes_of(K) % K
    first = jnp.where(cols <= rows, square, turned)
    second = jnp.where(cols < rows, turned, jnp.where(cols == rows, diag, square))
    return first, first + second


def split(x):
    high = x.astype(BF16)
    return high, (x - high.astype(F32)).astype(BF16)


def gram_of(high, low):
    both = dot_nt(jnp.concatenate([high, low], axis=0), high)
    return both[:K], both[K:]


def front_kernel(
    picks_hbm, ids_hbm, sweeps_hbm, x_hbm, w_hbm, v_hbm,
    send, cells, state, w_own, v_own,
    picks, ids, sweeps, x, w, v, choose, table, sems,
):
    core = lax.axis_index("c")
    tile = core * 8 + lax.axis_index("xh") * 4 + lax.axis_index("z")
    copies = [
        pltpu.make_async_copy(source, target, sems.at[i])
        for i, (source, target) in enumerate(
            [
                (picks_hbm, picks),
                (w_hbm, w),
                (v_hbm.at[0], v),
                (x_hbm, x),
                (ids_hbm, ids),
                (sweeps_hbm, sweeps),
            ]
        )
    ]
    for copy in copies:
        copy.start()
    copies[0].wait()
    pool = lax.broadcasted_iota(jnp.int32, (x.shape[1], N), 0)
    for r in range(2):
        choose[:, N * r : N * r + N] = (pool == picks[r : r + 1, :]).astype(F32).astype(BF16)
    cells[G:] = jnp.zeros((2 * HALF - G, 2 * N), BF16)
    copies[1].wait()
    copies[2].wait()

    @pl.when(tile < 15)
    def _():
        at = pl.multiple_of(jnp.minimum(tile, 14) * N, N)
        w_own[...] = w[:, pl.ds(at, N)]
        v_own[...] = v[:, pl.ds(at, N)]

    @pl.when(tile == 15)
    def _():
        w_own[...] = jnp.zeros((K, N), F32)
        v_own[...] = jnp.zeros((K, N), F32)
        w_own[:, :LAST] = w[:, 15 * N :]
        v_own[:, :LAST] = v[:, 15 * N :]

    specific = v[...]
    mixed_high, mixed_low = split(w[...] + specific)
    mixed_gram, mixed_cross = gram_of(mixed_high, mixed_low)
    own_gram, own_cross = gram_of(*split(specific))
    cross = mixed_cross + LAMBDA * own_cross
    gram = mixed_gram + LAMBDA * own_gram + cross + cross.T
    inverse = 1.0 / (diagonal(gram) + EPSILON)
    scaled = gram * inverse
    for copy in copies[3:]:
        copy.wait()
    cells[:G] = jnp.dot(x[...], choose[...], preferred_element_type=F32).astype(BF16)
    for k in range(K):
        table[k] = jnp.broadcast_to(scaled[:, k : k + 1], (K, N))
    target = jnp.dot(mixed_high, cells[:G], preferred_element_type=F32) * inverse
    count = sweeps[ids[0]]

    def column(_, k, j):
        return table[k, 8 * j : 8 * j + 8]

    def sweep(_, carry):
        parts = [list(part) for part in carry]
        coordinate_steps(parts[:2], parts[2:], column, False)
        return tuple(tuple(part) for part in parts)

    none = tuple(jnp.zeros((8, N), F32) for _ in range(K // 8))
    carry = (none, none, tuple(rows_of(target[:, :N])), tuple(rows_of(target[:, N:])))
    parts = [list(part) for part in lax.fori_loop(0, count - 1, sweep, carry)]
    first, second = coordinate_steps(parts[:2], parts[2:], column, True)
    zero = jnp.zeros((K, N), F32)
    both = jnp.concatenate([first, second], axis=1)
    block = jnp.concatenate(
        [jnp.concatenate([first, zero], axis=1), jnp.concatenate([zero, second], axis=1)], axis=0
    )
    state[...] = block
    away = pl.multiple_of((1 - core) * HALF, HALF)
    send[:HALF] = dot_nt(cells[pl.ds(away, HALF)], block.astype(BF16))
    send[HALF:] = fold_grams(dot_nt(both, block, HIGHEST))


def keep_kernel(cells, state, keep, loads):
    core = lax.axis_index("c")
    home = pl.multiple_of(core * HALF, HALF)
    block = state[...]
    loads[0] = block[:K, :N]
    loads[1] = block[K:, N:]
    keep[...] = dot_nt(cells[pl.ds(home, HALF)], block.astype(BF16))


def pack_kernel(keep, send, came, out):
    gram = send[HALF:] + came[HALF:]
    for i in range(8):
        out[i, :N] = keep[N * i : N * i + N] + came[N * i : N * i + N]
        out[i, N:] = gram


def group_kernel(came, v_own, out):
    total = came[0]
    for i in range(1, 8):
        total = total + came[i]
    rows = total[:N].T
    first, second = rows[:K], rows[:K] + rows[K:]
    stats = (left_left(first, second), right_right(first, second))
    bases = split_rows(v_own[...])
    for i in range(8):
        out[i, :K] = stats[i % 2]
        out[i, K : K + K // 2] = bases[i % 2]
        out[i, K + K // 2 :] = total[N:]


def dot_split(a, b):
    a_high = a.astype(BF16)
    b_high = b.astype(BF16)
    a_low = (a - a_high.astype(F32)).astype(BF16)
    b_low = (b - b_high.astype(F32)).astype(BF16)
    out = jnp.dot(a_high, b_low, preferred_element_type=F32)
    out = out + jnp.dot(a_low, b_high, preferred_element_type=F32)
    return out + jnp.dot(a_high, b_high, preferred_element_type=F32)


def one_pass(state, residual, tables, paired):
    sub = lax.broadcasted_iota(jnp.int32, (8, N), 0)
    half = jnp.where(lanes_of(8) < K, 0, K)
    for k in range(K):
        t, s = divmod(k, 8)
        for h, r, table in zip(state, residual, tables):
            change = jnp.maximum(-h[t], r[t])
            spread = jnp.broadcast_to(change[s : s + 1], (8, N))
            h[t] = jnp.where(sub == s, h[t] + change, h[t])
            for j in range(t if s < 7 else t + 1, K // 8):
                weight = table[8 * j : 8 * j + 8]
                if paired:
                    weight = jnp.take_along_axis(weight, half + k, axis=1, mode="promise_in_bounds")
                else:
                    weight = jnp.broadcast_to(weight[:, k : k + 1], (8, N))
                r[j] = r[j] - weight * spread
    return [jnp.concatenate(h, axis=0) for h in state]


def both_halves(x):
    return x + swapped(x)


def shared_pass(shared, gram, carried):
    inverse = 1.0 / jnp.maximum(diagonal(gram[:, :K]), 1.0)
    start = carried - dot_split(gram, jnp.concatenate([shared, jnp.zeros((K, N), F32)], axis=0))
    return one_pass([rows_of(shared)], [rows_of(start * inverse)], [gram * inverse], False)[0]


def ridge_scale(gram):
    rows = lax.broadcasted_iota(jnp.int32, (K, N), 0)
    left = jnp.sum(jnp.where(lanes_of(K) == rows, gram, 0.0), axis=1, keepdims=True)
    right = jnp.sum(jnp.where(lanes_of(K) == rows + K, gram, 0.0), axis=1, keepdims=True)
    return 1.0 / jnp.maximum(RIDGE * jnp.where(lanes_of(K) < K, left, right), 1.0)


def update_kernel(came, w_own, out, stats, grams_next, v_first):
    at_y, at_xl = lax.axis_index("y"), lax.axis_index("xl")
    pairs = range(4)
    stat, base, grams = [], [], []
    for p in pairs:
        a, b = 2 * p, 2 * p + 1
        stat.append(left_left(came[a, :K], came[b, :K]))
        stats[p] = right_right(came[a, :K], came[b, :K])
        base.append(pair_rows(came[a, K : K + K // 2], came[b, K : K + K // 2]))
        first, both = unfold_grams(came[a, K + K // 2 :], came[b, K + K // 2 :])
        grams.append(first)
        grams_next[p] = both
    wide = w_own[...]
    shared = jnp.where(at_xl == 0, left_left(wide, wide), right_right(wide, wide))

    pulls = [dot_split(grams[p], corners(base[p])) for p in pairs]
    carried = sum(stat[p] - pulls[p] for p in pairs)
    shared = shared_pass(shared, both_halves(sum(grams)), both_halves(carried))

    pushed = dot_split(jnp.concatenate(grams, axis=0), corners(shared))
    state, residual, tables = [], [], []
    for p in pairs:
        inverse = ridge_scale(grams[p])
        rest = stat[p] - pushed[K * p : K * p + K] - RIDGE * pulls[p]
        state.append(rows_of(base[p]))
        residual.append(rows_of(rest * inverse))
        tables.append((RIDGE * grams[p]) * inverse)
    values = one_pass(state, residual, tables, True)
    for p in pairs:
        v_first[p] = values[p]

    later = [grams_next[p] for p in pairs]
    pulled = dot_split(jnp.concatenate(later, axis=1), jnp.concatenate([corners(v) for v in values], axis=0))
    carried = sum(stats[p] for p in pairs) - pulled
    shared = shared_pass(shared, both_halves(sum(later)), both_halves(carried))

    gram, specific = grams_next[at_y], v_first[at_y]
    inverse = ridge_scale(gram)
    rest = stats[at_y] - dot_split(gram, corners(shared + RIDGE * specific))
    (specific,) = one_pass([rows_of(specific)], [rows_of(rest * inverse)], [(RIDGE * gram) * inverse], True)
    pieces = (left_left(shared, specific), jnp.where(lanes_of(K) < K, shared, specific))
    for i in range(16):
        out[i] = pieces[i // 8]


def finish_kernel(part, *refs):
    w, v = refs[-2:]
    for i in range(8):
        w[:, N * i : N * i + N] = left_left(part[i], part[8 + i])
        v[0, :, N * i : N * i + N] = right_right(part[i], part[8 + i])


def finish(part, half, name, earlier=()):
    return pl.pallas_call(
        finish_kernel,
        name=name,
        compiler_params=LIMIT,
        grid=(1,),
        out_shape=(shape(K, G), shape(1, K, G)),
        in_specs=[VM] + [FAR] * len(earlier),
        out_specs=[
            pl.BlockSpec((K, HALF), lambda i: (0, half())),
            pl.BlockSpec((1, K, HALF), lambda i: (0, 0, half())),
        ],
        input_output_aliases={1: 0, 2: 1} if earlier else {},
    )(held(part), *earlier)


def shape(*dims):
    return jax.ShapeDtypeStruct(dims, F32)


def near(*dims):
    return pltpu.VMEM(dims, F32)


def held(x):
    return pltpu.with_memory_space_constraint(x, pltpu.VMEM)


VM = pl.BlockSpec(memory_space=pltpu.VMEM)
FAR = pl.BlockSpec(memory_space=pltpu.HBM)
SWAP = [(0, 1), (1, 0)]
LIMIT = pltpu.CompilerParams(vmem_limit_bytes=24 << 20)


def on_device(expression, dataset_id, dataset_map, sweep_count, picks, shared_init, specific_init):
    send, cells, state, w_own, v_own = pl.pallas_call(
        front_kernel,
        name="front",
        out_shape=(
            near(HALF + PACKED, N),
            pltpu.VMEM((2 * HALF, 2 * N), BF16),
            near(N, 2 * N),
            near(K, N),
            near(K, N),
        ),
        in_specs=[FAR] * 6,
        out_specs=[VM] * 5,
        scratch_shapes=[
            pltpu.VMEM(picks.shape, jnp.int32),
            pltpu.SMEM(dataset_id.shape, jnp.int32),
            pltpu.SMEM(sweep_count.shape, jnp.int32),
            pltpu.VMEM(expression.shape, BF16),
            pltpu.VMEM(shared_init.shape, F32),
            pltpu.VMEM(shared_init.shape, F32),
            pltpu.VMEM((expression.shape[1], 2 * N), BF16),
            pltpu.VMEM((K, K, N), F32),
            pltpu.SemaphoreType.DMA((6,)),
        ],
    )(picks, dataset_id, sweep_count, expression, shared_init, specific_init)
    came = lax.ppermute(send, "c", SWAP)
    keep, loads = pl.pallas_call(
        keep_kernel,
        name="keep",
        compiler_params=LIMIT,
        out_shape=(near(HALF, N), shape(2, K, N)),
        in_specs=[VM, VM],
        out_specs=[VM, VM],
    )(held(cells), held(state))
    packed = pl.pallas_call(
        pack_kernel,
        name="pack",
        compiler_params=LIMIT,
        out_shape=near(8, N + PACKED, N),
        in_specs=[VM] * 3,
        out_specs=VM,
    )(held(keep), held(send), held(came))
    came = lax.all_to_all(packed, RING, 0, 0, tiled=True)
    spread = pl.pallas_call(
        group_kernel, name="group", compiler_params=LIMIT, out_shape=near(8, K + K // 2 + PACKED, N), in_specs=[VM, VM], out_specs=VM
    )(held(came), held(v_own))
    came = lax.all_to_all(spread, GRP, 0, 0, tiled=True)
    spread = pl.pallas_call(
        update_kernel,
        name="update",
        compiler_params=LIMIT,
        out_shape=near(16, K, N),
        in_specs=[VM, VM],
        out_specs=VM,
        scratch_shapes=[pltpu.VMEM((4, K, N), F32)] * 3,
    )(held(came), held(w_own))
    mine = lax.all_to_all(spread, PLANE, 0, 0, tiled=True)
    other = lax.ppermute(mine, "c", SWAP)
    bases = finish(mine, lambda: lax.axis_index("c"), "mine")
    shared, specific = finish(other, lambda: 1 - lax.axis_index("c"), "other", bases)
    return loads, shared, specific


def solution(mesh):
    fine = Mesh(mesh.devices.reshape(4, 2, 2, 4, 2), ALL)
    return jax.shard_map(
        on_device,
        mesh=fine,
        in_specs=(P(None, ALL), P(ALL), P(GRP), P(), P(None, ALL), P(), P(GRP, None, None)),
        out_specs=(P(None, None, ALL), P(), P(GRP, None, None)),
        check_vma=False,
    )
```

```python
import jax
import jax.numpy as jnp
from jax import lax
from jax.experimental import pallas as pl
from jax.experimental.pallas import tpu as pltpu
from jax.sharding import Mesh, PartitionSpec as P

K = 64
G = 2000
N = 128
HALF = 8 * N
PACKED = K // 2 + 8
LAST = G - 15 * N
EPSILON = 1e-06
LAMBDA = 5.0
RIDGE = 1.0 + LAMBDA
HIGHEST = lax.Precision.HIGHEST
GRP = ("y", "xl")
RING = ("xh", "z")
PLANE = ("xl", "xh", "z")
ALL = ("y", "xl", "xh", "z", "c")
NT = (((1,), (1,)), ((), ()))
F32 = jnp.float32
BF16 = jnp.bfloat16


def dot_nt(a, b, precision=None):
    return lax.dot_general(a, b, NT, precision=precision, preferred_element_type=F32)


def diagonal(square):
    n = square.shape[0]
    rows = lax.broadcasted_iota(jnp.int32, (n, n), 0)
    cols = lax.broadcasted_iota(jnp.int32, (n, n), 1)
    return jnp.sum(jnp.where(rows == cols, square, 0.0), axis=1, keepdims=True)


def rows_of(x):
    return [x[8 * t : 8 * t + 8] for t in range(K // 8)]


def coordinate_steps(state, residual, column, last):
    sub = lax.broadcasted_iota(jnp.int32, (8, N), 0)
    for k in range(K):
        t, s = divmod(k, 8)
        for half, (h, r) in enumerate(zip(state, residual)):
            change = jnp.maximum(-h[t], r[t])
            spread = jnp.broadcast_to(change[s : s + 1], (8, N))
            h[t] = jnp.where(sub == s, h[t] + change, h[t])
            for j in range((t if s < 7 else t + 1) if last else 0, K // 8):
                r[j] = r[j] - column(half, k, j) * spread
    return [jnp.concatenate(h, axis=0) for h in state]


def lanes_of(rows):
    return lax.broadcasted_iota(jnp.int32, (rows, N), 1)


def swapped(x):
    return pltpu.roll(x, K, 1)


def left_left(a, b):
    return jnp.where(lanes_of(a.shape[0]) < K, a, swapped(b))


def right_right(a, b):
    return jnp.where(lanes_of(a.shape[0]) < K, swapped(a), b)


def split_rows(x):
    return left_left(x[: K // 2], x[K // 2 :]), right_right(x[: K // 2], x[K // 2 :])


def pair_rows(a, b):
    return jnp.concatenate([left_left(a, b), right_right(a, b)], axis=0)


def corners(x):
    left = lanes_of(K) < K
    return jnp.concatenate([jnp.where(left, x, 0.0), jnp.where(left, 0.0, x)], axis=0)


def fold_grams(gram):
    rows = lax.broadcasted_iota(jnp.int32, (K, N), 0)
    other = swapped(gram)
    square = jnp.where(lanes_of(K) <= rows, gram, other)
    packed = left_left(square[: K // 2], square[K // 2 :])
    diag = jnp.sum(jnp.where(lanes_of(K) == rows, other, 0.0), axis=0, keepdims=True)
    return jnp.concatenate([packed, jnp.broadcast_to(diag, (8, N))], axis=0)


def unfold_grams(a, b):
    square = pair_rows(a[: K // 2], b[: K // 2])
    turned = corners(square).T
    turned = turned[:K] + turned[K:]
    diag = left_left(a[K // 2 :], b[K // 2 :])[:1]
    rows = lax.broadcasted_iota(jnp.int32, (K, N), 0)
    cols = lanes_of(K) % K
    first = jnp.where(cols <= rows, square, turned)
    second = jnp.where(cols < rows, turned, jnp.where(cols == rows, diag, square))
    return first, first + second


def split(x):
    high = x.astype(BF16)
    return high, (x - high.astype(F32)).astype(BF16)


def gram_of(high, low):
    both = dot_nt(jnp.concatenate([high, low], axis=0), high)
    return both[:K], both[K:]


def front_kernel(
    picks_hbm, ids_hbm, sweeps_hbm, x_hbm, w_hbm, v_hbm,
    send, cells, state, w_own, v_own,
    picks, ids, sweeps, x, w, v, choose, table, sems,
):
    core = lax.axis_index("c")
    tile = core * 8 + lax.axis_index("xh") * 4 + lax.axis_index("z")
    copies = [
        pltpu.make_async_copy(source, target, sems.at[i])
        for i, (source, target) in enumerate(
            [
                (picks_hbm, picks),
                (w_hbm, w),
                (v_hbm.at[0], v),
                (x_hbm, x),
                (ids_hbm, ids),
                (sweeps_hbm, sweeps),
            ]
        )
    ]
    for copy in copies:
        copy.start()
    copies[0].wait()
    pool = lax.broadcasted_iota(jnp.int32, (x.shape[1], N), 0)
    for r in range(2):
        choose[:, N * r : N * r + N] = (pool == picks[r : r + 1, :]).astype(F32).astype(BF16)
    cells[G:] = jnp.zeros((2 * HALF - G, 2 * N), BF16)
    copies[1].wait()
    copies[2].wait()

    @pl.when(tile < 15)
    def _():
        at = pl.multiple_of(jnp.minimum(tile, 14) * N, N)
        w_own[...] = w[:, pl.ds(at, N)]
        v_own[...] = v[:, pl.ds(at, N)]

    @pl.when(tile == 15)
    def _():
        w_own[...] = jnp.zeros((K, N), F32)
        v_own[...] = jnp.zeros((K, N), F32)
        w_own[:, :LAST] = w[:, 15 * N :]
        v_own[:, :LAST] = v[:, 15 * N :]

    specific = v[...]
    mixed_high, mixed_low = split(w[...] + specific)
    mixed_gram, mixed_cross = gram_of(mixed_high, mixed_low)
    own_gram, own_cross = gram_of(*split(specific))
    cross = mixed_cross + LAMBDA * own_cross
    gram = mixed_gram + LAMBDA * own_gram + cross + cross.T
    inverse = 1.0 / (diagonal(gram) + EPSILON)
    scaled = gram * inverse
    for copy in copies[3:]:
        copy.wait()
    cells[:G] = jnp.dot(x[...], choose[...], preferred_element_type=F32).astype(BF16)
    for k in range(K):
        table[k] = jnp.broadcast_to(scaled[:, k : k + 1], (K, N))
    target = jnp.dot(mixed_high, cells[:G], preferred_element_type=F32) * inverse
    count = sweeps[ids[0]]

    def column(_, k, j):
        return table[k, 8 * j : 8 * j + 8]

    def sweep(_, carry):
        parts = [list(part) for part in carry]
        coordinate_steps(parts[:2], parts[2:], column, False)
        return tuple(tuple(part) for part in parts)

    none = tuple(jnp.zeros((8, N), F32) for _ in range(K // 8))
    carry = (none, none, tuple(rows_of(target[:, :N])), tuple(rows_of(target[:, N:])))
    parts = [list(part) for part in lax.fori_loop(0, count - 1, sweep, carry)]
    first, second = coordinate_steps(parts[:2], parts[2:], column, True)
    zero = jnp.zeros((K, N), F32)
    both = jnp.concatenate([first, second], axis=1)
    block = jnp.concatenate(
        [jnp.concatenate([first, zero], axis=1), jnp.concatenate([zero, second], axis=1)], axis=0
    )
    state[...] = block
    away = pl.multiple_of((1 - core) * HALF, HALF)
    send[:HALF] = dot_nt(cells[pl.ds(away, HALF)], block.astype(BF16))
    send[HALF:] = fold_grams(dot_nt(both, block, HIGHEST))


def keep_kernel(cells, state, keep, loads, spread):
    rows = lax.broadcasted_iota(jnp.int32, (2 * N, N), 0) % N
    at = rows - jnp.where(lanes_of(2 * N) < K, 0, K)
    for k in range(K):
        spread[:, N * k : N * k + N] = (at == k).astype(F32).astype(BF16)
    core = lax.axis_index("c")
    home = pl.multiple_of(core * HALF, HALF)
    block = state[...]
    loads[0] = block[:K, :N]
    loads[1] = block[K:, N:]
    keep[...] = dot_nt(cells[pl.ds(home, HALF)], block.astype(BF16))


def pack_kernel(keep, send, came, out):
    gram = send[HALF:] + came[HALF:]
    for i in range(8):
        out[i, :N] = keep[N * i : N * i + N] + came[N * i : N * i + N]
        out[i, N:] = gram


def group_kernel(came, v_own, out):
    total = came[0]
    for i in range(1, 8):
        total = total + came[i]
    rows = total[:N].T
    first, second = rows[:K], rows[:K] + rows[K:]
    stats = (left_left(first, second), right_right(first, second))
    bases = split_rows(v_own[...])
    for i in range(8):
        out[i, :K] = stats[i % 2]
        out[i, K : K + K // 2] = bases[i % 2]
        out[i, K + K // 2 :] = total[N:]


def dot_split(a, b):
    a_high = a.astype(BF16)
    b_high = b.astype(BF16)
    a_low = (a - a_high.astype(F32)).astype(BF16)
    b_low = (b - b_high.astype(F32)).astype(BF16)
    out = jnp.dot(a_high, b_low, preferred_element_type=F32)
    out = out + jnp.dot(a_low, b_high, preferred_element_type=F32)
    return out + jnp.dot(a_high, b_high, preferred_element_type=F32)


def one_pass(state, residual, weight, beside=None):
    sub = lax.broadcasted_iota(jnp.int32, (8, N), 0)
    for k in range(K):
        t, s = divmod(k, 8)
        if beside is not None:
            beside(k)
        for i, (h, r) in enumerate(zip(state, residual)):
            change = jnp.maximum(-h[t], r[t])
            spread = jnp.broadcast_to(change[s : s + 1], (8, N))
            h[t] = jnp.where(sub == s, h[t] + change, h[t])
            for j in range(t if s < 7 else t + 1, K // 8):
                r[j] = r[j] - weight(i, k, j) * spread
    return [jnp.concatenate(h, axis=0) for h in state]


def column_of(table, k, j):
    return jnp.broadcast_to(table[8 * j : 8 * j + 8, k : k + 1], (8, N))


def columns_of(table, k, j):
    half = jnp.where(lanes_of(8) < K, k, K + k)
    return jnp.take_along_axis(table[8 * j : 8 * j + 8], half, axis=1, mode="promise_in_bounds")


def both_halves(x):
    return x + swapped(x)


def shared_start(shared, gram, inverse, carried):
    start = carried - dot_split(gram, jnp.concatenate([shared, jnp.zeros((K, N), F32)], axis=0))
    return [rows_of(shared)], [rows_of(start * inverse)]


def shared_scale(gram):
    return 1.0 / jnp.maximum(diagonal(gram[:, :K]), 1.0)


def ridge_scale(gram):
    rows = lax.broadcasted_iota(jnp.int32, (K, N), 0)
    left = jnp.sum(jnp.where(lanes_of(K) == rows, gram, 0.0), axis=1, keepdims=True)
    right = jnp.sum(jnp.where(lanes_of(K) == rows + K, gram, 0.0), axis=1, keepdims=True)
    return 1.0 / jnp.maximum(RIDGE * jnp.where(lanes_of(K) < K, left, right), 1.0)


def update_kernel(came, w_own, spread, out, stats, grams_next, v_first, wide, later_shared, later_own):
    at_y, at_xl = lax.axis_index("y"), lax.axis_index("xl")
    pairs = range(4)
    stat, base, grams = [], [], []
    for p in pairs:
        a, b = 2 * p, 2 * p + 1
        stat.append(left_left(came[a, :K], came[b, :K]))
        stats[p] = right_right(came[a, :K], came[b, :K])
        base.append(pair_rows(came[a, K : K + K // 2], came[b, K : K + K // 2]))
        first, both = unfold_grams(came[a, K + K // 2 :], came[b, K + K // 2 :])
        grams.append(first)
        grams_next[p] = both
    shared = w_own[...]
    shared = jnp.where(at_xl == 0, left_left(shared, shared), right_right(shared, shared))

    inverses = [ridge_scale(gram) for gram in grams]
    parts = []
    for p in pairs:
        high, low = split((RIDGE * grams[p]) * inverses[p])
        parts.append(jnp.concatenate([high.astype(F32), low.astype(F32)], axis=1))

    def widen(k):
        if k % 8:
            return
        rows = K - k
        left = jnp.concatenate([part[k:] for part in parts], axis=0).astype(BF16)
        columns = jnp.dot(left, spread[:, N * k : N * k + 8 * N], preferred_element_type=F32)
        for i in range(8):
            for p in pairs:
                wide[k + i, K * p + k : K * p + K] = columns[rows * p : rows * p + rows, N * i : N * i + N]

    pulls = [dot_split(grams[p], corners(base[p])) for p in pairs]
    carried = sum(stat[p] - pulls[p] for p in pairs)
    total = both_halves(sum(grams))
    scale = shared_scale(total)
    table = total * scale
    state, residual = shared_start(shared, total, scale, both_halves(carried))
    (shared,) = one_pass(state, residual, lambda i, k, j: column_of(table, k, j), widen)

    later = [grams_next[p] for p in pairs]
    later_total = both_halves(sum(later))
    later_scale = shared_scale(later_total)
    later_table = later_total * later_scale
    own = grams_next[at_y]
    own_scale = ridge_scale(own)
    own_table = (RIDGE * own) * own_scale

    def prepare(k):
        for j in range(k // 8, K // 8):
            later_shared[k, 8 * j : 8 * j + 8] = column_of(later_table, k, j)
            later_own[k, 8 * j : 8 * j + 8] = columns_of(own_table, k, j)

    pushed = dot_split(jnp.concatenate(grams, axis=0), corners(shared))
    state, residual = [], []
    for p in pairs:
        rest = stat[p] - pushed[K * p : K * p + K] - RIDGE * pulls[p]
        state.append(rows_of(base[p]))
        residual.append(rows_of(rest * inverses[p]))
    values = one_pass(state, residual, lambda i, k, j: wide[k, K * i + 8 * j : K * i + 8 * j + 8], prepare)
    for p in pairs:
        v_first[p] = values[p]

    pulled = dot_split(jnp.concatenate(later, axis=1), jnp.concatenate([corners(v) for v in values], axis=0))
    carried = sum(stats[p] for p in pairs) - pulled
    state, residual = shared_start(shared, later_total, later_scale, both_halves(carried))
    (shared,) = one_pass(state, residual, lambda i, k, j: later_shared[k, 8 * j : 8 * j + 8])

    specific = v_first[at_y]
    rest = stats[at_y] - dot_split(own, corners(shared + RIDGE * specific))
    (specific,) = one_pass(
        [rows_of(specific)], [rows_of(rest * own_scale)], lambda i, k, j: later_own[k, 8 * j : 8 * j + 8]
    )
    pieces = (left_left(shared, specific), jnp.where(lanes_of(K) < K, shared, specific))
    for i in range(16):
        out[i] = pieces[i // 8]


def finish_kernel(part, *refs):
    w, v = refs[-2:]
    for i in range(8):
        w[:, N * i : N * i + N] = left_left(part[i], part[8 + i])
        v[0, :, N * i : N * i + N] = right_right(part[i], part[8 + i])


def finish(part, half, name, earlier=()):
    return pl.pallas_call(
        finish_kernel,
        name=name,
        compiler_params=LIMIT,
        grid=(1,),
        out_shape=(shape(K, G), shape(1, K, G)),
        in_specs=[VM] + [FAR] * len(earlier),
        out_specs=[
            pl.BlockSpec((K, HALF), lambda i: (0, half())),
            pl.BlockSpec((1, K, HALF), lambda i: (0, 0, half())),
        ],
        input_output_aliases={1: 0, 2: 1} if earlier else {},
    )(held(part), *earlier)


def shape(*dims):
    return jax.ShapeDtypeStruct(dims, F32)


def near(*dims):
    return pltpu.VMEM(dims, F32)


def held(x):
    return pltpu.with_memory_space_constraint(x, pltpu.VMEM)


VM = pl.BlockSpec(memory_space=pltpu.VMEM)
FAR = pl.BlockSpec(memory_space=pltpu.HBM)
SWAP = [(0, 1), (1, 0)]
LIMIT = pltpu.CompilerParams(vmem_limit_bytes=24 << 20)


def on_device(expression, dataset_id, dataset_map, sweep_count, picks, shared_init, specific_init):
    send, cells, state, w_own, v_own = pl.pallas_call(
        front_kernel,
        name="front",
        out_shape=(
            near(HALF + PACKED, N),
            pltpu.VMEM((2 * HALF, 2 * N), BF16),
            near(N, 2 * N),
            near(K, N),
            near(K, N),
        ),
        in_specs=[FAR] * 6,
        out_specs=[VM] * 5,
        scratch_shapes=[
            pltpu.VMEM(picks.shape, jnp.int32),
            pltpu.SMEM(dataset_id.shape, jnp.int32),
            pltpu.SMEM(sweep_count.shape, jnp.int32),
            pltpu.VMEM(expression.shape, BF16),
            pltpu.VMEM(shared_init.shape, F32),
            pltpu.VMEM(shared_init.shape, F32),
            pltpu.VMEM((expression.shape[1], 2 * N), BF16),
            pltpu.VMEM((K, K, N), F32),
            pltpu.SemaphoreType.DMA((6,)),
        ],
    )(picks, dataset_id, sweep_count, expression, shared_init, specific_init)
    came = lax.ppermute(send, "c", SWAP)
    keep, loads, spreader = pl.pallas_call(
        keep_kernel,
        name="keep",
        compiler_params=LIMIT,
        out_shape=(near(HALF, N), shape(2, K, N), pltpu.VMEM((2 * N, K * N), BF16)),
        in_specs=[VM, VM],
        out_specs=[VM] * 3,
    )(held(cells), held(state))
    packed = pl.pallas_call(
        pack_kernel,
        name="pack",
        compiler_params=LIMIT,
        out_shape=near(8, N + PACKED, N),
        in_specs=[VM] * 3,
        out_specs=VM,
    )(held(keep), held(send), held(came))
    came = lax.all_to_all(packed, RING, 0, 0, tiled=True)
    spread = pl.pallas_call(
        group_kernel, name="group", compiler_params=LIMIT, out_shape=near(8, K + K // 2 + PACKED, N), in_specs=[VM, VM], out_specs=VM
    )(held(came), held(v_own))
    came = lax.all_to_all(spread, GRP, 0, 0, tiled=True)
    spread = pl.pallas_call(
        update_kernel,
        name="update",
        compiler_params=LIMIT,
        out_shape=near(16, K, N),
        in_specs=[VM] * 3,
        out_specs=VM,
        scratch_shapes=[pltpu.VMEM((4, K, N), F32)] * 3
        + [pltpu.VMEM((K, 4 * K, N), F32)]
        + [pltpu.VMEM((K, K, N), F32)] * 2,
    )(held(came), held(w_own), held(spreader))
    mine = lax.all_to_all(spread, PLANE, 0, 0, tiled=True)
    other = lax.ppermute(mine, "c", SWAP)
    bases = finish(mine, lambda: lax.axis_index("c"), "mine")
    shared, specific = finish(other, lambda: 1 - lax.axis_index("c"), "other", bases)
    return loads, shared, specific


def solution(mesh):
    fine = Mesh(mesh.devices.reshape(4, 2, 2, 4, 2), ALL)
    return jax.shard_map(
        on_device,
        mesh=fine,
        in_specs=(P(None, ALL), P(ALL), P(GRP), P(), P(None, ALL), P(), P(GRP, None, None)),
        out_specs=(P(None, None, ALL), P(), P(GRP, None, None)),
        check_vma=False,
    )
```

```python
import jax
import jax.numpy as jnp
from jax import lax
from jax.experimental import pallas as pl
from jax.experimental.pallas import tpu as pltpu
from jax.sharding import Mesh, PartitionSpec as P

K = 64
G = 2000
N = 128
HALF = 8 * N
PACKED = K // 2 + 8
LAST = G - 15 * N
EPSILON = 1e-06
LAMBDA = 5.0
RIDGE = 1.0 + LAMBDA
HIGHEST = lax.Precision.HIGHEST
SLOTS = ("y", "xl")
GRP = ("xl", "y")
RING = ("xh", "z")
PLANE = ("xh", "xl", "z")
ALL = ("y", "xl", "xh", "z", "c")
NT = (((1,), (1,)), ((), ()))
F32 = jnp.float32
BF16 = jnp.bfloat16


def dot_nt(a, b, precision=None):
    return lax.dot_general(a, b, NT, precision=precision, preferred_element_type=F32)


def diagonal(square):
    n = square.shape[0]
    rows = lax.broadcasted_iota(jnp.int32, (n, n), 0)
    cols = lax.broadcasted_iota(jnp.int32, (n, n), 1)
    return jnp.sum(jnp.where(rows == cols, square, 0.0), axis=1, keepdims=True)


def rows_of(x):
    return [x[8 * t : 8 * t + 8] for t in range(K // 8)]


def coordinate_steps(state, residual, column, last):
    sub = lax.broadcasted_iota(jnp.int32, (8, N), 0)
    for k in range(K):
        t, s = divmod(k, 8)
        if s == 0:
            floors = [-h[t] for h in state]
            changes = [None] * len(state)
        for half, r in enumerate(residual):
            change = jnp.maximum(floors[half], r[t])
            spread = jnp.broadcast_to(change[s : s + 1], (8, N))
            changes[half] = change if s == 0 else jnp.where(sub >= s, change, changes[half])
            for j in range((t if s < 7 else t + 1) if last else 0, K // 8):
                r[j] = r[j] - column(half, k, j) * spread
        if s == 7:
            for h, change in zip(state, changes):
                h[t] = h[t] + change
    return [jnp.concatenate(h, axis=0) for h in state]


def lanes_of(rows):
    return lax.broadcasted_iota(jnp.int32, (rows, N), 1)


def swapped(x):
    return pltpu.roll(x, K, 1)


def left_left(a, b):
    return jnp.where(lanes_of(a.shape[0]) < K, a, swapped(b))


def right_right(a, b):
    return jnp.where(lanes_of(a.shape[0]) < K, swapped(a), b)


def split_rows(x):
    return left_left(x[: K // 2], x[K // 2 :]), right_right(x[: K // 2], x[K // 2 :])


def pair_rows(a, b):
    return jnp.concatenate([left_left(a, b), right_right(a, b)], axis=0)


def corners(x):
    left = lanes_of(K) < K
    return jnp.concatenate([jnp.where(left, x, 0.0), jnp.where(left, 0.0, x)], axis=0)


def fold_grams(gram):
    rows = lax.broadcasted_iota(jnp.int32, (K, N), 0)
    other = swapped(gram)
    square = jnp.where(lanes_of(K) <= rows, gram, other)
    packed = left_left(square[: K // 2], square[K // 2 :])
    diag = jnp.sum(jnp.where(lanes_of(K) == rows, other, 0.0), axis=0, keepdims=True)
    return jnp.concatenate([packed, jnp.broadcast_to(diag, (8, N))], axis=0)


def unfold_grams(a, b):
    square = pair_rows(a[: K // 2], b[: K // 2])
    turned = corners(square).T
    turned = turned[:K] + turned[K:]
    diag = left_left(a[K // 2 :], b[K // 2 :])[:1]
    rows = lax.broadcasted_iota(jnp.int32, (K, N), 0)
    cols = lanes_of(K) % K
    first = jnp.where(cols <= rows, square, turned)
    second = jnp.where(cols < rows, turned, jnp.where(cols == rows, diag, square))
    return first, first + second


def split(x):
    high = x.astype(BF16)
    return high, (x - high.astype(F32)).astype(BF16)


def gram_of(high, low):
    both = dot_nt(jnp.concatenate([high, low], axis=0), high)
    return both[:K], both[K:]


def front_kernel(
    picks_hbm, ids_hbm, sweeps_hbm, x_hbm, w_hbm, v_hbm,
    send, cells, state, w_own, v_own,
    picks, ids, sweeps, x, w, v, choose, table, sems,
):
    core = lax.axis_index("c")
    tile = core * 8 + lax.axis_index("xh") * 4 + lax.axis_index("z")
    copies = [
        pltpu.make_async_copy(source, target, sems.at[i])
        for i, (source, target) in enumerate(
            [
                (picks_hbm, picks),
                (w_hbm, w),
                (v_hbm.at[0], v),
                (x_hbm, x),
                (ids_hbm, ids),
                (sweeps_hbm, sweeps),
            ]
        )
    ]
    for copy in copies:
        copy.start()
    copies[0].wait()
    pool = lax.broadcasted_iota(jnp.int32, (x.shape[1], N), 0)
    for r in range(2):
        choose[:, N * r : N * r + N] = (pool == picks[r : r + 1, :]).astype(F32).astype(BF16)
    cells[G:] = jnp.zeros((2 * HALF - G, 2 * N), BF16)
    copies[1].wait()
    copies[2].wait()

    @pl.when(tile < 15)
    def _():
        at = pl.multiple_of(jnp.minimum(tile, 14) * N, N)
        w_own[...] = w[:, pl.ds(at, N)]
        v_own[...] = v[:, pl.ds(at, N)]

    @pl.when(tile == 15)
    def _():
        w_own[...] = jnp.zeros((K, N), F32)
        v_own[...] = jnp.zeros((K, N), F32)
        w_own[:, :LAST] = w[:, 15 * N :]
        v_own[:, :LAST] = v[:, 15 * N :]

    specific = v[...]
    mixed_high, mixed_low = split(w[...] + specific)
    mixed_gram, mixed_cross = gram_of(mixed_high, mixed_low)
    own_gram, own_cross = gram_of(*split(specific))
    cross = mixed_cross + LAMBDA * own_cross
    gram = mixed_gram + LAMBDA * own_gram + cross + cross.T
    inverse = 1.0 / (diagonal(gram) + EPSILON)
    scaled = gram * inverse
    for copy in copies[3:]:
        copy.wait()
    cells[:G] = jnp.dot(x[...], choose[...], preferred_element_type=F32).astype(BF16)
    for k in range(K):
        table[k] = jnp.broadcast_to(scaled[:, k : k + 1], (K, N))
    target = jnp.dot(mixed_high, cells[:G], preferred_element_type=F32) * inverse
    count = sweeps[ids[0]]

    def column(_, k, j):
        return table[k, 8 * j : 8 * j + 8]

    def sweep(_, carry):
        parts = [list(part) for part in carry]
        coordinate_steps(parts[:2], parts[2:], column, False)
        return tuple(tuple(part) for part in parts)

    none = tuple(jnp.zeros((8, N), F32) for _ in range(K // 8))
    carry = (none, none, tuple(rows_of(target[:, :N])), tuple(rows_of(target[:, N:])))
    parts = [list(part) for part in lax.fori_loop(0, count - 1, sweep, carry)]
    first, second = coordinate_steps(parts[:2], parts[2:], column, True)
    zero = jnp.zeros((K, N), F32)
    both = jnp.concatenate([first, second], axis=1)
    block = jnp.concatenate(
        [jnp.concatenate([first, zero], axis=1), jnp.concatenate([zero, second], axis=1)], axis=0
    )
    state[...] = block
    away = pl.multiple_of((1 - core) * HALF, HALF)
    send[:HALF] = dot_nt(cells[pl.ds(away, HALF)], block.astype(BF16))
    send[HALF:] = fold_grams(dot_nt(both, block, HIGHEST))


def keep_kernel(cells, state, keep, loads, spread):
    rows = lax.broadcasted_iota(jnp.int32, (2 * N, N), 0) % N
    at = rows - jnp.where(lanes_of(2 * N) < K, 0, K)
    for k in range(K):
        spread[:, N * k : N * k + N] = (at == k).astype(F32).astype(BF16)
    core = lax.axis_index("c")
    home = pl.multiple_of(core * HALF, HALF)
    block = state[...]
    loads[0] = block[:K, :N]
    loads[1] = block[K:, N:]
    keep[...] = dot_nt(cells[pl.ds(home, HALF)], block.astype(BF16))


def pack_kernel(keep, send, came, out):
    gram = send[HALF:] + came[HALF:]
    for i in range(8):
        out[i, :N] = keep[N * i : N * i + N] + came[N * i : N * i + N]
        out[i, N:] = gram


def group_kernel(came, v_own, out):
    total = came[0]
    for i in range(1, 8):
        total = total + came[i]
    rows = total[:N].T
    first, second = rows[:K], rows[:K] + rows[K:]
    stats = (left_left(first, second), right_right(first, second))
    bases = split_rows(v_own[...])
    for i in range(8):
        out[i, :K] = stats[i // 4]
        out[i, K : K + K // 2] = bases[i // 4]
        out[i, K + K // 2 :] = total[N:]


def dot_split(a, b):
    a_high = a.astype(BF16)
    b_high = b.astype(BF16)
    a_low = (a - a_high.astype(F32)).astype(BF16)
    b_low = (b - b_high.astype(F32)).astype(BF16)
    out = jnp.dot(a_high, b_low, preferred_element_type=F32)
    out = out + jnp.dot(a_low, b_high, preferred_element_type=F32)
    return out + jnp.dot(a_high, b_high, preferred_element_type=F32)


def one_pass(state, residual, weight, beside=None):
    sub = lax.broadcasted_iota(jnp.int32, (8, N), 0)
    for k in range(K):
        t, s = divmod(k, 8)
        if beside is not None:
            beside(k)
        if s == 0:
            floors = [-h[t] for h in state]
            changes = [None] * len(state)
        for i, r in enumerate(residual):
            change = jnp.maximum(floors[i], r[t])
            spread = jnp.broadcast_to(change[s : s + 1], (8, N))
            changes[i] = change if s == 0 else jnp.where(sub >= s, change, changes[i])
            for j in range(t if s < 7 else t + 1, K // 8):
                r[j] = r[j] - weight(i, k, j) * spread
        if s == 7:
            for h, change in zip(state, changes):
                h[t] = h[t] + change
    return [jnp.concatenate(h, axis=0) for h in state]


def column_of(table, k, j):
    return jnp.broadcast_to(table[8 * j : 8 * j + 8, k : k + 1], (8, N))


def columns_of(table, k, j):
    half = jnp.where(lanes_of(8) < K, k, K + k)
    return jnp.take_along_axis(table[8 * j : 8 * j + 8], half, axis=1, mode="promise_in_bounds")


def both_halves(x):
    return x + swapped(x)


def shared_start(shared, gram, inverse, carried):
    start = carried - dot_split(gram, jnp.concatenate([shared, jnp.zeros((K, N), F32)], axis=0))
    return [rows_of(shared)], [rows_of(start * inverse)]


def shared_scale(gram):
    return 1.0 / jnp.maximum(diagonal(gram[:, :K]), 1.0)


def ridge_scale(gram):
    rows = lax.broadcasted_iota(jnp.int32, (K, N), 0)
    left = jnp.sum(jnp.where(lanes_of(K) == rows, gram, 0.0), axis=1, keepdims=True)
    right = jnp.sum(jnp.where(lanes_of(K) == rows + K, gram, 0.0), axis=1, keepdims=True)
    return 1.0 / jnp.maximum(RIDGE * jnp.where(lanes_of(K) < K, left, right), 1.0)


def update_kernel(came, w_own, spread, out, stats, grams_next, v_first, wide, later_shared, later_own):
    at_y, at_xl = lax.axis_index("y"), lax.axis_index("xl")
    pairs = range(4)
    stat, base, grams = [], [], []
    for p in pairs:
        a, b = p, 4 + p
        stat.append(left_left(came[a, :K], came[b, :K]))
        stats[p] = right_right(came[a, :K], came[b, :K])
        base.append(pair_rows(came[a, K : K + K // 2], came[b, K : K + K // 2]))
        first, both = unfold_grams(came[a, K + K // 2 :], came[b, K + K // 2 :])
        grams.append(first)
        grams_next[p] = both
    shared = w_own[...]
    shared = jnp.where(at_xl == 0, left_left(shared, shared), right_right(shared, shared))

    inverses = [ridge_scale(gram) for gram in grams]
    parts = []
    for p in pairs:
        high, low = split((RIDGE * grams[p]) * inverses[p])
        parts.append(jnp.concatenate([high.astype(F32), low.astype(F32)], axis=1))

    def widen(k):
        if k % 8:
            return
        rows = K - k
        left = jnp.concatenate([part[k:] for part in parts], axis=0).astype(BF16)
        columns = jnp.dot(left, spread[:, N * k : N * k + 8 * N], preferred_element_type=F32)
        for i in range(8):
            for p in pairs:
                wide[k + i, K * p + k : K * p + K] = columns[rows * p : rows * p + rows, N * i : N * i + N]

    pulls = [dot_split(grams[p], corners(base[p])) for p in pairs]
    carried = sum(stat[p] - pulls[p] for p in pairs)
    total = both_halves(sum(grams))
    scale = shared_scale(total)
    table = total * scale
    state, residual = shared_start(shared, total, scale, both_halves(carried))
    (shared,) = one_pass(state, residual, lambda i, k, j: column_of(table, k, j), widen)

    later = [grams_next[p] for p in pairs]
    later_total = both_halves(sum(later))
    later_scale = shared_scale(later_total)
    later_table = later_total * later_scale
    own = grams_next[at_y]
    own_scale = ridge_scale(own)
    own_table = (RIDGE * own) * own_scale

    def prepare(k):
        for j in range(k // 8, K // 8):
            later_shared[k, 8 * j : 8 * j + 8] = column_of(later_table, k, j)
            later_own[k, 8 * j : 8 * j + 8] = columns_of(own_table, k, j)

    pushed = dot_split(jnp.concatenate(grams, axis=0), corners(shared))
    state, residual = [], []
    for p in pairs:
        rest = stat[p] - pushed[K * p : K * p + K] - RIDGE * pulls[p]
        state.append(rows_of(base[p]))
        residual.append(rows_of(rest * inverses[p]))
    values = one_pass(state, residual, lambda i, k, j: wide[k, K * i + 8 * j : K * i + 8 * j + 8], prepare)
    for p in pairs:
        v_first[p] = values[p]

    pulled = dot_split(jnp.concatenate(later, axis=1), jnp.concatenate([corners(v) for v in values], axis=0))
    carried = sum(stats[p] for p in pairs) - pulled
    state, residual = shared_start(shared, later_total, later_scale, both_halves(carried))
    (shared,) = one_pass(state, residual, lambda i, k, j: later_shared[k, 8 * j : 8 * j + 8])

    specific = v_first[at_y]
    rest = stats[at_y] - dot_split(own, corners(shared + RIDGE * specific))
    (specific,) = one_pass(
        [rows_of(specific)], [rows_of(rest * own_scale)], lambda i, k, j: later_own[k, 8 * j : 8 * j + 8]
    )
    pieces = (left_left(shared, specific), jnp.where(lanes_of(K) < K, shared, specific))
    for i in range(16):
        out[i] = pieces[i // 4 % 2]


def finish_kernel(part, *refs):
    w, v = refs[-2:]
    for i in range(8):
        left = part[i // 4 * 8 + i % 4]
        right = part[i // 4 * 8 + i % 4 + 4]
        w[:, N * i : N * i + N] = left_left(left, right)
        v[0, :, N * i : N * i + N] = right_right(left, right)


def finish(part, half, name, earlier=()):
    return pl.pallas_call(
        finish_kernel,
        name=name,
        compiler_params=LIMIT,
        grid=(1,),
        out_shape=(shape(K, G), shape(1, K, G)),
        in_specs=[VM] + [FAR] * len(earlier),
        out_specs=[
            pl.BlockSpec((K, HALF), lambda i: (0, half())),
            pl.BlockSpec((1, K, HALF), lambda i: (0, 0, half())),
        ],
        input_output_aliases={1: 0, 2: 1} if earlier else {},
    )(held(part), *earlier)


def shape(*dims):
    return jax.ShapeDtypeStruct(dims, F32)


def near(*dims):
    return pltpu.VMEM(dims, F32)


def held(x):
    return pltpu.with_memory_space_constraint(x, pltpu.VMEM)


VM = pl.BlockSpec(memory_space=pltpu.VMEM)
FAR = pl.BlockSpec(memory_space=pltpu.HBM)
SWAP = [(0, 1), (1, 0)]
LIMIT = pltpu.CompilerParams(vmem_limit_bytes=24 << 20)


def on_device(expression, dataset_id, dataset_map, sweep_count, picks, shared_init, specific_init):
    send, cells, state, w_own, v_own = pl.pallas_call(
        front_kernel,
        name="front",
        out_shape=(
            near(HALF + PACKED, N),
            pltpu.VMEM((2 * HALF, 2 * N), BF16),
            near(N, 2 * N),
            near(K, N),
            near(K, N),
        ),
        in_specs=[FAR] * 6,
        out_specs=[VM] * 5,
        scratch_shapes=[
            pltpu.VMEM(picks.shape, jnp.int32),
            pltpu.SMEM(dataset_id.shape, jnp.int32),
            pltpu.SMEM(sweep_count.shape, jnp.int32),
            pltpu.VMEM(expression.shape, BF16),
            pltpu.VMEM(shared_init.shape, F32),
            pltpu.VMEM(shared_init.shape, F32),
            pltpu.VMEM((expression.shape[1], 2 * N), BF16),
            pltpu.VMEM((K, K, N), F32),
            pltpu.SemaphoreType.DMA((6,)),
        ],
    )(picks, dataset_id, sweep_count, expression, shared_init, specific_init)
    came = lax.ppermute(send, "c", SWAP)
    keep, loads, spreader = pl.pallas_call(
        keep_kernel,
        name="keep",
        compiler_params=LIMIT,
        out_shape=(near(HALF, N), shape(2, K, N), pltpu.VMEM((2 * N, K * N), BF16)),
        in_specs=[VM, VM],
        out_specs=[VM] * 3,
    )(held(cells), held(state))
    packed = pl.pallas_call(
        pack_kernel,
        name="pack",
        compiler_params=LIMIT,
        out_shape=near(8, N + PACKED, N),
        in_specs=[VM] * 3,
        out_specs=VM,
    )(held(keep), held(send), held(came))
    came = lax.all_to_all(packed, RING, 0, 0, tiled=True)
    spread = pl.pallas_call(
        group_kernel, name="group", compiler_params=LIMIT, out_shape=near(8, K + K // 2 + PACKED, N), in_specs=[VM, VM], out_specs=VM
    )(held(came), held(v_own))
    came = lax.all_to_all(spread, GRP, 0, 0, tiled=True)
    spread = pl.pallas_call(
        update_kernel,
        name="update",
        compiler_params=LIMIT,
        out_shape=near(16, K, N),
        in_specs=[VM] * 3,
        out_specs=VM,
        scratch_shapes=[pltpu.VMEM((4, K, N), F32)] * 3
        + [pltpu.VMEM((K, 4 * K, N), F32)]
        + [pltpu.VMEM((K, K, N), F32)] * 2,
    )(held(came), held(w_own), held(spreader))
    mine = lax.all_to_all(spread, PLANE, 0, 0, tiled=True)
    other = lax.ppermute(mine, "c", SWAP)
    bases = finish(mine, lambda: lax.axis_index("c"), "mine")
    shared, specific = finish(other, lambda: 1 - lax.axis_index("c"), "other", bases)
    return loads, shared, specific


def solution(mesh):
    fine = Mesh(mesh.devices.reshape(4, 2, 2, 4, 2), ALL)
    return jax.shard_map(
        on_device,
        mesh=fine,
        in_specs=(P(None, ALL), P(ALL), P(SLOTS), P(), P(None, ALL), P(), P(SLOTS, None, None)),
        out_specs=(P(None, None, ALL), P(), P(SLOTS, None, None)),
        check_vma=False,
    )
```

```python
import jax
import jax.numpy as jnp
from jax import lax
from jax.experimental import pallas as pl
from jax.experimental.pallas import tpu as pltpu
from jax.sharding import Mesh, PartitionSpec as P

K = 64
G = 2000
N = 128
HALF = 8 * N
PACKED = K // 2 + 8
LAST = G - 15 * N
EPSILON = 1e-06
LAMBDA = 5.0
RIDGE = 1.0 + LAMBDA
HIGHEST = lax.Precision.HIGHEST
SLOTS = ("y", "xl")
GRP = ("xl", "y")
RING = ("z", "xh")
PLANE = ("xh", "xl", "z")
ALL = ("y", "xl", "xh", "z", "c")
NT = (((1,), (1,)), ((), ()))
F32 = jnp.float32
BF16 = jnp.bfloat16


def dot_nt(a, b, precision=None):
    return lax.dot_general(a, b, NT, precision=precision, preferred_element_type=F32)


def diagonal(square):
    n = square.shape[0]
    rows = lax.broadcasted_iota(jnp.int32, (n, n), 0)
    cols = lax.broadcasted_iota(jnp.int32, (n, n), 1)
    return jnp.sum(jnp.where(rows == cols, square, 0.0), axis=1, keepdims=True)


def rows_of(x):
    return [x[8 * t : 8 * t + 8] for t in range(K // 8)]


def coordinate_steps(state, residual, column, last):
    sub = lax.broadcasted_iota(jnp.int32, (8, N), 0)
    for k in range(K):
        t, s = divmod(k, 8)
        if s == 0:
            floors = [-h[t] for h in state]
            changes = [None] * len(state)
        for half, r in enumerate(residual):
            change = jnp.maximum(floors[half], r[t])
            spread = jnp.broadcast_to(change[s : s + 1], (8, N))
            changes[half] = change if s == 0 else jnp.where(sub >= s, change, changes[half])
            for j in range((t if s < 7 else t + 1) if last else 0, K // 8):
                r[j] = r[j] - column(half, k, j) * spread
        if s == 7:
            for h, change in zip(state, changes):
                h[t] = h[t] + change
    return [jnp.concatenate(h, axis=0) for h in state]


def lanes_of(rows):
    return lax.broadcasted_iota(jnp.int32, (rows, N), 1)


def swapped(x):
    return pltpu.roll(x, K, 1)


def left_left(a, b):
    return jnp.where(lanes_of(a.shape[0]) < K, a, swapped(b))


def right_right(a, b):
    return jnp.where(lanes_of(a.shape[0]) < K, swapped(a), b)


def split_rows(x):
    return left_left(x[: K // 2], x[K // 2 :]), right_right(x[: K // 2], x[K // 2 :])


def pair_rows(a, b):
    return jnp.concatenate([left_left(a, b), right_right(a, b)], axis=0)


def corners(x):
    left = lanes_of(K) < K
    return jnp.concatenate([jnp.where(left, x, 0.0), jnp.where(left, 0.0, x)], axis=0)


def fold_grams(gram):
    rows = lax.broadcasted_iota(jnp.int32, (K, N), 0)
    other = swapped(gram)
    square = jnp.where(lanes_of(K) <= rows, gram, other)
    packed = left_left(square[: K // 2], square[K // 2 :])
    diag = jnp.sum(jnp.where(lanes_of(K) == rows, other, 0.0), axis=0, keepdims=True)
    return jnp.concatenate([packed, jnp.broadcast_to(diag, (8, N))], axis=0)


def unfold_grams(a, b):
    square = pair_rows(a[: K // 2], b[: K // 2])
    turned = corners(square).T
    turned = turned[:K] + turned[K:]
    diag = left_left(a[K // 2 :], b[K // 2 :])[:1]
    rows = lax.broadcasted_iota(jnp.int32, (K, N), 0)
    cols = lanes_of(K) % K
    first = jnp.where(cols <= rows, square, turned)
    second = jnp.where(cols < rows, turned, jnp.where(cols == rows, diag, square))
    return first, first + second


def split(x):
    high = x.astype(BF16)
    return high, (x - high.astype(F32)).astype(BF16)


def gram_of(high, low):
    both = dot_nt(jnp.concatenate([high, low], axis=0), high)
    return both[:K], both[K:]


def front_kernel(
    picks_hbm, ids_hbm, sweeps_hbm, x_hbm, w_hbm, v_hbm,
    send, cells, state, w_own, v_own,
    picks, ids, sweeps, x, w, v, choose, table, sems,
):
    core = lax.axis_index("c")
    tile = core * 8 + lax.axis_index("z") * 2 + lax.axis_index("xh")
    copies = [
        pltpu.make_async_copy(source, target, sems.at[i])
        for i, (source, target) in enumerate(
            [
                (picks_hbm, picks),
                (w_hbm, w),
                (v_hbm.at[0], v),
                (x_hbm, x),
                (ids_hbm, ids),
                (sweeps_hbm, sweeps),
            ]
        )
    ]
    for copy in copies:
        copy.start()
    copies[0].wait()
    pool = lax.broadcasted_iota(jnp.int32, (x.shape[1], N), 0)
    for r in range(2):
        choose[:, N * r : N * r + N] = (pool == picks[r : r + 1, :]).astype(F32).astype(BF16)
    cells[G:] = jnp.zeros((2 * HALF - G, 2 * N), BF16)
    copies[1].wait()
    copies[2].wait()

    @pl.when(tile < 15)
    def _():
        at = pl.multiple_of(jnp.minimum(tile, 14) * N, N)
        w_own[...] = w[:, pl.ds(at, N)]
        v_own[...] = v[:, pl.ds(at, N)]

    @pl.when(tile == 15)
    def _():
        w_own[...] = jnp.zeros((K, N), F32)
        v_own[...] = jnp.zeros((K, N), F32)
        w_own[:, :LAST] = w[:, 15 * N :]
        v_own[:, :LAST] = v[:, 15 * N :]

    specific = v[...]
    mixed_high, mixed_low = split(w[...] + specific)
    mixed_gram, mixed_cross = gram_of(mixed_high, mixed_low)
    own_gram, own_cross = gram_of(*split(specific))
    cross = mixed_cross + LAMBDA * own_cross
    gram = mixed_gram + LAMBDA * own_gram + cross + cross.T
    inverse = 1.0 / (diagonal(gram) + EPSILON)
    scaled = gram * inverse
    for copy in copies[3:]:
        copy.wait()
    cells[:G] = jnp.dot(x[...], choose[...], preferred_element_type=F32).astype(BF16)
    for k in range(K):
        table[k] = jnp.broadcast_to(scaled[:, k : k + 1], (K, N))
    target = jnp.dot(mixed_high, cells[:G], preferred_element_type=F32) * inverse
    count = sweeps[ids[0]]

    def column(_, k, j):
        return table[k, 8 * j : 8 * j + 8]

    def sweep(_, carry):
        parts = [list(part) for part in carry]
        coordinate_steps(parts[:2], parts[2:], column, False)
        return tuple(tuple(part) for part in parts)

    none = tuple(jnp.zeros((8, N), F32) for _ in range(K // 8))
    carry = (none, none, tuple(rows_of(target[:, :N])), tuple(rows_of(target[:, N:])))
    parts = [list(part) for part in lax.fori_loop(0, count - 1, sweep, carry)]
    first, second = coordinate_steps(parts[:2], parts[2:], column, True)
    zero = jnp.zeros((K, N), F32)
    both = jnp.concatenate([first, second], axis=1)
    block = jnp.concatenate(
        [jnp.concatenate([first, zero], axis=1), jnp.concatenate([zero, second], axis=1)], axis=0
    )
    state[...] = block
    away = pl.multiple_of((1 - core) * HALF, HALF)
    send[:HALF] = dot_nt(cells[pl.ds(away, HALF)], block.astype(BF16))
    send[HALF:] = fold_grams(dot_nt(both, block, HIGHEST))


def keep_kernel(cells, state, keep, loads, spread):
    rows = lax.broadcasted_iota(jnp.int32, (2 * N, N), 0) % N
    at = rows - jnp.where(lanes_of(2 * N) < K, 0, K)
    for k in range(K):
        spread[:, N * k : N * k + N] = (at == k).astype(F32).astype(BF16)
    core = lax.axis_index("c")
    home = pl.multiple_of(core * HALF, HALF)
    block = state[...]
    loads[0] = block[:K, :N]
    loads[1] = block[K:, N:]
    keep[...] = dot_nt(cells[pl.ds(home, HALF)], block.astype(BF16))


def pack_kernel(keep, send, came, out):
    gram = send[HALF:] + came[HALF:]
    for i in range(8):
        out[i, :N] = keep[N * i : N * i + N] + came[N * i : N * i + N]
        out[i, N:] = gram


def group_kernel(came, v_own, out):
    total = came[0]
    for i in range(1, 8):
        total = total + came[i]
    rows = total[:N].T
    first, second = rows[:K], rows[:K] + rows[K:]
    stats = (left_left(first, second), right_right(first, second))
    bases = split_rows(v_own[...])
    for i in range(8):
        out[i, :K] = stats[i // 4]
        out[i, K : K + K // 2] = bases[i // 4]
        out[i, K + K // 2 :] = total[N:]


def dot_split(a, b):
    a_high = a.astype(BF16)
    b_high = b.astype(BF16)
    a_low = (a - a_high.astype(F32)).astype(BF16)
    b_low = (b - b_high.astype(F32)).astype(BF16)
    out = jnp.dot(a_high, b_low, preferred_element_type=F32)
    out = out + jnp.dot(a_low, b_high, preferred_element_type=F32)
    return out + jnp.dot(a_high, b_high, preferred_element_type=F32)


def one_pass(state, residual, weight, beside=None):
    sub = lax.broadcasted_iota(jnp.int32, (8, N), 0)
    for k in range(K):
        t, s = divmod(k, 8)
        if beside is not None:
            beside(k)
        if s == 0:
            floors = [-h[t] for h in state]
            changes = [None] * len(state)
        for i, r in enumerate(residual):
            change = jnp.maximum(floors[i], r[t])
            spread = jnp.broadcast_to(change[s : s + 1], (8, N))
            changes[i] = change if s == 0 else jnp.where(sub >= s, change, changes[i])
            for j in range(t if s < 7 else t + 1, K // 8):
                r[j] = r[j] - weight(i, k, j) * spread
        if s == 7:
            for h, change in zip(state, changes):
                h[t] = h[t] + change
    return [jnp.concatenate(h, axis=0) for h in state]


def column_of(table, k, j):
    return jnp.broadcast_to(table[8 * j : 8 * j + 8, k : k + 1], (8, N))


def columns_of(table, k, j):
    half = jnp.where(lanes_of(8) < K, k, K + k)
    return jnp.take_along_axis(table[8 * j : 8 * j + 8], half, axis=1, mode="promise_in_bounds")


def both_halves(x):
    return x + swapped(x)


def shared_start(shared, gram, inverse, carried):
    start = carried - dot_split(gram, jnp.concatenate([shared, jnp.zeros((K, N), F32)], axis=0))
    return [rows_of(shared)], [rows_of(start * inverse)]


def shared_scale(gram):
    return 1.0 / jnp.maximum(diagonal(gram[:, :K]), 1.0)


def ridge_scale(gram):
    rows = lax.broadcasted_iota(jnp.int32, (K, N), 0)
    left = jnp.sum(jnp.where(lanes_of(K) == rows, gram, 0.0), axis=1, keepdims=True)
    right = jnp.sum(jnp.where(lanes_of(K) == rows + K, gram, 0.0), axis=1, keepdims=True)
    return 1.0 / jnp.maximum(RIDGE * jnp.where(lanes_of(K) < K, left, right), 1.0)


def update_kernel(came, w_own, spread, out, stats, grams_next, v_first, wide, later_shared, later_own):
    at_y, at_xl = lax.axis_index("y"), lax.axis_index("xl")
    pairs = range(4)
    stat, base, grams = [], [], []
    for p in pairs:
        a, b = p, 4 + p
        stat.append(left_left(came[a, :K], came[b, :K]))
        stats[p] = right_right(came[a, :K], came[b, :K])
        base.append(pair_rows(came[a, K : K + K // 2], came[b, K : K + K // 2]))
        first, both = unfold_grams(came[a, K + K // 2 :], came[b, K + K // 2 :])
        grams.append(first)
        grams_next[p] = both
    shared = w_own[...]
    shared = jnp.where(at_xl == 0, left_left(shared, shared), right_right(shared, shared))

    inverses = [ridge_scale(gram) for gram in grams]
    parts = []
    for p in pairs:
        high, low = split((RIDGE * grams[p]) * inverses[p])
        parts.append(jnp.concatenate([high.astype(F32), low.astype(F32)], axis=1))

    def widen(k):
        if k % 8:
            return
        rows = K - k
        left = jnp.concatenate([part[k:] for part in parts], axis=0).astype(BF16)
        columns = jnp.dot(left, spread[:, N * k : N * k + 8 * N], preferred_element_type=F32)
        for i in range(8):
            for p in pairs:
                wide[k + i, K * p + k : K * p + K] = columns[rows * p : rows * p + rows, N * i : N * i + N]

    pulls = [dot_split(grams[p], corners(base[p])) for p in pairs]
    carried = sum(stat[p] - pulls[p] for p in pairs)
    total = both_halves(sum(grams))
    scale = shared_scale(total)
    table = total * scale
    state, residual = shared_start(shared, total, scale, both_halves(carried))
    (shared,) = one_pass(state, residual, lambda i, k, j: column_of(table, k, j), widen)

    later = [grams_next[p] for p in pairs]
    later_total = both_halves(sum(later))
    later_scale = shared_scale(later_total)
    later_table = later_total * later_scale
    own = grams_next[at_y]
    own_scale = ridge_scale(own)
    own_table = (RIDGE * own) * own_scale

    def prepare(k):
        for j in range(k // 8, K // 8):
            later_shared[k, 8 * j : 8 * j + 8] = column_of(later_table, k, j)
            later_own[k, 8 * j : 8 * j + 8] = columns_of(own_table, k, j)

    pushed = dot_split(jnp.concatenate(grams, axis=0), corners(shared))
    state, residual = [], []
    for p in pairs:
        rest = stat[p] - pushed[K * p : K * p + K] - RIDGE * pulls[p]
        state.append(rows_of(base[p]))
        residual.append(rows_of(rest * inverses[p]))
    values = one_pass(state, residual, lambda i, k, j: wide[k, K * i + 8 * j : K * i + 8 * j + 8], prepare)
    for p in pairs:
        v_first[p] = values[p]

    pulled = dot_split(jnp.concatenate(later, axis=1), jnp.concatenate([corners(v) for v in values], axis=0))
    carried = sum(stats[p] for p in pairs) - pulled
    state, residual = shared_start(shared, later_total, later_scale, both_halves(carried))
    (shared,) = one_pass(state, residual, lambda i, k, j: later_shared[k, 8 * j : 8 * j + 8])

    specific = v_first[at_y]
    rest = stats[at_y] - dot_split(own, corners(shared + RIDGE * specific))
    (specific,) = one_pass(
        [rows_of(specific)], [rows_of(rest * own_scale)], lambda i, k, j: later_own[k, 8 * j : 8 * j + 8]
    )
    pieces = (left_left(shared, specific), jnp.where(lanes_of(K) < K, shared, specific))
    for i in range(16):
        out[i] = pieces[i // 4 % 2]


def finish_kernel(part, *refs):
    w, v = refs[-2:]
    for i in range(8):
        left = part[i % 2 * 8 + i // 2]
        right = part[i % 2 * 8 + i // 2 + 4]
        w[:, N * i : N * i + N] = left_left(left, right)
        v[0, :, N * i : N * i + N] = right_right(left, right)


def finish(part, half, name, earlier=()):
    return pl.pallas_call(
        finish_kernel,
        name=name,
        compiler_params=LIMIT,
        grid=(1,),
        out_shape=(shape(K, G), shape(1, K, G)),
        in_specs=[VM] + [FAR] * len(earlier),
        out_specs=[
            pl.BlockSpec((K, HALF), lambda i: (0, half())),
            pl.BlockSpec((1, K, HALF), lambda i: (0, 0, half())),
        ],
        input_output_aliases={1: 0, 2: 1} if earlier else {},
    )(held(part), *earlier)


def shape(*dims):
    return jax.ShapeDtypeStruct(dims, F32)


def near(*dims):
    return pltpu.VMEM(dims, F32)


def held(x):
    return pltpu.with_memory_space_constraint(x, pltpu.VMEM)


VM = pl.BlockSpec(memory_space=pltpu.VMEM)
FAR = pl.BlockSpec(memory_space=pltpu.HBM)
SWAP = [(0, 1), (1, 0)]
LIMIT = pltpu.CompilerParams(vmem_limit_bytes=24 << 20)


def on_device(expression, dataset_id, dataset_map, sweep_count, picks, shared_init, specific_init):
    send, cells, state, w_own, v_own = pl.pallas_call(
        front_kernel,
        name="front",
        out_shape=(
            near(HALF + PACKED, N),
            pltpu.VMEM((2 * HALF, 2 * N), BF16),
            near(N, 2 * N),
            near(K, N),
            near(K, N),
        ),
        in_specs=[FAR] * 6,
        out_specs=[VM] * 5,
        scratch_shapes=[
            pltpu.VMEM(picks.shape, jnp.int32),
            pltpu.SMEM(dataset_id.shape, jnp.int32),
            pltpu.SMEM(sweep_count.shape, jnp.int32),
            pltpu.VMEM(expression.shape, BF16),
            pltpu.VMEM(shared_init.shape, F32),
            pltpu.VMEM(shared_init.shape, F32),
            pltpu.VMEM((expression.shape[1], 2 * N), BF16),
            pltpu.VMEM((K, K, N), F32),
            pltpu.SemaphoreType.DMA((6,)),
        ],
    )(picks, dataset_id, sweep_count, expression, shared_init, specific_init)
    came = lax.ppermute(send, "c", SWAP)
    keep, loads, spreader = pl.pallas_call(
        keep_kernel,
        name="keep",
        compiler_params=LIMIT,
        out_shape=(near(HALF, N), shape(2, K, N), pltpu.VMEM((2 * N, K * N), BF16)),
        in_specs=[VM, VM],
        out_specs=[VM] * 3,
    )(held(cells), held(state))
    packed = pl.pallas_call(
        pack_kernel,
        name="pack",
        compiler_params=LIMIT,
        out_shape=near(8, N + PACKED, N),
        in_specs=[VM] * 3,
        out_specs=VM,
    )(held(keep), held(send), held(came))
    came = lax.all_to_all(packed, RING, 0, 0, tiled=True)
    spread = pl.pallas_call(
        group_kernel, name="group", compiler_params=LIMIT, out_shape=near(8, K + K // 2 + PACKED, N), in_specs=[VM, VM], out_specs=VM
    )(held(came), held(v_own))
    came = lax.all_to_all(spread, GRP, 0, 0, tiled=True)
    spread = pl.pallas_call(
        update_kernel,
        name="update",
        compiler_params=LIMIT,
        out_shape=near(16, K, N),
        in_specs=[VM] * 3,
        out_specs=VM,
        scratch_shapes=[pltpu.VMEM((4, K, N), F32)] * 3
        + [pltpu.VMEM((K, 4 * K, N), F32)]
        + [pltpu.VMEM((K, K, N), F32)] * 2,
    )(held(came), held(w_own), held(spreader))
    mine = lax.all_to_all(spread, PLANE, 0, 0, tiled=True)
    other = lax.ppermute(mine, "c", SWAP)
    bases = finish(mine, lambda: lax.axis_index("c"), "mine")
    shared, specific = finish(other, lambda: 1 - lax.axis_index("c"), "other", bases)
    return loads, shared, specific


def solution(mesh):
    fine = Mesh(mesh.devices.reshape(4, 2, 2, 4, 2), ALL)
    return jax.shard_map(
        on_device,
        mesh=fine,
        in_specs=(P(None, ALL), P(ALL), P(SLOTS), P(), P(None, ALL), P(), P(SLOTS, None, None)),
        out_specs=(P(None, None, ALL), P(), P(SLOTS, None, None)),
        check_vma=False,
    )
```

```python
import jax
import jax.numpy as jnp
from jax import lax
from jax.experimental import pallas as pl
from jax.experimental.pallas import tpu as pltpu
from jax.sharding import Mesh, PartitionSpec as P

K = 64
G = 2000
N = 128
HALF = 8 * N
PACKED = K // 2 + 8
LAST = G - 15 * N
EPSILON = 1e-06
LAMBDA = 5.0
RIDGE = 1.0 + LAMBDA
HIGHEST = lax.Precision.HIGHEST
SLOTS = ("y", "xl")
GRP = ("xl", "y")
RING = ("z", "xh")
PLANE = ("xh", "xl", "z")
ALL = ("y", "xl", "xh", "z", "c")
NT = (((1,), (1,)), ((), ()))
F32 = jnp.float32
BF16 = jnp.bfloat16


def dot_nt(a, b, precision=None):
    return lax.dot_general(a, b, NT, precision=precision, preferred_element_type=F32)


def diagonal(square):
    n = square.shape[0]
    rows = lax.broadcasted_iota(jnp.int32, (n, n), 0)
    cols = lax.broadcasted_iota(jnp.int32, (n, n), 1)
    return jnp.sum(jnp.where(rows == cols, square, 0.0), axis=1, keepdims=True)


def rows_of(x):
    return [x[8 * t : 8 * t + 8] for t in range(K // 8)]


def coordinate_steps(state, residual, column, last):
    sub = lax.broadcasted_iota(jnp.int32, (8, N), 0)
    for k in range(K):
        t, s = divmod(k, 8)
        if s == 0:
            floors = [-h[t] for h in state]
            changes = [None] * len(state)
        for half, r in enumerate(residual):
            change = jnp.maximum(floors[half], r[t])
            spread = jnp.broadcast_to(change[s : s + 1], (8, N))
            changes[half] = change if s == 0 else jnp.where(sub >= s, change, changes[half])
            for j in range((t if s < 7 else t + 1) if last else 0, K // 8):
                r[j] = r[j] - column(half, k, j) * spread
        if s == 7:
            for h, change in zip(state, changes):
                h[t] = h[t] + change
    return [jnp.concatenate(h, axis=0) for h in state]


def lanes_of(rows):
    return lax.broadcasted_iota(jnp.int32, (rows, N), 1)


def swapped(x):
    return pltpu.roll(x, K, 1)


def left_left(a, b):
    return jnp.where(lanes_of(a.shape[0]) < K, a, swapped(b))


def right_right(a, b):
    return jnp.where(lanes_of(a.shape[0]) < K, swapped(a), b)


def split_rows(x):
    return left_left(x[: K // 2], x[K // 2 :]), right_right(x[: K // 2], x[K // 2 :])


def pair_rows(a, b):
    return jnp.concatenate([left_left(a, b), right_right(a, b)], axis=0)


def corners(x):
    left = lanes_of(K) < K
    return jnp.concatenate([jnp.where(left, x, 0.0), jnp.where(left, 0.0, x)], axis=0)


def fold_grams(gram):
    rows = lax.broadcasted_iota(jnp.int32, (K, N), 0)
    other = swapped(gram)
    square = jnp.where(lanes_of(K) <= rows, gram, other)
    packed = left_left(square[: K // 2], square[K // 2 :])
    diag = jnp.sum(jnp.where(lanes_of(K) == rows, other, 0.0), axis=0, keepdims=True)
    return jnp.concatenate([packed, jnp.broadcast_to(diag, (8, N))], axis=0)


def unfold_grams(a, b):
    square = pair_rows(a[: K // 2], b[: K // 2])
    turned = corners(square).T
    turned = turned[:K] + turned[K:]
    diag = left_left(a[K // 2 :], b[K // 2 :])[:1]
    rows = lax.broadcasted_iota(jnp.int32, (K, N), 0)
    cols = lanes_of(K) % K
    first = jnp.where(cols <= rows, square, turned)
    second = jnp.where(cols < rows, turned, jnp.where(cols == rows, diag, square))
    return first, first + second


def split(x):
    high = x.astype(BF16)
    return high, (x - high.astype(F32)).astype(BF16)


def gram_of(high, low):
    both = dot_nt(jnp.concatenate([high, low], axis=0), high)
    return both[:K], both[K:]


def front_kernel(
    picks_hbm, ids_hbm, sweeps_hbm, x_hbm, w_hbm, v_hbm,
    send, cells, state, w_own, v_own,
    picks, ids, sweeps, x, w, v, choose, table, sems,
):
    core = lax.axis_index("c")
    tile = core * 8 + lax.axis_index("z") * 2 + lax.axis_index("xh")
    copies = [
        pltpu.make_async_copy(source, target, sems.at[i])
        for i, (source, target) in enumerate(
            [
                (picks_hbm, picks),
                (w_hbm, w),
                (v_hbm.at[0], v),
                (x_hbm, x),
                (ids_hbm, ids),
                (sweeps_hbm, sweeps),
            ]
        )
    ]
    for copy in copies:
        copy.start()
    copies[0].wait()
    pool = lax.broadcasted_iota(jnp.int32, (x.shape[1], N), 0)
    for r in range(2):
        choose[:, N * r : N * r + N] = (pool == picks[r : r + 1, :]).astype(F32).astype(BF16)
    cells[G:] = jnp.zeros((2 * HALF - G, 2 * N), BF16)
    copies[1].wait()
    copies[2].wait()

    @pl.when(tile < 15)
    def _():
        at = pl.multiple_of(jnp.minimum(tile, 14) * N, N)
        w_own[...] = w[:, pl.ds(at, N)]
        v_own[...] = v[:, pl.ds(at, N)]

    @pl.when(tile == 15)
    def _():
        w_own[...] = jnp.zeros((K, N), F32)
        v_own[...] = jnp.zeros((K, N), F32)
        w_own[:, :LAST] = w[:, 15 * N :]
        v_own[:, :LAST] = v[:, 15 * N :]

    specific = v[...]
    mixed_high, mixed_low = split(w[...] + specific)
    mixed_gram, mixed_cross = gram_of(mixed_high, mixed_low)
    own_gram, own_cross = gram_of(*split(specific))
    cross = mixed_cross + LAMBDA * own_cross
    gram = mixed_gram + LAMBDA * own_gram + cross + cross.T
    inverse = 1.0 / (diagonal(gram) + EPSILON)
    scaled = gram * inverse
    for copy in copies[3:]:
        copy.wait()
    cells[:G] = jnp.dot(x[...], choose[...], preferred_element_type=F32).astype(BF16)
    for k in range(K):
        table[k] = jnp.broadcast_to(scaled[:, k : k + 1], (K, N))
    target = jnp.dot(mixed_high, cells[:G], preferred_element_type=F32) * inverse
    count = sweeps[ids[0]]

    def column(_, k, j):
        return table[k, 8 * j : 8 * j + 8]

    def sweep(_, carry):
        parts = [list(part) for part in carry]
        coordinate_steps(parts[:2], parts[2:], column, False)
        return tuple(tuple(part) for part in parts)

    none = tuple(jnp.zeros((8, N), F32) for _ in range(K // 8))
    carry = (none, none, tuple(rows_of(target[:, :N])), tuple(rows_of(target[:, N:])))
    parts = [list(part) for part in lax.fori_loop(0, count - 1, sweep, carry)]
    first, second = coordinate_steps(parts[:2], parts[2:], column, True)
    zero = jnp.zeros((K, N), F32)
    both = jnp.concatenate([first, second], axis=1)
    block = jnp.concatenate(
        [jnp.concatenate([first, zero], axis=1), jnp.concatenate([zero, second], axis=1)], axis=0
    )
    state[...] = block
    away = pl.multiple_of((1 - core) * HALF, HALF)
    high, low = split(both)
    rounded = block.astype(BF16)
    gram = dot_nt(jnp.concatenate([high, low], axis=0), rounded)
    gram = gram[:K] + gram[K:] + dot_nt(high, split(block)[1])
    send[HALF:] = fold_grams(gram)
    send[:HALF] = dot_nt(cells[pl.ds(away, HALF)], rounded)


def keep_kernel(cells, state, keep, loads, spread):
    rows = lax.broadcasted_iota(jnp.int32, (2 * N, N), 0) % N
    at = rows - jnp.where(lanes_of(2 * N) < K, 0, K)
    for k in range(K):
        spread[:, N * k : N * k + N] = (at == k).astype(F32).astype(BF16)
    core = lax.axis_index("c")
    home = pl.multiple_of(core * HALF, HALF)
    block = state[...]
    loads[0] = block[:K, :N]
    loads[1] = block[K:, N:]
    keep[...] = dot_nt(cells[pl.ds(home, HALF)], block.astype(BF16))


def pack_kernel(keep, send, came, out):
    gram = send[HALF:] + came[HALF:]
    for i in range(8):
        out[i, :N] = keep[N * i : N * i + N] + came[N * i : N * i + N]
        out[i, N:] = gram


def group_kernel(came, v_own, out):
    total = came[0]
    for i in range(1, 8):
        total = total + came[i]
    rows = total[:N].T
    first, second = rows[:K], rows[:K] + rows[K:]
    stats = (left_left(first, second), right_right(first, second))
    bases = split_rows(v_own[...])
    for i in range(8):
        out[i, :K] = stats[i // 4]
        out[i, K : K + K // 2] = bases[i // 4]
        out[i, K + K // 2 :] = total[N:]


def dot_split(a, b):
    a_high = a.astype(BF16)
    b_high = b.astype(BF16)
    a_low = (a - a_high.astype(F32)).astype(BF16)
    b_low = (b - b_high.astype(F32)).astype(BF16)
    out = jnp.dot(a_high, b_low, preferred_element_type=F32)
    out = out + jnp.dot(a_low, b_high, preferred_element_type=F32)
    return out + jnp.dot(a_high, b_high, preferred_element_type=F32)


def one_pass(state, residual, weight, beside=None):
    sub = lax.broadcasted_iota(jnp.int32, (8, N), 0)
    for k in range(K):
        t, s = divmod(k, 8)
        if beside is not None:
            beside(k)
        if s == 0:
            floors = [-h[t] for h in state]
            changes = [None] * len(state)
        for i, r in enumerate(residual):
            change = jnp.maximum(floors[i], r[t])
            spread = jnp.broadcast_to(change[s : s + 1], (8, N))
            changes[i] = change if s == 0 else jnp.where(sub >= s, change, changes[i])
            for j in range(t if s < 7 else t + 1, K // 8):
                r[j] = r[j] - weight(i, k, j) * spread
        if s == 7:
            for h, change in zip(state, changes):
                h[t] = h[t] + change
    return [jnp.concatenate(h, axis=0) for h in state]


def column_of(table, k, j):
    return jnp.broadcast_to(table[8 * j : 8 * j + 8, k : k + 1], (8, N))


def columns_of(table, k, j):
    half = jnp.where(lanes_of(8) < K, k, K + k)
    return jnp.take_along_axis(table[8 * j : 8 * j + 8], half, axis=1, mode="promise_in_bounds")


def both_halves(x):
    return x + swapped(x)


def shared_start(shared, gram, inverse, carried):
    start = carried - dot_split(gram, jnp.concatenate([shared, jnp.zeros((K, N), F32)], axis=0))
    return [rows_of(shared)], [rows_of(start * inverse)]


def shared_scale(gram):
    return 1.0 / jnp.maximum(diagonal(gram[:, :K]), 1.0)


def ridge_scale(gram):
    rows = lax.broadcasted_iota(jnp.int32, (K, N), 0)
    left = jnp.sum(jnp.where(lanes_of(K) == rows, gram, 0.0), axis=1, keepdims=True)
    right = jnp.sum(jnp.where(lanes_of(K) == rows + K, gram, 0.0), axis=1, keepdims=True)
    return 1.0 / jnp.maximum(RIDGE * jnp.where(lanes_of(K) < K, left, right), 1.0)


def update_kernel(came, w_own, spread, out, stats, grams_next, v_first, wide, later_shared, later_own):
    at_y, at_xl = lax.axis_index("y"), lax.axis_index("xl")
    pairs = range(4)
    stat, base, grams = [], [], []
    for p in pairs:
        a, b = p, 4 + p
        stat.append(left_left(came[a, :K], came[b, :K]))
        stats[p] = right_right(came[a, :K], came[b, :K])
        base.append(pair_rows(came[a, K : K + K // 2], came[b, K : K + K // 2]))
        first, both = unfold_grams(came[a, K + K // 2 :], came[b, K + K // 2 :])
        grams.append(first)
        grams_next[p] = both
    shared = w_own[...]
    shared = jnp.where(at_xl == 0, left_left(shared, shared), right_right(shared, shared))

    inverses = [ridge_scale(gram) for gram in grams]
    parts = []
    for p in pairs:
        high, low = split((RIDGE * grams[p]) * inverses[p])
        parts.append(jnp.concatenate([high.astype(F32), low.astype(F32)], axis=1))

    def widen(k):
        if k % 8:
            return
        rows = K - k
        left = jnp.concatenate([part[k:] for part in parts], axis=0).astype(BF16)
        columns = jnp.dot(left, spread[:, N * k : N * k + 8 * N], preferred_element_type=F32)
        for i in range(8):
            for p in pairs:
                wide[k + i, K * p + k : K * p + K] = columns[rows * p : rows * p + rows, N * i : N * i + N]

    pulls = [dot_split(grams[p], corners(base[p])) for p in pairs]
    carried = sum(stat[p] - pulls[p] for p in pairs)
    total = both_halves(sum(grams))
    scale = shared_scale(total)
    table = total * scale
    state, residual = shared_start(shared, total, scale, both_halves(carried))
    (shared,) = one_pass(state, residual, lambda i, k, j: column_of(table, k, j), widen)

    later = [grams_next[p] for p in pairs]
    later_total = both_halves(sum(later))
    later_scale = shared_scale(later_total)
    later_table = later_total * later_scale
    own = grams_next[at_y]
    own_scale = ridge_scale(own)
    own_table = (RIDGE * own) * own_scale

    def prepare(k):
        for j in range(k // 8, K // 8):
            later_shared[k, 8 * j : 8 * j + 8] = column_of(later_table, k, j)
            later_own[k, 8 * j : 8 * j + 8] = columns_of(own_table, k, j)

    pushed = dot_split(jnp.concatenate(grams, axis=0), corners(shared))
    state, residual = [], []
    for p in pairs:
        rest = stat[p] - pushed[K * p : K * p + K] - RIDGE * pulls[p]
        state.append(rows_of(base[p]))
        residual.append(rows_of(rest * inverses[p]))
    values = one_pass(state, residual, lambda i, k, j: wide[k, K * i + 8 * j : K * i + 8 * j + 8], prepare)
    for p in pairs:
        v_first[p] = values[p]

    pulled = dot_split(jnp.concatenate(later, axis=1), jnp.concatenate([corners(v) for v in values], axis=0))
    carried = sum(stats[p] for p in pairs) - pulled
    state, residual = shared_start(shared, later_total, later_scale, both_halves(carried))
    (shared,) = one_pass(state, residual, lambda i, k, j: later_shared[k, 8 * j : 8 * j + 8])

    specific = v_first[at_y]
    rest = stats[at_y] - dot_split(own, corners(shared + RIDGE * specific))
    (specific,) = one_pass(
        [rows_of(specific)], [rows_of(rest * own_scale)], lambda i, k, j: later_own[k, 8 * j : 8 * j + 8]
    )
    pieces = (left_left(shared, specific), jnp.where(lanes_of(K) < K, shared, specific))
    for i in range(16):
        out[i] = pieces[i // 4 % 2]


def finish_kernel(part, *refs):
    w, v = refs[-2:]
    for i in range(8):
        left = part[i % 2 * 8 + i // 2]
        right = part[i % 2 * 8 + i // 2 + 4]
        w[:, N * i : N * i + N] = left_left(left, right)
        v[0, :, N * i : N * i + N] = right_right(left, right)


def finish(part, half, name, earlier=()):
    return pl.pallas_call(
        finish_kernel,
        name=name,
        compiler_params=LIMIT,
        grid=(1,),
        out_shape=(shape(K, G), shape(1, K, G)),
        in_specs=[VM] + [FAR] * len(earlier),
        out_specs=[
            pl.BlockSpec((K, HALF), lambda i: (0, half())),
            pl.BlockSpec((1, K, HALF), lambda i: (0, 0, half())),
        ],
        input_output_aliases={1: 0, 2: 1} if earlier else {},
    )(held(part), *earlier)


def shape(*dims):
    return jax.ShapeDtypeStruct(dims, F32)


def near(*dims):
    return pltpu.VMEM(dims, F32)


def held(x):
    return pltpu.with_memory_space_constraint(x, pltpu.VMEM)


VM = pl.BlockSpec(memory_space=pltpu.VMEM)
FAR = pl.BlockSpec(memory_space=pltpu.HBM)
SWAP = [(0, 1), (1, 0)]
LIMIT = pltpu.CompilerParams(vmem_limit_bytes=24 << 20)


def on_device(expression, dataset_id, dataset_map, sweep_count, picks, shared_init, specific_init):
    send, cells, state, w_own, v_own = pl.pallas_call(
        front_kernel,
        name="front",
        out_shape=(
            near(HALF + PACKED, N),
            pltpu.VMEM((2 * HALF, 2 * N), BF16),
            near(N, 2 * N),
            near(K, N),
            near(K, N),
        ),
        in_specs=[FAR] * 6,
        out_specs=[VM] * 5,
        scratch_shapes=[
            pltpu.VMEM(picks.shape, jnp.int32),
            pltpu.SMEM(dataset_id.shape, jnp.int32),
            pltpu.SMEM(sweep_count.shape, jnp.int32),
            pltpu.VMEM(expression.shape, BF16),
            pltpu.VMEM(shared_init.shape, F32),
            pltpu.VMEM(shared_init.shape, F32),
            pltpu.VMEM((expression.shape[1], 2 * N), BF16),
            pltpu.VMEM((K, K, N), F32),
            pltpu.SemaphoreType.DMA((6,)),
        ],
    )(picks, dataset_id, sweep_count, expression, shared_init, specific_init)
    came = lax.ppermute(send, "c", SWAP)
    keep, loads, spreader = pl.pallas_call(
        keep_kernel,
        name="keep",
        compiler_params=LIMIT,
        out_shape=(near(HALF, N), shape(2, K, N), pltpu.VMEM((2 * N, K * N), BF16)),
        in_specs=[VM, VM],
        out_specs=[VM] * 3,
    )(held(cells), held(state))
    packed = pl.pallas_call(
        pack_kernel,
        name="pack",
        compiler_params=LIMIT,
        out_shape=near(8, N + PACKED, N),
        in_specs=[VM] * 3,
        out_specs=VM,
    )(held(keep), held(send), held(came))
    came = lax.all_to_all(packed, RING, 0, 0, tiled=True)
    spread = pl.pallas_call(
        group_kernel, name="group", compiler_params=LIMIT, out_shape=near(8, K + K // 2 + PACKED, N), in_specs=[VM, VM], out_specs=VM
    )(held(came), held(v_own))
    came = lax.all_to_all(spread, GRP, 0, 0, tiled=True)
    spread = pl.pallas_call(
        update_kernel,
        name="update",
        compiler_params=LIMIT,
        out_shape=near(16, K, N),
        in_specs=[VM] * 3,
        out_specs=VM,
        scratch_shapes=[pltpu.VMEM((4, K, N), F32)] * 3
        + [pltpu.VMEM((K, 4 * K, N), F32)]
        + [pltpu.VMEM((K, K, N), F32)] * 2,
    )(held(came), held(w_own), held(spreader))
    mine = lax.all_to_all(spread, PLANE, 0, 0, tiled=True)
    other = lax.ppermute(mine, "c", SWAP)
    bases = finish(mine, lambda: lax.axis_index("c"), "mine")
    shared, specific = finish(other, lambda: 1 - lax.axis_index("c"), "other", bases)
    return loads, shared, specific


def solution(mesh):
    fine = Mesh(mesh.devices.reshape(4, 2, 2, 4, 2), ALL)
    return jax.shard_map(
        on_device,
        mesh=fine,
        in_specs=(P(None, ALL), P(ALL), P(SLOTS), P(), P(None, ALL), P(), P(SLOTS, None, None)),
        out_specs=(P(None, None, ALL), P(), P(SLOTS, None, None)),
        check_vma=False,
    )
```

```python
import jax
import jax.numpy as jnp
from jax import lax
from jax.experimental import pallas as pl
from jax.experimental.pallas import tpu as pltpu
from jax.sharding import Mesh, PartitionSpec as P

K = 64
G = 2000
N = 128
HALF = 8 * N
PACKED = K // 2 + 8
LAST = G - 15 * N
EPSILON = 1e-06
LAMBDA = 5.0
RIDGE = 1.0 + LAMBDA
HIGHEST = lax.Precision.HIGHEST
SLOTS = ("y", "xl")
GRP = ("xl", "y")
RING = ("z", "xh")
PLANE = ("xh", "xl", "z")
ALL = ("y", "xl", "xh", "z", "c")
NT = (((1,), (1,)), ((), ()))
F32 = jnp.float32
BF16 = jnp.bfloat16


def dot_nt(a, b, precision=None):
    return lax.dot_general(a, b, NT, precision=precision, preferred_element_type=F32)


def diagonal(square):
    n = square.shape[0]
    rows = lax.broadcasted_iota(jnp.int32, (n, n), 0)
    cols = lax.broadcasted_iota(jnp.int32, (n, n), 1)
    return jnp.sum(jnp.where(rows == cols, square, 0.0), axis=1, keepdims=True)


def rows_of(x):
    return [x[8 * t : 8 * t + 8] for t in range(K // 8)]


def coordinate_steps(state, residual, column, last):
    sub = lax.broadcasted_iota(jnp.int32, (8, N), 0)
    for k in range(K):
        t, s = divmod(k, 8)
        if s == 0:
            floors = [-h[t] for h in state]
            changes = [None] * len(state)
        for half, r in enumerate(residual):
            change = jnp.maximum(floors[half], r[t])
            spread = jnp.broadcast_to(change[s : s + 1], (8, N))
            changes[half] = change if s == 0 else jnp.where(sub >= s, change, changes[half])
            for j in range((t if s < 7 else t + 1) if last else 0, K // 8):
                r[j] = r[j] - column(half, k, j) * spread
        if s == 7:
            for h, change in zip(state, changes):
                h[t] = h[t] + change
    return [jnp.concatenate(h, axis=0) for h in state]


def lanes_of(rows):
    return lax.broadcasted_iota(jnp.int32, (rows, N), 1)


def swapped(x):
    return pltpu.roll(x, K, 1)


def left_left(a, b):
    return jnp.where(lanes_of(a.shape[0]) < K, a, swapped(b))


def right_right(a, b):
    return jnp.where(lanes_of(a.shape[0]) < K, swapped(a), b)


def split_rows(x):
    return left_left(x[: K // 2], x[K // 2 :]), right_right(x[: K // 2], x[K // 2 :])


def pair_rows(a, b):
    return jnp.concatenate([left_left(a, b), right_right(a, b)], axis=0)


def corners(x):
    left = lanes_of(K) < K
    return jnp.concatenate([jnp.where(left, x, 0.0), jnp.where(left, 0.0, x)], axis=0)


def fold_grams(gram):
    rows = lax.broadcasted_iota(jnp.int32, (K, N), 0)
    other = swapped(gram)
    square = jnp.where(lanes_of(K) <= rows, gram, other)
    packed = left_left(square[: K // 2], square[K // 2 :])
    diag = jnp.sum(jnp.where(lanes_of(K) == rows, other, 0.0), axis=0, keepdims=True)
    return jnp.concatenate([packed, jnp.broadcast_to(diag, (8, N))], axis=0)


def unfold_grams(a, b):
    square = pair_rows(a[: K // 2], b[: K // 2])
    turned = corners(square).T
    turned = turned[:K] + turned[K:]
    diag = left_left(a[K // 2 :], b[K // 2 :])[:1]
    rows = lax.broadcasted_iota(jnp.int32, (K, N), 0)
    cols = lanes_of(K) % K
    first = jnp.where(cols <= rows, square, turned)
    second = jnp.where(cols < rows, turned, jnp.where(cols == rows, diag, square))
    return first, first + second


def split(x):
    high = x.astype(BF16)
    return high, (x - high.astype(F32)).astype(BF16)


def gram_of(high, low):
    both = dot_nt(jnp.concatenate([high, low], axis=0), high)
    return both[:K], both[K:]


def front_kernel(
    picks_hbm, ids_hbm, sweeps_hbm, x_hbm, w_hbm, v_hbm,
    send, cells, state, w_own, v_own,
    picks, ids, sweeps, x, w, v, choose, table, sems,
):
    core = lax.axis_index("c")
    tile = core * 8 + lax.axis_index("z") * 2 + lax.axis_index("xh")
    copies = [
        pltpu.make_async_copy(source, target, sems.at[i])
        for i, (source, target) in enumerate(
            [
                (picks_hbm, picks),
                (w_hbm, w),
                (v_hbm.at[0], v),
                (x_hbm, x),
                (ids_hbm, ids),
                (sweeps_hbm, sweeps),
            ]
        )
    ]
    for copy in copies:
        copy.start()
    copies[0].wait()
    pool = lax.broadcasted_iota(jnp.int32, (x.shape[1], N), 0)
    for r in range(2):
        choose[:, N * r : N * r + N] = (pool == picks[r : r + 1, :]).astype(F32).astype(BF16)
    cells[G:] = jnp.zeros((2 * HALF - G, 2 * N), BF16)
    copies[1].wait()
    copies[2].wait()

    @pl.when(tile < 15)
    def _():
        at = pl.multiple_of(jnp.minimum(tile, 14) * N, N)
        w_own[...] = w[:, pl.ds(at, N)]
        v_own[...] = v[:, pl.ds(at, N)]

    @pl.when(tile == 15)
    def _():
        w_own[...] = jnp.zeros((K, N), F32)
        v_own[...] = jnp.zeros((K, N), F32)
        w_own[:, :LAST] = w[:, 15 * N :]
        v_own[:, :LAST] = v[:, 15 * N :]

    specific = v[...]
    mixed_high, mixed_low = split(w[...] + specific)
    mixed_gram, mixed_cross = gram_of(mixed_high, mixed_low)
    own_gram, own_cross = gram_of(*split(specific))
    cross = mixed_cross + LAMBDA * own_cross
    gram = mixed_gram + LAMBDA * own_gram + cross + cross.T
    inverse = 1.0 / (diagonal(gram) + EPSILON)
    scaled = gram * inverse
    for copy in copies[3:]:
        copy.wait()
    cells[:G] = jnp.dot(x[...], choose[...], preferred_element_type=F32).astype(BF16)
    for k in range(K):
        table[k] = jnp.broadcast_to(scaled[:, k : k + 1], (K, N))
    target = jnp.dot(mixed_high, cells[:G], preferred_element_type=F32) * inverse
    count = sweeps[ids[0]]

    def column(_, k, j):
        return table[k, 8 * j : 8 * j + 8]

    def sweep(_, carry):
        parts = [list(part) for part in carry]
        coordinate_steps(parts[:2], parts[2:], column, False)
        return tuple(tuple(part) for part in parts)

    none = tuple(jnp.zeros((8, N), F32) for _ in range(K // 8))
    carry = (none, none, tuple(rows_of(target[:, :N])), tuple(rows_of(target[:, N:])))
    parts = [list(part) for part in lax.fori_loop(0, count - 1, sweep, carry)]
    first, second = coordinate_steps(parts[:2], parts[2:], column, True)
    zero = jnp.zeros((K, N), F32)
    both = jnp.concatenate([first, second], axis=1)
    block = jnp.concatenate(
        [jnp.concatenate([first, zero], axis=1), jnp.concatenate([zero, second], axis=1)], axis=0
    )
    state[...] = block
    away = pl.multiple_of((1 - core) * HALF, HALF)
    high, low = split(both)
    rounded = block.astype(BF16)
    gram = dot_nt(jnp.concatenate([high, low], axis=0), rounded)
    gram = gram[:K] + gram[K:] + dot_nt(high, split(block)[1])
    send[HALF:] = fold_grams(gram)
    send[:HALF] = dot_nt(cells[pl.ds(away, HALF)], rounded)


def keep_kernel(cells, state, keep, loads, spread):
    rows = lax.broadcasted_iota(jnp.int32, (2 * N, N), 0) % N
    at = rows - jnp.where(lanes_of(2 * N) < K, 0, K)
    for k in range(K):
        spread[:, N * k : N * k + N] = (at == k).astype(F32).astype(BF16)
    core = lax.axis_index("c")
    home = pl.multiple_of(core * HALF, HALF)
    block = state[...]
    loads[0] = block[:K, :N]
    loads[1] = block[K:, N:]
    keep[...] = dot_nt(cells[pl.ds(home, HALF)], block.astype(BF16))


def pack_kernel(keep, send, came, out):
    gram = send[HALF:] + came[HALF:]
    for i in range(8):
        out[i, :N] = keep[N * i : N * i + N] + came[N * i : N * i + N]
        out[i, N:] = gram


def group_kernel(came, v_own, out):
    total = came[0]
    for i in range(1, 8):
        total = total + came[i]
    rows = total[:N].T
    first, second = rows[:K], rows[:K] + rows[K:]
    stats = (left_left(first, second), right_right(first, second))
    bases = split_rows(v_own[...])
    for i in range(8):
        out[i, :K] = stats[i // 4]
        out[i, K : K + K // 2] = bases[i // 4]
        out[i, K + K // 2 :] = total[N:]


def dot_split(a, b):
    a_high, a_low = split(a)
    b_high, b_low = split(b)
    left = jnp.concatenate([a_high, a_low, a_high], axis=1)
    return jnp.dot(left, jnp.concatenate([b_high, b_high, b_low], axis=0), preferred_element_type=F32)


def one_pass(state, residual, weight, beside=None):
    sub = lax.broadcasted_iota(jnp.int32, (8, N), 0)
    for k in range(K):
        t, s = divmod(k, 8)
        if beside is not None:
            beside(k)
        if s == 0:
            floors = [-h[t] for h in state]
            changes = [None] * len(state)
        for i, r in enumerate(residual):
            change = jnp.maximum(floors[i], r[t])
            spread = jnp.broadcast_to(change[s : s + 1], (8, N))
            changes[i] = change if s == 0 else jnp.where(sub >= s, change, changes[i])
            for j in range(t if s < 7 else t + 1, K // 8):
                r[j] = r[j] - weight(i, k, j) * spread
        if s == 7:
            for h, change in zip(state, changes):
                h[t] = h[t] + change
    return [jnp.concatenate(h, axis=0) for h in state]


def column_of(table, k, j):
    return jnp.broadcast_to(table[8 * j : 8 * j + 8, k : k + 1], (8, N))


def columns_of(table, k, j):
    half = jnp.where(lanes_of(8) < K, k, K + k)
    return jnp.take_along_axis(table[8 * j : 8 * j + 8], half, axis=1, mode="promise_in_bounds")


def both_halves(x):
    return x + swapped(x)


def shared_start(shared, gram, inverse, carried):
    start = carried - dot_split(gram, jnp.concatenate([shared, jnp.zeros((K, N), F32)], axis=0))
    return [rows_of(shared)], [rows_of(start * inverse)]


def shared_scale(gram):
    return 1.0 / jnp.maximum(diagonal(gram[:, :K]), 1.0)


def ridge_scale(gram):
    rows = lax.broadcasted_iota(jnp.int32, (K, N), 0)
    left = jnp.sum(jnp.where(lanes_of(K) == rows, gram, 0.0), axis=1, keepdims=True)
    right = jnp.sum(jnp.where(lanes_of(K) == rows + K, gram, 0.0), axis=1, keepdims=True)
    return 1.0 / jnp.maximum(RIDGE * jnp.where(lanes_of(K) < K, left, right), 1.0)


def update_kernel(came, w_own, spread, out, stats, grams_next, v_first, wide, later_shared, later_own):
    at_y, at_xl = lax.axis_index("y"), lax.axis_index("xl")
    pairs = range(4)
    stat, base, grams = [], [], []
    for p in pairs:
        a, b = p, 4 + p
        stat.append(left_left(came[a, :K], came[b, :K]))
        stats[p] = right_right(came[a, :K], came[b, :K])
        base.append(pair_rows(came[a, K : K + K // 2], came[b, K : K + K // 2]))
        first, both = unfold_grams(came[a, K + K // 2 :], came[b, K + K // 2 :])
        grams.append(first)
        grams_next[p] = both
    shared = w_own[...]
    shared = jnp.where(at_xl == 0, left_left(shared, shared), right_right(shared, shared))

    inverses = [ridge_scale(gram) for gram in grams]
    parts = []
    for p in pairs:
        high, low = split((RIDGE * grams[p]) * inverses[p])
        parts.append(jnp.concatenate([high.astype(F32), low.astype(F32)], axis=1))

    def widen(k):
        if k % 8:
            return
        rows = K - k
        left = jnp.concatenate([part[k:] for part in parts], axis=0).astype(BF16)
        columns = jnp.dot(left, spread[:, N * k : N * k + 8 * N], preferred_element_type=F32)
        for i in range(8):
            for p in pairs:
                wide[k + i, K * p + k : K * p + K] = columns[rows * p : rows * p + rows, N * i : N * i + N]

    pulls = [dot_split(grams[p], corners(base[p])) for p in pairs]
    carried = sum(stat[p] - pulls[p] for p in pairs)
    total = both_halves(sum(grams))
    scale = shared_scale(total)
    table = total * scale
    state, residual = shared_start(shared, total, scale, both_halves(carried))
    (shared,) = one_pass(state, residual, lambda i, k, j: column_of(table, k, j), widen)

    later = [grams_next[p] for p in pairs]
    later_total = both_halves(sum(later))
    later_scale = shared_scale(later_total)
    later_table = later_total * later_scale
    own = grams_next[at_y]
    own_scale = ridge_scale(own)
    own_table = (RIDGE * own) * own_scale

    def prepare(k):
        for j in range(k // 8, K // 8):
            later_shared[k, 8 * j : 8 * j + 8] = column_of(later_table, k, j)
            later_own[k, 8 * j : 8 * j + 8] = columns_of(own_table, k, j)

    pushed = dot_split(jnp.concatenate(grams, axis=0), corners(shared))
    state, residual = [], []
    for p in pairs:
        rest = stat[p] - pushed[K * p : K * p + K] - RIDGE * pulls[p]
        state.append(rows_of(base[p]))
        residual.append(rows_of(rest * inverses[p]))
    values = one_pass(state, residual, lambda i, k, j: wide[k, K * i + 8 * j : K * i + 8 * j + 8], prepare)
    for p in pairs:
        v_first[p] = values[p]

    pulled = dot_split(jnp.concatenate(later, axis=1), jnp.concatenate([corners(v) for v in values], axis=0))
    carried = sum(stats[p] for p in pairs) - pulled
    state, residual = shared_start(shared, later_total, later_scale, both_halves(carried))
    (shared,) = one_pass(state, residual, lambda i, k, j: later_shared[k, 8 * j : 8 * j + 8])

    specific = v_first[at_y]
    rest = stats[at_y] - dot_split(own, corners(shared + RIDGE * specific))
    (specific,) = one_pass(
        [rows_of(specific)], [rows_of(rest * own_scale)], lambda i, k, j: later_own[k, 8 * j : 8 * j + 8]
    )
    pieces = (left_left(shared, specific), jnp.where(lanes_of(K) < K, shared, specific))
    for i in range(16):
        out[i] = pieces[i // 4 % 2]


def finish_kernel(part, *refs):
    w, v = refs[-2:]
    for i in range(8):
        left = part[i % 2 * 8 + i // 2]
        right = part[i % 2 * 8 + i // 2 + 4]
        w[:, N * i : N * i + N] = left_left(left, right)
        v[0, :, N * i : N * i + N] = right_right(left, right)


def finish(part, half, name, earlier=()):
    return pl.pallas_call(
        finish_kernel,
        name=name,
        compiler_params=LIMIT,
        grid=(1,),
        out_shape=(shape(K, G), shape(1, K, G)),
        in_specs=[VM] + [FAR] * len(earlier),
        out_specs=[
            pl.BlockSpec((K, HALF), lambda i: (0, half())),
            pl.BlockSpec((1, K, HALF), lambda i: (0, 0, half())),
        ],
        input_output_aliases={1: 0, 2: 1} if earlier else {},
    )(held(part), *earlier)


def shape(*dims):
    return jax.ShapeDtypeStruct(dims, F32)


def near(*dims):
    return pltpu.VMEM(dims, F32)


def held(x):
    return pltpu.with_memory_space_constraint(x, pltpu.VMEM)


VM = pl.BlockSpec(memory_space=pltpu.VMEM)
FAR = pl.BlockSpec(memory_space=pltpu.HBM)
SWAP = [(0, 1), (1, 0)]
LIMIT = pltpu.CompilerParams(vmem_limit_bytes=24 << 20)


def on_device(expression, dataset_id, dataset_map, sweep_count, picks, shared_init, specific_init):
    send, cells, state, w_own, v_own = pl.pallas_call(
        front_kernel,
        name="front",
        out_shape=(
            near(HALF + PACKED, N),
            pltpu.VMEM((2 * HALF, 2 * N), BF16),
            near(N, 2 * N),
            near(K, N),
            near(K, N),
        ),
        in_specs=[FAR] * 6,
        out_specs=[VM] * 5,
        scratch_shapes=[
            pltpu.VMEM(picks.shape, jnp.int32),
            pltpu.SMEM(dataset_id.shape, jnp.int32),
            pltpu.SMEM(sweep_count.shape, jnp.int32),
            pltpu.VMEM(expression.shape, BF16),
            pltpu.VMEM(shared_init.shape, F32),
            pltpu.VMEM(shared_init.shape, F32),
            pltpu.VMEM((expression.shape[1], 2 * N), BF16),
            pltpu.VMEM((K, K, N), F32),
            pltpu.SemaphoreType.DMA((6,)),
        ],
    )(picks, dataset_id, sweep_count, expression, shared_init, specific_init)
    came = lax.ppermute(send, "c", SWAP)
    keep, loads, spreader = pl.pallas_call(
        keep_kernel,
        name="keep",
        compiler_params=LIMIT,
        out_shape=(near(HALF, N), shape(2, K, N), pltpu.VMEM((2 * N, K * N), BF16)),
        in_specs=[VM, VM],
        out_specs=[VM] * 3,
    )(held(cells), held(state))
    packed = pl.pallas_call(
        pack_kernel,
        name="pack",
        compiler_params=LIMIT,
        out_shape=near(8, N + PACKED, N),
        in_specs=[VM] * 3,
        out_specs=VM,
    )(held(keep), held(send), held(came))
    came = lax.all_to_all(packed, RING, 0, 0, tiled=True)
    spread = pl.pallas_call(
        group_kernel, name="group", compiler_params=LIMIT, out_shape=near(8, K + K // 2 + PACKED, N), in_specs=[VM, VM], out_specs=VM
    )(held(came), held(v_own))
    came = lax.all_to_all(spread, GRP, 0, 0, tiled=True)
    spread = pl.pallas_call(
        update_kernel,
        name="update",
        compiler_params=LIMIT,
        out_shape=near(16, K, N),
        in_specs=[VM] * 3,
        out_specs=VM,
        scratch_shapes=[pltpu.VMEM((4, K, N), F32)] * 3
        + [pltpu.VMEM((K, 4 * K, N), F32)]
        + [pltpu.VMEM((K, K, N), F32)] * 2,
    )(held(came), held(w_own), held(spreader))
    mine = lax.all_to_all(spread, PLANE, 0, 0, tiled=True)
    other = lax.ppermute(mine, "c", SWAP)
    bases = finish(mine, lambda: lax.axis_index("c"), "mine")
    shared, specific = finish(other, lambda: 1 - lax.axis_index("c"), "other", bases)
    return loads, shared, specific


def solution(mesh):
    fine = Mesh(mesh.devices.reshape(4, 2, 2, 4, 2), ALL)
    return jax.shard_map(
        on_device,
        mesh=fine,
        in_specs=(P(None, ALL), P(ALL), P(SLOTS), P(), P(None, ALL), P(), P(SLOTS, None, None)),
        out_specs=(P(None, None, ALL), P(), P(SLOTS, None, None)),
        check_vma=False,
    )
```

```python
import jax
import jax.numpy as jnp
from jax import lax
from jax.experimental import pallas as pl
from jax.experimental.pallas import tpu as pltpu
from jax.sharding import Mesh, PartitionSpec as P

K = 64
G = 2000
N = 128
HALF = 8 * N
PACKED = K // 2 + 8
LAST = G - 15 * N
EPSILON = 1e-06
LAMBDA = 5.0
RIDGE = 1.0 + LAMBDA
HIGHEST = lax.Precision.HIGHEST
SLOTS = ("y", "xl")
GRP = ("xl", "y")
RING = ("z", "xh")
PLANE = ("xh", "xl", "z")
ALL = ("y", "xl", "xh", "z", "c")
NT = (((1,), (1,)), ((), ()))
F32 = jnp.float32
BF16 = jnp.bfloat16


def dot_nt(a, b, precision=None):
    return lax.dot_general(a, b, NT, precision=precision, preferred_element_type=F32)


def diagonal(square):
    n = square.shape[0]
    rows = lax.broadcasted_iota(jnp.int32, (n, n), 0)
    cols = lax.broadcasted_iota(jnp.int32, (n, n), 1)
    return jnp.sum(jnp.where(rows == cols, square, 0.0), axis=1, keepdims=True)


def rows_of(x):
    return [x[8 * t : 8 * t + 8] for t in range(K // 8)]


def coordinate_steps(state, residual, column, last):
    sub = lax.broadcasted_iota(jnp.int32, (8, N), 0)
    for k in range(K):
        t, s = divmod(k, 8)
        if s == 0:
            floors = [-h[t] for h in state]
            changes = [None] * len(state)
        for half, r in enumerate(residual):
            change = jnp.maximum(floors[half], r[t])
            spread = jnp.broadcast_to(change[s : s + 1], (8, N))
            changes[half] = change if s == 0 else jnp.where(sub >= s, change, changes[half])
            for j in range((t if s < 7 else t + 1) if last else 0, K // 8):
                r[j] = r[j] - column(half, k, j) * spread
        if s == 7:
            for h, change in zip(state, changes):
                h[t] = h[t] + change
    return [jnp.concatenate(h, axis=0) for h in state]


def lanes_of(rows):
    return lax.broadcasted_iota(jnp.int32, (rows, N), 1)


def swapped(x):
    return pltpu.roll(x, K, 1)


def left_left(a, b):
    return jnp.where(lanes_of(a.shape[0]) < K, a, swapped(b))


def right_right(a, b):
    return jnp.where(lanes_of(a.shape[0]) < K, swapped(a), b)


def split_rows(x):
    return left_left(x[: K // 2], x[K // 2 :]), right_right(x[: K // 2], x[K // 2 :])


def pair_rows(a, b):
    return jnp.concatenate([left_left(a, b), right_right(a, b)], axis=0)


def corners(x):
    left = lanes_of(K) < K
    return jnp.concatenate([jnp.where(left, x, 0.0), jnp.where(left, 0.0, x)], axis=0)


def fold_grams(gram):
    rows = lax.broadcasted_iota(jnp.int32, (K, N), 0)
    other = swapped(gram)
    square = jnp.where(lanes_of(K) <= rows, gram, other)
    packed = left_left(square[: K // 2], square[K // 2 :])
    diag = jnp.sum(jnp.where(lanes_of(K) == rows, other, 0.0), axis=0, keepdims=True)
    return jnp.concatenate([packed, jnp.broadcast_to(diag, (8, N))], axis=0)


def unfold_grams(a, b):
    square = pair_rows(a[: K // 2], b[: K // 2])
    turned = corners(square).T
    turned = turned[:K] + turned[K:]
    diag = left_left(a[K // 2 :], b[K // 2 :])[:1]
    rows = lax.broadcasted_iota(jnp.int32, (K, N), 0)
    cols = lanes_of(K) % K
    first = jnp.where(cols <= rows, square, turned)
    second = jnp.where(cols < rows, turned, jnp.where(cols == rows, diag, square))
    return first, first + second


def split(x):
    high = x.astype(BF16)
    return high, (x - high.astype(F32)).astype(BF16)


def front_kernel(
    picks_hbm, ids_hbm, sweeps_hbm, x_hbm, w_hbm, v_hbm,
    send, cells, state, w_own, v_own,
    picks, ids, sweeps, x, w, v, choose, table, sems,
):
    core = lax.axis_index("c")
    tile = core * 8 + lax.axis_index("z") * 2 + lax.axis_index("xh")
    copies = [
        pltpu.make_async_copy(source, target, sems.at[i])
        for i, (source, target) in enumerate(
            [
                (picks_hbm, picks),
                (w_hbm, w),
                (v_hbm.at[0], v),
                (x_hbm, x),
                (ids_hbm, ids),
                (sweeps_hbm, sweeps),
            ]
        )
    ]
    for copy in copies:
        copy.start()
    copies[0].wait()
    pool = lax.broadcasted_iota(jnp.int32, (x.shape[1], N), 0)
    for r in range(2):
        choose[:, N * r : N * r + N] = (pool == picks[r : r + 1, :]).astype(F32).astype(BF16)
    cells[G:] = jnp.zeros((2 * HALF - G, 2 * N), BF16)
    copies[1].wait()
    copies[2].wait()

    @pl.when(tile < 15)
    def _():
        at = pl.multiple_of(jnp.minimum(tile, 14) * N, N)
        w_own[...] = w[:, pl.ds(at, N)]
        v_own[...] = v[:, pl.ds(at, N)]

    @pl.when(tile == 15)
    def _():
        w_own[...] = jnp.zeros((K, N), F32)
        v_own[...] = jnp.zeros((K, N), F32)
        w_own[:, :LAST] = w[:, 15 * N :]
        v_own[:, :LAST] = v[:, 15 * N :]

    specific = v[...]
    mixed_high, mixed_low = split(w[...] + specific)
    own_high, own_low = split(specific)
    both = dot_nt(jnp.concatenate([mixed_high, mixed_low], axis=0), mixed_high)
    other = dot_nt(jnp.concatenate([own_high, own_low], axis=0), own_high)
    total = both + LAMBDA * other
    gram = total[:K] + total[K:] + total[K:].T
    inverse = 1.0 / (diagonal(gram) + EPSILON)
    scaled = gram * inverse
    for copy in copies[3:]:
        copy.wait()
    cells[:G] = jnp.dot(x[...], choose[...], preferred_element_type=F32).astype(BF16)
    for k in range(K):
        table[k] = jnp.broadcast_to(scaled[:, k : k + 1], (K, N))
    target = jnp.dot(mixed_high, cells[:G], preferred_element_type=F32) * inverse
    count = sweeps[ids[0]]

    def column(_, k, j):
        return table[k, 8 * j : 8 * j + 8]

    def sweep(_, carry):
        parts = [list(part) for part in carry]
        coordinate_steps(parts[:2], parts[2:], column, False)
        return tuple(tuple(part) for part in parts)

    none = tuple(jnp.zeros((8, N), F32) for _ in range(K // 8))
    carry = (none, none, tuple(rows_of(target[:, :N])), tuple(rows_of(target[:, N:])))
    parts = [list(part) for part in lax.fori_loop(0, count - 1, sweep, carry)]
    first, second = coordinate_steps(parts[:2], parts[2:], column, True)
    zero = jnp.zeros((K, N), F32)
    both = jnp.concatenate([first, second], axis=1)
    block = jnp.concatenate(
        [jnp.concatenate([first, zero], axis=1), jnp.concatenate([zero, second], axis=1)], axis=0
    )
    state[...] = block
    away = pl.multiple_of((1 - core) * HALF, HALF)
    high, low = split(both)
    rounded = block.astype(BF16)
    gram = dot_nt(jnp.concatenate([high, low], axis=0), rounded)
    gram = gram[:K] + gram[K:] + dot_nt(high, split(block)[1])
    send[HALF:] = fold_grams(gram)
    send[:HALF] = dot_nt(cells[pl.ds(away, HALF)], rounded)


def keep_kernel(cells, state, keep, loads, spread):
    rows = lax.broadcasted_iota(jnp.int32, (2 * N, N), 0) % N
    at = rows - jnp.where(lanes_of(2 * N) < K, 0, K)
    for k in range(K):
        spread[:, N * k : N * k + N] = (at == k).astype(F32).astype(BF16)
    core = lax.axis_index("c")
    home = pl.multiple_of(core * HALF, HALF)
    block = state[...]
    loads[0] = block[:K, :N]
    loads[1] = block[K:, N:]
    keep[...] = dot_nt(cells[pl.ds(home, HALF)], block.astype(BF16))


def pack_kernel(keep, send, came, out):
    gram = send[HALF:] + came[HALF:]
    for i in range(8):
        out[i, :N] = keep[N * i : N * i + N] + came[N * i : N * i + N]
        out[i, N:] = gram


def group_kernel(came, v_own, out):
    total = came[0]
    for i in range(1, 8):
        total = total + came[i]
    rows = total[:N].T
    first, second = rows[:K], rows[:K] + rows[K:]
    stats = (left_left(first, second), right_right(first, second))
    bases = split_rows(v_own[...])
    for i in range(8):
        out[i, :K] = stats[i // 4]
        out[i, K : K + K // 2] = bases[i // 4]
        out[i, K + K // 2 :] = total[N:]


def dot_split(a, b):
    a_high, a_low = split(a)
    b_high, b_low = split(b)
    left = jnp.concatenate([a_high, a_low, a_high], axis=1)
    return jnp.dot(left, jnp.concatenate([b_high, b_high, b_low], axis=0), preferred_element_type=F32)


def one_pass(state, residual, weight, beside=None):
    sub = lax.broadcasted_iota(jnp.int32, (8, N), 0)
    for k in range(K):
        t, s = divmod(k, 8)
        if beside is not None:
            beside(k)
        if s == 0:
            floors = [-h[t] for h in state]
            changes = [None] * len(state)
        for i, r in enumerate(residual):
            change = jnp.maximum(floors[i], r[t])
            spread = jnp.broadcast_to(change[s : s + 1], (8, N))
            changes[i] = change if s == 0 else jnp.where(sub >= s, change, changes[i])
            for j in range(t if s < 7 else t + 1, K // 8):
                r[j] = r[j] - weight(i, k, j) * spread
        if s == 7:
            for h, change in zip(state, changes):
                h[t] = h[t] + change
    return [jnp.concatenate(h, axis=0) for h in state]


def column_of(table, k, j):
    return jnp.broadcast_to(table[8 * j : 8 * j + 8, k : k + 1], (8, N))


def columns_of(table, k, j):
    half = jnp.where(lanes_of(8) < K, k, K + k)
    return jnp.take_along_axis(table[8 * j : 8 * j + 8], half, axis=1, mode="promise_in_bounds")


def both_halves(x):
    return x + swapped(x)


def shared_start(shared, gram, inverse, carried):
    start = carried - dot_split(gram, jnp.concatenate([shared, jnp.zeros((K, N), F32)], axis=0))
    return [rows_of(shared)], [rows_of(start * inverse)]


def shared_scale(gram):
    return 1.0 / jnp.maximum(diagonal(gram[:, :K]), 1.0)


def ridge_scale(gram):
    rows = lax.broadcasted_iota(jnp.int32, (K, N), 0)
    left = jnp.sum(jnp.where(lanes_of(K) == rows, gram, 0.0), axis=1, keepdims=True)
    right = jnp.sum(jnp.where(lanes_of(K) == rows + K, gram, 0.0), axis=1, keepdims=True)
    return 1.0 / jnp.maximum(RIDGE * jnp.where(lanes_of(K) < K, left, right), 1.0)


def update_kernel(came, w_own, spread, out, stats, grams_next, v_first, wide, later_shared, later_own):
    at_y, at_xl = lax.axis_index("y"), lax.axis_index("xl")
    pairs = range(4)
    stat, base, grams = [], [], []
    for p in pairs:
        a, b = p, 4 + p
        stat.append(left_left(came[a, :K], came[b, :K]))
        stats[p] = right_right(came[a, :K], came[b, :K])
        base.append(pair_rows(came[a, K : K + K // 2], came[b, K : K + K // 2]))
        first, both = unfold_grams(came[a, K + K // 2 :], came[b, K + K // 2 :])
        grams.append(first)
        grams_next[p] = both
    shared = w_own[...]
    shared = jnp.where(at_xl == 0, left_left(shared, shared), right_right(shared, shared))

    inverses = [ridge_scale(gram) for gram in grams]
    parts = []
    for p in pairs:
        high, low = split((RIDGE * grams[p]) * inverses[p])
        parts.append(jnp.concatenate([high.astype(F32), low.astype(F32)], axis=1))

    def widen(k):
        if k % 8:
            return
        rows = K - k
        left = jnp.concatenate([part[k:] for part in parts], axis=0).astype(BF16)
        columns = jnp.dot(left, spread[:, N * k : N * k + 8 * N], preferred_element_type=F32)
        for i in range(8):
            for p in pairs:
                wide[k + i, K * p + k : K * p + K] = columns[rows * p : rows * p + rows, N * i : N * i + N]

    pulls = [dot_split(grams[p], corners(base[p])) for p in pairs]
    carried = sum(stat[p] - pulls[p] for p in pairs)
    total = both_halves(sum(grams))
    scale = shared_scale(total)
    table = total * scale
    state, residual = shared_start(shared, total, scale, both_halves(carried))
    (shared,) = one_pass(state, residual, lambda i, k, j: column_of(table, k, j), widen)

    later = [grams_next[p] for p in pairs]
    later_total = both_halves(sum(later))
    later_scale = shared_scale(later_total)
    later_table = later_total * later_scale
    own = grams_next[at_y]
    own_scale = ridge_scale(own)
    own_table = (RIDGE * own) * own_scale

    def prepare(k):
        for j in range(k // 8, K // 8):
            later_shared[k, 8 * j : 8 * j + 8] = column_of(later_table, k, j)
            later_own[k, 8 * j : 8 * j + 8] = columns_of(own_table, k, j)

    pushed = dot_split(jnp.concatenate(grams, axis=0), corners(shared))
    state, residual = [], []
    for p in pairs:
        rest = stat[p] - pushed[K * p : K * p + K] - RIDGE * pulls[p]
        state.append(rows_of(base[p]))
        residual.append(rows_of(rest * inverses[p]))
    values = one_pass(state, residual, lambda i, k, j: wide[k, K * i + 8 * j : K * i + 8 * j + 8], prepare)
    for p in pairs:
        v_first[p] = values[p]

    pulled = dot_split(jnp.concatenate(later, axis=1), jnp.concatenate([corners(v) for v in values], axis=0))
    carried = sum(stats[p] for p in pairs) - pulled
    state, residual = shared_start(shared, later_total, later_scale, both_halves(carried))
    (shared,) = one_pass(state, residual, lambda i, k, j: later_shared[k, 8 * j : 8 * j + 8])

    specific = v_first[at_y]
    rest = stats[at_y] - dot_split(own, corners(shared + RIDGE * specific))
    (specific,) = one_pass(
        [rows_of(specific)], [rows_of(rest * own_scale)], lambda i, k, j: later_own[k, 8 * j : 8 * j + 8]
    )
    pieces = (left_left(shared, specific), jnp.where(lanes_of(K) < K, shared, specific))
    for i in range(16):
        out[i] = pieces[i // 4 % 2]


def finish_kernel(part, *refs):
    w, v = refs[-2:]
    for i in range(8):
        left = part[i % 2 * 8 + i // 2]
        right = part[i % 2 * 8 + i // 2 + 4]
        w[:, N * i : N * i + N] = left_left(left, right)
        v[0, :, N * i : N * i + N] = right_right(left, right)


def finish(part, half, name, earlier=()):
    return pl.pallas_call(
        finish_kernel,
        name=name,
        compiler_params=LIMIT,
        grid=(1,),
        out_shape=(shape(K, G), shape(1, K, G)),
        in_specs=[VM] + [FAR] * len(earlier),
        out_specs=[
            pl.BlockSpec((K, HALF), lambda i: (0, half())),
            pl.BlockSpec((1, K, HALF), lambda i: (0, 0, half())),
        ],
        input_output_aliases={1: 0, 2: 1} if earlier else {},
    )(held(part), *earlier)


def shape(*dims):
    return jax.ShapeDtypeStruct(dims, F32)


def near(*dims):
    return pltpu.VMEM(dims, F32)


def held(x):
    return pltpu.with_memory_space_constraint(x, pltpu.VMEM)


VM = pl.BlockSpec(memory_space=pltpu.VMEM)
FAR = pl.BlockSpec(memory_space=pltpu.HBM)
SWAP = [(0, 1), (1, 0)]
LIMIT = pltpu.CompilerParams(vmem_limit_bytes=24 << 20)


def on_device(expression, dataset_id, dataset_map, sweep_count, picks, shared_init, specific_init):
    send, cells, state, w_own, v_own = pl.pallas_call(
        front_kernel,
        name="front",
        out_shape=(
            near(HALF + PACKED, N),
            pltpu.VMEM((2 * HALF, 2 * N), BF16),
            near(N, 2 * N),
            near(K, N),
            near(K, N),
        ),
        in_specs=[FAR] * 6,
        out_specs=[VM] * 5,
        scratch_shapes=[
            pltpu.VMEM(picks.shape, jnp.int32),
            pltpu.SMEM(dataset_id.shape, jnp.int32),
            pltpu.SMEM(sweep_count.shape, jnp.int32),
            pltpu.VMEM(expression.shape, BF16),
            pltpu.VMEM(shared_init.shape, F32),
            pltpu.VMEM(shared_init.shape, F32),
            pltpu.VMEM((expression.shape[1], 2 * N), BF16),
            pltpu.VMEM((K, K, N), F32),
            pltpu.SemaphoreType.DMA((6,)),
        ],
    )(picks, dataset_id, sweep_count, expression, shared_init, specific_init)
    came = lax.ppermute(send, "c", SWAP)
    keep, loads, spreader = pl.pallas_call(
        keep_kernel,
        name="keep",
        compiler_params=LIMIT,
        out_shape=(near(HALF, N), shape(2, K, N), pltpu.VMEM((2 * N, K * N), BF16)),
        in_specs=[VM, VM],
        out_specs=[VM] * 3,
    )(held(cells), held(state))
    packed = pl.pallas_call(
        pack_kernel,
        name="pack",
        compiler_params=LIMIT,
        out_shape=near(8, N + PACKED, N),
        in_specs=[VM] * 3,
        out_specs=VM,
    )(held(keep), held(send), held(came))
    came = lax.all_to_all(packed, RING, 0, 0, tiled=True)
    spread = pl.pallas_call(
        group_kernel, name="group", compiler_params=LIMIT, out_shape=near(8, K + K // 2 + PACKED, N), in_specs=[VM, VM], out_specs=VM
    )(held(came), held(v_own))
    came = lax.all_to_all(spread, GRP, 0, 0, tiled=True)
    spread = pl.pallas_call(
        update_kernel,
        name="update",
        compiler_params=LIMIT,
        out_shape=near(16, K, N),
        in_specs=[VM] * 3,
        out_specs=VM,
        scratch_shapes=[pltpu.VMEM((4, K, N), F32)] * 3
        + [pltpu.VMEM((K, 4 * K, N), F32)]
        + [pltpu.VMEM((K, K, N), F32)] * 2,
    )(held(came), held(w_own), held(spreader))
    mine = lax.all_to_all(spread, PLANE, 0, 0, tiled=True)
    other = lax.ppermute(mine, "c", SWAP)
    bases = finish(mine, lambda: lax.axis_index("c"), "mine")
    shared, specific = finish(other, lambda: 1 - lax.axis_index("c"), "other", bases)
    return loads, shared, specific


def solution(mesh):
    fine = Mesh(mesh.devices.reshape(4, 2, 2, 4, 2), ALL)
    return jax.shard_map(
        on_device,
        mesh=fine,
        in_specs=(P(None, ALL), P(ALL), P(SLOTS), P(), P(None, ALL), P(), P(SLOTS, None, None)),
        out_specs=(P(None, None, ALL), P(), P(SLOTS, None, None)),
        check_vma=False,
    )
```
